256 devices in a mesh: ctx: 64 (over z, x_hi, y), head: 4 (over x_lo, core).
Axes of the slice: x: 4 (x_hi: 2, x_lo: 2; x = x_hi * 2 + x_lo), y: 4, z: 8, core: 2. Of those that a mesh axis runs over, the one named last changes fastest.
Arguments:
- queries: bfloat16 [16384, 5120], P('ctx', 'head'), parts along dimension 1, may hold values from -6 to 6
- query_tangents: bfloat16 [16384, 5120], P('ctx', 'head'), parts along dimension 1, may hold values from -6 to 6
- keys: bfloat16 [16384, 5120], P('ctx', 'head'), parts along dimension 1, may hold values from -6 to 6
- key_tangents: bfloat16 [16384, 5120], P('ctx', 'head'), parts along dimension 1, may hold values from -6 to 6
- values: bfloat16 [16384, 5120], P('ctx', 'head'), parts along dimension 1, may hold values from -6 to 6
- value_tangents: bfloat16 [16384, 5120], P('ctx', 'head'), parts along dimension 1, may hold values from -6 to 6
- selection: int32 [128, 14], P('ctx'), may hold values from 0 to 1, as said below
Outputs:
- attention_out: bfloat16 [16384, 5120], P('ctx', 'head'), parts along dimension 1
- attention_tangent: bfloat16 [16384, 5120], P('ctx', 'head'), parts along dimension 1
The draws below stay inside these ranges and needn't reach their ends.
There are 4 independent parts, one for each index of `head`. The reference program is written for one: setup_inputs(seed, part) draws one part's arguments, and reference() takes and returns one part's arrays. A program takes and returns all parts, laid end to end along the dimension named above; an argument that names none is the same for every part. Nothing has to cross between parts.
Inputs may be any that keep to these rules, and one draw needn't show every extreme that they name: `selection`: column 6 + b mod 2 of row b, the query block's own block, is always 1.
All inputs are finite; a program needn't handle non-finite values.
Results may differ from the reference program's by a relative error of at most 0.012.
Values may be sent and summed in bfloat16 or wider, within the bound.
No kernel may reach another device: no remote copies, remote signals or barrier semaphores. Data moves between devices by JAX's collectives and lax.ppermute only.
A program may use at most 128 MiB of HBM per device.

```python
import jax
import jax.numpy as jnp
from jax import lax

HEADS = 10
HEAD_DIM = 128
BLK = 128
REACH = 3
TOK_DEV = 256
TOKENS = 16384
BPD = 2
QBLOCKS = 128
WIN = 14
N_CTX = 64


def draw_queries(key, part):
    sample_field = jax.random.normal(jax.random.fold_in(key, 21), (TOKENS, HEADS * HEAD_DIM), jnp.float32) * 1.4
    return jnp.clip(sample_field, -6.0, 6.0).astype(jnp.bfloat16)


def draw_keys(key, part):
    sample_field = jax.random.normal(jax.random.fold_in(key, 22), (TOKENS, HEADS * HEAD_DIM), jnp.float32) * 1.4
    return jnp.clip(sample_field, -6.0, 6.0).astype(jnp.bfloat16)


def draw_selection(key, part):
    levels = jax.random.randint(jax.random.fold_in(key, 31), (N_CTX,), 0, 8)
    dice_rolls = jax.random.randint(jax.random.fold_in(key, 32), (QBLOCKS, WIN), 0, 16)
    blocks = jnp.arange(QBLOCKS, dtype=jnp.int32)
    owners = blocks // BPD
    limits = 2 + 2 * jnp.take(levels, owners)
    chosen = dice_rolls < limits[:, None]
    columns = jnp.arange(WIN, dtype=jnp.int32)
    itself = columns[None, :] == (REACH * BPD + blocks % BPD)[:, None]
    return jnp.where(chosen | itself, 1, 0).astype(jnp.int32)


def block_levels(own_key, shape, split, low, top_value):
    def one(axis_at, parts):
        heights = jax.random.uniform(jax.random.fold_in(jax.random.fold_in(own_key, 6), axis_at), (parts,), jnp.float32, low / len(split), top_value / len(split))
        return jnp.repeat(jnp.exp(heights), shape[axis_at] // parts).reshape((-1,) + (1,) * (len(shape) - axis_at - 1))

    level = one(*split[0])
    for cut in split[1:]:
        level = level * one(*cut)
    return level


def noise(stream_key, dims, width, bound, cuts=(), kind=jnp.bfloat16):
    values = jax.random.normal(stream_key, dims, jnp.float32) * width
    if len(cuts) > 0:
        values = block_levels(stream_key, dims, cuts, -0.22, 0.18) * values
    return jnp.clip(values, min=-bound, max=bound).astype(kind)


def setup_inputs(seed: int = 0, part: int = 0) -> dict:
    key_of = jax.random.split(jax.random.key(seed), 8)
    part_splits = jax.random.split(jax.random.fold_in(key_of[7], part), 8)
    return {
        "queries": draw_queries(jax.random.fold_in(jax.random.fold_in(key_of[7], part), 71), part),
        "query_tangents": noise(part_splits[1], (TOKENS, HEADS * HEAD_DIM), 1.0, 6.0, ((0, 64),)),
        "keys": draw_keys(jax.random.fold_in(jax.random.fold_in(key_of[7], part), 71), part),
        "key_tangents": noise(part_splits[3], (TOKENS, HEADS * HEAD_DIM), 1.0, 6.0, ((0, 64),)),
        "values": noise(part_splits[4], (TOKENS, HEADS * HEAD_DIM), 1.0, 6.0, ((0, 64),)),
        "value_tangents": noise(part_splits[5], (TOKENS, HEADS * HEAD_DIM), 1.0, 6.0, ((0, 64),)),
        "selection": draw_selection(jax.random.fold_in(key_of[7], 71), part),
    }


big_negative = -1.0e30


def reference(queries, query_tangents, keys, key_tangents, values, value_tangents, selection):
    score_scale = HEAD_DIM ** -0.5
    per_device = TOK_DEV // BLK
    window = (2 * REACH + 1) * per_device
    block_count = TOKENS // BLK

    def split_blocks(flat_array):
        return flat_array.reshape(block_count, BLK, HEADS, HEAD_DIM)

    query_blocks = split_blocks(queries)
    query_tangent_blocks = split_blocks(query_tangents)
    key_blocks = split_blocks(keys)
    key_tangent_blocks = split_blocks(key_tangents)
    value_blocks = split_blocks(values)
    value_tangent_blocks = split_blocks(value_tangents)
    columns = jnp.arange(window, dtype=jnp.int32)

    def one_block(block_index):
        owner_device = block_index // per_device
        source = ((owner_device + columns // per_device - REACH) % N_CTX) * per_device + columns % per_device
        source = source.astype(jnp.int32)

        def window_of(blocks):
            return jnp.take(blocks, source, axis=0).reshape(window * BLK, HEADS, HEAD_DIM).astype(jnp.float32)

        key_window = window_of(key_blocks)
        key_tangent_window = window_of(key_tangent_blocks)
        value_window = window_of(value_blocks)
        value_tangent_window = window_of(value_tangent_blocks)
        query_block = lax.dynamic_index_in_dim(query_blocks, block_index, 0, keepdims=False).astype(jnp.float32)
        query_tangent = lax.dynamic_index_in_dim(query_tangent_blocks, block_index, 0, keepdims=False).astype(jnp.float32)
        chosen = lax.dynamic_index_in_dim(selection, block_index, 0, keepdims=False) != 0
        key_mask = jnp.repeat(chosen, BLK)[None, None, :]
        scores = jnp.einsum("qhd,khd->qhk", query_block, key_window) * score_scale
        score_tangents = (jnp.einsum("qhd,khd->qhk", query_tangent, key_window)
                          + jnp.einsum("qhd,khd->qhk", query_block, key_tangent_window)) * score_scale
        masked = jnp.where(key_mask, scores, big_negative)
        peak_score = masked.max(axis=2, keepdims=True)
        weights = jnp.where(key_mask, jnp.exp(masked - peak_score), 0.0)
        weighted = weights * score_tangents
        weight_total = weights.sum(axis=2)
        tangent_total = weighted.sum(axis=2)
        rounded_weights = weights.astype(jnp.bfloat16).astype(jnp.float32)
        rounded_tangent = weighted.astype(jnp.bfloat16).astype(jnp.float32)
        mixed_sum = jnp.einsum("qhk,khd->qhd", rounded_weights, value_window)
        mixed_tangent = (jnp.einsum("qhk,khd->qhd", rounded_tangent, value_window)
                         + jnp.einsum("qhk,khd->qhd", rounded_weights, value_tangent_window))
        output = mixed_sum / weight_total[:, :, None]
        tangent = (mixed_tangent - output * tangent_total[:, :, None]) / weight_total[:, :, None]
        return (output.astype(jnp.bfloat16).reshape(BLK, HEADS * HEAD_DIM),
                tangent.astype(jnp.bfloat16).reshape(BLK, HEADS * HEAD_DIM))

    outputs, tangents = lax.map(one_block, jnp.arange(block_count, dtype=jnp.int32))
    return outputs.reshape(TOKENS, HEADS * HEAD_DIM), tangents.reshape(TOKENS, HEADS * HEAD_DIM)
```

```python
import functools

import jax
import jax.numpy as jnp
from jax import lax
from jax.experimental import pallas as pl
from jax.experimental.pallas import tpu as pltpu
from jax.sharding import PartitionSpec as P

HEADS = 10
HEAD_DIM = 128
BLK = 128
REACH = 3
TOK = 256
WIN = 14
PLANE = 8
CHUNKS = 2 * REACH + 1
NEG = -1.0e30
LOG2E = 1.4426950408889634
SCALE = HEAD_DIM ** -0.5
MIB = 1 << 20

VMEM_SPEC = pl.BlockSpec(memory_space=pltpu.VMEM)
SMEM_SPEC = pl.BlockSpec(memory_space=pltpu.SMEM)


def pack_kernel(par_ref, q, qt, k, kt, v, vt, sel, kv_out, q_out, kv_same, kv_opp, q_same, q_opp):
    par = par_ref[0]
    for j in range(PLANE):
        cols = pl.ds(j * HEAD_DIM, HEAD_DIM)
        for n, ref in enumerate((k, kt, v, vt)):
            kv_out[j, :, n * HEAD_DIM:(n + 1) * HEAD_DIM] = ref[:, cols]
        for n, ref in enumerate((qt, q)):
            q_out[j, 0:TOK, n * HEAD_DIM:(n + 1) * HEAD_DIM] = ref[:, cols]
        q_out[j, TOK:TOK + 16, :] = sel[...]
    for which, kv_to, q_to in ((par, kv_same, q_same), (1 - par, kv_opp, q_opp)):
        cols = pl.ds(pl.multiple_of((PLANE + which) * HEAD_DIM, HEAD_DIM), HEAD_DIM)
        for n, ref in enumerate((k, kt, v, vt)):
            kv_to[:, n * HEAD_DIM:(n + 1) * HEAD_DIM] = ref[:, cols]
        for n, ref in enumerate((qt, q)):
            q_to[:, n * HEAD_DIM:(n + 1) * HEAD_DIM] = ref[:, cols]


def attend(sel_ref, row, base, qcat, kk, vv, s_scr, p_scr, t_scr):
    dims = (((1,), (1,)), ((), ()))
    query = qcat[:, HEAD_DIM:]
    peak = [None, None]
    for t in range(CHUNKS):
        keys = kk[pl.ds(base + t * TOK, TOK), :HEAD_DIM]
        s = lax.dot_general(query, keys, dims, preferred_element_type=jnp.float32)
        for qb in range(2):
            for kb in range(2):
                listed = sel_ref[row, qb * WIN + 2 * t + kb]
                bias = jnp.where(listed != 0, 0.0, NEG)
                piece = s[qb * BLK:(qb + 1) * BLK, kb * BLK:(kb + 1) * BLK] + bias
                s_scr[qb * BLK:(qb + 1) * BLK, t * TOK + kb * BLK:t * TOK + (kb + 1) * BLK] = piece
                peak[qb] = piece if peak[qb] is None else jnp.maximum(peak[qb], piece)
    factor = SCALE * LOG2E
    top = jnp.concatenate([jnp.max(p, axis=1, keepdims=True) for p in peak], axis=0) * factor
    total = jnp.zeros((TOK, BLK), jnp.float32)
    tangent_total = jnp.zeros((TOK, BLK), jnp.float32)
    for t in range(CHUNKS):
        both = kk[pl.ds(base + t * TOK, TOK), :]
        st = lax.dot_general(qcat, both, dims, preferred_element_type=jnp.float32)
        weights = jnp.exp2(s_scr[:, t * TOK:(t + 1) * TOK] * factor - top)
        weighted = weights * st
        total += weights[:, :BLK] + weights[:, BLK:]
        tangent_total += weighted[:, :BLK] + weighted[:, BLK:]
        p_scr[:, t * TOK:(t + 1) * TOK] = weights.astype(jnp.bfloat16)
        t_scr[:, t * TOK:(t + 1) * TOK] = weighted.astype(jnp.bfloat16)
    window = pl.ds(base, CHUNKS * TOK)
    first = jnp.dot(p_scr[...], vv[window, :], preferred_element_type=jnp.float32)
    second = jnp.dot(t_scr[...], vv[window, :HEAD_DIM], preferred_element_type=jnp.float32)
    inverse = 1.0 / jnp.sum(total, axis=1, keepdims=True)
    out = first[:, :HEAD_DIM] * inverse
    tangent_sum = jnp.sum(tangent_total, axis=1, keepdims=True)
    tangent = ((second - out * tangent_sum) * SCALE + first[:, HEAD_DIM:]) * inverse
    return jnp.concatenate([out.astype(jnp.bfloat16), tangent.astype(jnp.bfloat16)], axis=1)


def plane_kernel(sel_ref, q_ref, main, up, dn, o_ref, kk, vv, s_scr, p_scr, t_scr):
    half = 2 * HEAD_DIM
    for slot in range(PLANE + 2 * REACH):
        if slot < REACH:
            piece = up.at[slot]
        elif slot < REACH + PLANE:
            piece = main.at[slot - REACH]
        else:
            piece = dn.at[slot - REACH - PLANE]
        kk[slot * TOK:(slot + 1) * TOK, :] = piece[:, :half]
        vv[slot * TOK:(slot + 1) * TOK, :] = piece[:, half:]

    def step(i, carry):
        base = pl.multiple_of(i * TOK, TOK)
        o_ref[i] = attend(sel_ref, i, base, q_ref[i, :TOK, :], kk, vv, s_scr, p_scr, t_scr)
        return carry

    lax.fori_loop(0, PLANE, step, 0)


def pair_kernel(where_ref, sel_ref, q_own, q_other, a3, a2, a1, own, b1, b2, b3, far, o_own, o_other,
                kk, vv, s_scr, p_scr, t_scr):
    half = 2 * HEAD_DIM
    par, row = where_ref[0], where_ref[1]
    for place, piece in enumerate((a3, a2, a1, own, b1, b2, b3)):
        rows = pl.ds(pl.multiple_of((place + par) * TOK, TOK), TOK)
        kk[rows, :] = piece[:, :half]
        vv[rows, :] = piece[:, half:]
    rows = pl.ds(pl.multiple_of((1 - par) * CHUNKS * TOK, TOK), TOK)
    kk[rows, :] = far[:, :half]
    vv[rows, :] = far[:, half:]
    base = pl.multiple_of(par * TOK, TOK)
    o_own[...] = attend(sel_ref, row, base, q_own[...], kk, vv, s_scr, p_scr, t_scr)
    base = pl.multiple_of((1 - par) * TOK, TOK)
    o_other[...] = attend(sel_ref, row + 1 - 2 * par, base, q_other[...], kk, vv, s_scr, p_scr, t_scr)


def unpack_kernel(par_ref, mine, own, other, o_ref, t_ref):
    par = par_ref[0]
    for j in range(PLANE):
        cols = pl.ds(j * HEAD_DIM, HEAD_DIM)
        o_ref[:, cols] = mine[j, :, :HEAD_DIM]
        t_ref[:, cols] = mine[j, :, HEAD_DIM:]
    for which, piece in ((par, own), (1 - par, other)):
        cols = pl.ds(pl.multiple_of((PLANE + which) * HEAD_DIM, HEAD_DIM), HEAD_DIM)
        o_ref[:, cols] = piece[:, :HEAD_DIM]
        t_ref[:, cols] = piece[:, HEAD_DIM:]


def bf16(*shape):
    return jax.ShapeDtypeStruct(shape, jnp.bfloat16)


def scratch(slots):
    return [
        pltpu.VMEM((slots * TOK, 2 * HEAD_DIM), jnp.bfloat16),
        pltpu.VMEM((slots * TOK, 2 * HEAD_DIM), jnp.bfloat16),
        pltpu.VMEM((TOK, CHUNKS * TOK), jnp.float32),
        pltpu.VMEM((TOK, CHUNKS * TOK), jnp.bfloat16),
        pltpu.VMEM((TOK, CHUNKS * TOK), jnp.bfloat16),
    ]


def cost(positions):
    products = positions * CHUNKS * TOK * TOK
    return pl.CostEstimate(
        flops=10 * HEAD_DIM * products,
        bytes_accessed=(positions + 2 * REACH) * 4 * TOK * HEAD_DIM * 2 + positions * TOK * 4 * HEAD_DIM * 2,
        transcendentals=products,
    )


def body(queries, query_tangents, keys, key_tangents, values, value_tangents, selection):
    devices = lax.axis_size("ctx")
    me = lax.axis_index("ctx")
    par = (me % 2).astype(jnp.int32)
    where = jnp.stack([par, (me % PLANE).astype(jnp.int32)])
    planes = [[z * PLANE + i for i in range(PLANE)] for z in range(devices // PLANE)]


    def send(array, pairs):
        return lax.ppermute(array, "ctx", pairs)

    def shifted(by):
        return [(i, (i + by) % devices) for i in range(devices)]

    def exchange(array):
        return lax.all_to_all(array, "ctx", 0, 0, axis_index_groups=planes, tiled=True)

    sel_rows = jnp.pad(selection.astype(jnp.bfloat16).reshape(1, 2 * WIN), ((0, 15), (0, 2 * HEAD_DIM - 2 * WIN)))
    kv_out, q_out, kv_same, kv_opp, q_same, q_opp = pl.pallas_call(
        pack_kernel,
        out_shape=(bf16(PLANE, TOK, 512), bf16(PLANE, TOK + 16, 256), bf16(TOK, 512), bf16(TOK, 512),
                   bf16(TOK, 256), bf16(TOK, 256)),
        in_specs=[SMEM_SPEC] + [VMEM_SPEC] * 7,
        out_specs=(VMEM_SPEC,) * 6,
        compiler_params=pltpu.CompilerParams(vmem_limit_bytes=20 * MIB),
        name="pack",
    )(where, queries, query_tangents, keys, key_tangents, values, value_tangents, sel_rows)

    main = exchange(kv_out)
    up = send(main[PLANE - REACH:], shifted(PLANE))
    dn = send(main[:REACH], shifted(-PLANE))
    q_all = exchange(q_out)
    sel_all = q_all[:, TOK, :2 * WIN].astype(jnp.int32)

    swap = [(i, i ^ 1) for i in range(devices)]
    far_pairs = [(i, (i - 4) % devices) if i % 2 == 0 else (i, (i + 4) % devices) for i in range(devices)]
    a3 = send(kv_opp, shifted(3))
    b3 = send(kv_opp, shifted(-3))
    a2 = send(kv_same, shifted(2))
    b2 = send(kv_same, shifted(-2))
    a1 = send(kv_opp, shifted(1))
    b1 = send(kv_opp, shifted(-1))
    far = send(kv_same, far_pairs)
    q_other = send(q_opp, swap)

    mine = pl.pallas_call(
        plane_kernel,
        out_shape=bf16(PLANE, TOK, 256),
        in_specs=[SMEM_SPEC] + [VMEM_SPEC] * 4,
        out_specs=VMEM_SPEC,
        scratch_shapes=scratch(PLANE + 2 * REACH),
        compiler_params=pltpu.CompilerParams(vmem_limit_bytes=32 * MIB),
        cost_estimate=cost(PLANE),
        name="plane",
    )(sel_all, q_all, main, up, dn)
    back = exchange(mine)

    own, other = pl.pallas_call(
        pair_kernel,
        out_shape=(bf16(TOK, 256), bf16(TOK, 256)),
        in_specs=[SMEM_SPEC] * 2 + [VMEM_SPEC] * 10,
        out_specs=(VMEM_SPEC,) * 2,
        scratch_shapes=scratch(2 + 2 * REACH),
        compiler_params=pltpu.CompilerParams(vmem_limit_bytes=24 * MIB),
        cost_estimate=cost(2),
        name="pair",
    )(where, sel_all, q_same, q_other, a3, a2, a1, kv_same, b1, b2, b3, far)
    partner = send(other, swap)

    return pl.pallas_call(
        unpack_kernel,
        out_shape=(bf16(TOK, HEADS * HEAD_DIM), bf16(TOK, HEADS * HEAD_DIM)),
        in_specs=[SMEM_SPEC] + [VMEM_SPEC] * 3,
        out_specs=(VMEM_SPEC,) * 2,
        compiler_params=pltpu.CompilerParams(vmem_limit_bytes=12 * MIB),
        name="unpack",
    )(where, back, own, partner)


def solution(mesh):
    wide = P("ctx", "head")
    return jax.shard_map(
        body,
        mesh=mesh,
        in_specs=(wide,) * 6 + (P("ctx", None),),
        out_specs=(wide, wide),
        check_vma=False,
    )
```

```python
import jax
import jax.numpy as jnp
from jax import lax
from jax.experimental import pallas as pl
from jax.experimental.pallas import tpu as pltpu
from jax.sharding import PartitionSpec as P

HEADS = 10
HEAD_DIM = 128
BLK = 128
REACH = 3
TOK = 256
WIN = 14
PLANE = 8
CHUNKS = 2 * REACH + 1
SLOTS = PLANE + 2 * REACH
NEG = -1.0e30
LOG2E = 1.4426950408889634
SCALE = HEAD_DIM ** -0.5
MIB = 1 << 20

VMEM_SPEC = pl.BlockSpec(memory_space=pltpu.VMEM)
HBM_SPEC = pl.BlockSpec(memory_space=pltpu.HBM)
SMEM_SPEC = pl.BlockSpec(memory_space=pltpu.SMEM)


def run_copies(pairs, sem):
    copies = [pltpu.make_async_copy(source, target, sem.at[n]) for n, (source, target) in enumerate(pairs)]
    for copy in copies:
        copy.start()
    for copy in copies:
        copy.wait()


def lanes(n):
    return pl.ds(n * HEAD_DIM, HEAD_DIM)


def cut_keys_kernel(k, kt, v, vt, out, sem):
    run_copies([(ref.at[:, lanes(j)], out.at[j, :, lanes(n)])
                for j in range(PLANE) for n, ref in enumerate((k, kt, v, vt))], sem)


def cut_rest_kernel(row_ref, q, qt, k, kt, v, vt, q_out, q_same, q_opp, kv_same, kv_opp, sem):
    pairs = [(ref.at[:, lanes(j)], q_out.at[j, 0:TOK, lanes(n)]) for j in range(PLANE) for n, ref in enumerate((qt, q))]
    par = row_ref[0] % 2
    for which, q_to, kv_to in ((par, q_same, kv_same), (1 - par, q_opp, kv_opp)):
        cols = pl.ds(pl.multiple_of((PLANE + which) * HEAD_DIM, HEAD_DIM), HEAD_DIM)
        pairs += [(ref.at[:, cols], q_to.at[:, lanes(n)]) for n, ref in enumerate((qt, q))]
        pairs += [(ref.at[:, cols], kv_to.at[:, lanes(n)]) for n, ref in enumerate((k, kt, v, vt))]
    run_copies(pairs, sem)


def attend(sel_ref, row, base, qcat, kk, vv, s_scr, p_scr, t_scr):
    dims = (((1,), (1,)), ((), ()))
    query = qcat[:, HEAD_DIM:]
    peak = [None, None]
    for t in range(CHUNKS):
        keys = kk[pl.ds(base + t * TOK, TOK), :HEAD_DIM]
        s = lax.dot_general(query, keys, dims, preferred_element_type=jnp.float32)
        for qb in range(2):
            for kb in range(2):
                listed = sel_ref[row, qb * WIN + 2 * t + kb]
                bias = jnp.where(listed != 0, 0.0, NEG)
                piece = s[qb * BLK:(qb + 1) * BLK, kb * BLK:(kb + 1) * BLK] + bias
                s_scr[qb * BLK:(qb + 1) * BLK, t * TOK + kb * BLK:t * TOK + (kb + 1) * BLK] = piece
                peak[qb] = piece if peak[qb] is None else jnp.maximum(peak[qb], piece)
    factor = SCALE * LOG2E
    top = jnp.concatenate([jnp.max(p, axis=1, keepdims=True) for p in peak], axis=0) * factor
    total = jnp.zeros((TOK, BLK), jnp.float32)
    tangent_total = jnp.zeros((TOK, BLK), jnp.float32)
    for t in range(CHUNKS):
        both = kk[pl.ds(base + t * TOK, TOK), :]
        st = lax.dot_general(qcat, both, dims, preferred_element_type=jnp.float32)
        weights = jnp.exp2(s_scr[:, t * TOK:(t + 1) * TOK] * factor - top)
        weighted = weights * st
        total += weights[:, :BLK] + weights[:, BLK:]
        tangent_total += weighted[:, :BLK] + weighted[:, BLK:]
        p_scr[:, t * TOK:(t + 1) * TOK] = weights.astype(jnp.bfloat16)
        t_scr[:, t * TOK:(t + 1) * TOK] = weighted.astype(jnp.bfloat16)
    window = pl.ds(base, CHUNKS * TOK)
    first = jnp.dot(p_scr[...], vv[window, :], preferred_element_type=jnp.float32)
    second = jnp.dot(t_scr[...], vv[window, :HEAD_DIM], preferred_element_type=jnp.float32)
    inverse = 1.0 / jnp.sum(total, axis=1, keepdims=True)
    out = first[:, :HEAD_DIM] * inverse
    tangent_sum = jnp.sum(tangent_total, axis=1, keepdims=True)
    tangent = ((second - out * tangent_sum) * SCALE + first[:, HEAD_DIM:]) * inverse
    return jnp.concatenate([out.astype(jnp.bfloat16), tangent.astype(jnp.bfloat16)], axis=1)


def plane_kernel(sel_ref, q_ref, main, up, dn, o_ref, kk, vv, s_scr, p_scr, t_scr):
    half = 2 * HEAD_DIM
    for slot in range(SLOTS):
        if slot < REACH:
            piece = up.at[slot]
        elif slot < REACH + PLANE:
            piece = main.at[slot - REACH]
        else:
            piece = dn.at[slot - REACH - PLANE]
        kk[slot * TOK:(slot + 1) * TOK, :] = piece[:, :half]
        vv[slot * TOK:(slot + 1) * TOK, :] = piece[:, half:]

    def step(i, carry):
        base = pl.multiple_of(i * TOK, TOK)
        o_ref[i] = attend(sel_ref, i, base, q_ref[i, :TOK, :], kk, vv, s_scr, p_scr, t_scr)
        return carry

    lax.fori_loop(0, PLANE, step, 0)


def pair_kernel(row_ref, sel_ref, q_own, q_other, a3, a2, a1, own, b1, b2, b3, far, o_own, o_other,
                kk, vv, s_scr, p_scr, t_scr):
    half = 2 * HEAD_DIM
    row = row_ref[0]
    par = row % 2
    for place, piece in enumerate((a3, a2, a1, own, b1, b2, b3)):
        rows = pl.ds(pl.multiple_of((place + par) * TOK, TOK), TOK)
        kk[rows, :] = piece[:, :half]
        vv[rows, :] = piece[:, half:]
    rows = pl.ds(pl.multiple_of((1 - par) * CHUNKS * TOK, TOK), TOK)
    kk[rows, :] = far[:, :half]
    vv[rows, :] = far[:, half:]
    for q_ref, at, place, o_ref in ((q_own, row, par, o_own), (q_other, row + 1 - 2 * par, 1 - par, o_other)):
        base = pl.multiple_of(place * TOK, TOK)
        o_ref[...] = attend(sel_ref, at, base, q_ref[...], kk, vv, s_scr, p_scr, t_scr)


def unpack_kernel(par_ref, mine, own, other, o_ref, t_ref):
    par = par_ref[0] % 2
    for j in range(PLANE):
        cols = pl.ds(j * HEAD_DIM, HEAD_DIM)
        o_ref[:, cols] = mine[j, :, :HEAD_DIM]
        t_ref[:, cols] = mine[j, :, HEAD_DIM:]
    for which, piece in ((par, own), (1 - par, other)):
        cols = pl.ds(pl.multiple_of((PLANE + which) * HEAD_DIM, HEAD_DIM), HEAD_DIM)
        o_ref[:, cols] = piece[:, :HEAD_DIM]
        t_ref[:, cols] = piece[:, HEAD_DIM:]


def bf16(*shape):
    return jax.ShapeDtypeStruct(shape, jnp.bfloat16)


def scratch(slots):
    return [
        pltpu.VMEM((slots * TOK, 2 * HEAD_DIM), jnp.bfloat16),
        pltpu.VMEM((slots * TOK, 2 * HEAD_DIM), jnp.bfloat16),
        pltpu.VMEM((TOK, CHUNKS * TOK), jnp.float32),
        pltpu.VMEM((TOK, CHUNKS * TOK), jnp.bfloat16),
        pltpu.VMEM((TOK, CHUNKS * TOK), jnp.bfloat16),
    ]


def cost(positions):
    products = positions * CHUNKS * TOK * TOK
    return pl.CostEstimate(
        flops=10 * HEAD_DIM * products,
        bytes_accessed=(positions + 2 * REACH) * 4 * TOK * HEAD_DIM * 2 + positions * TOK * 4 * HEAD_DIM * 2,
        transcendentals=products,
    )


def body(queries, query_tangents, keys, key_tangents, values, value_tangents, selection):
    devices = lax.axis_size("ctx")
    row = (lax.axis_index("ctx") % PLANE).astype(jnp.int32)[None]
    planes = [[z * PLANE + i for i in range(PLANE)] for z in range(devices // PLANE)]

    def send(array, by):
        return lax.ppermute(array, "ctx", [(i, (i + by) % devices) for i in range(devices)])

    def swapped(array):
        return lax.ppermute(array, "ctx", [(i, i ^ 1) for i in range(devices)])

    def exchange(array):
        return lax.all_to_all(array, "ctx", 0, 0, axis_index_groups=planes, tiled=True)

    wide = [pltpu.with_memory_space_constraint(array, pltpu.HBM) for array in
            (queries, query_tangents, keys, key_tangents, values, value_tangents)]
    kv_out = pl.pallas_call(
        cut_keys_kernel,
        out_shape=bf16(PLANE, TOK, 512),
        in_specs=[HBM_SPEC] * 4,
        out_specs=VMEM_SPEC,
        scratch_shapes=[pltpu.SemaphoreType.DMA((4 * PLANE,))],
        compiler_params=pltpu.CompilerParams(vmem_limit_bytes=8 * MIB),
        name="cut_keys",
    )(*wide[2:])
    q_out, q_same, q_opp, kv_same, kv_opp = pl.pallas_call(
        cut_rest_kernel,
        out_shape=(bf16(PLANE, TOK, 256), bf16(TOK, 256), bf16(TOK, 256), bf16(TOK, 512), bf16(TOK, 512)),
        in_specs=[SMEM_SPEC] + [HBM_SPEC] * 6,
        out_specs=(VMEM_SPEC,) * 5,
        scratch_shapes=[pltpu.SemaphoreType.DMA((2 * PLANE + 12,))],
        compiler_params=pltpu.CompilerParams(vmem_limit_bytes=8 * MIB),
        name="cut_rest",
    )(row, *wide)
    sel_rows = jnp.pad(selection.astype(jnp.bfloat16).reshape(1, 1, 2 * WIN), ((0, 0), (0, 15), (0, 256 - 2 * WIN)))
    q_out = jnp.concatenate([q_out, jnp.broadcast_to(sel_rows, (PLANE, 16, 256))], axis=1)

    main = exchange(kv_out)
    main, q_out, kv_same, kv_opp, q_opp = lax.optimization_barrier((main, q_out, kv_same, kv_opp, q_opp))
    up = send(main[PLANE - REACH:], PLANE)
    dn = send(main[:REACH], -PLANE)
    q_all = exchange(q_out)
    a3, b3, a2 = send(kv_opp, 3), send(kv_opp, -3), send(kv_same, 2)
    q_all, up, dn, a3, b3, a2, kv_same, kv_opp, q_opp = lax.optimization_barrier(
        (q_all, up, dn, a3, b3, a2, kv_same, kv_opp, q_opp))
    b2, a1, b1 = send(kv_same, -2), send(kv_opp, 1), send(kv_opp, -1)
    far = lax.ppermute(kv_same, "ctx", [(i, (i - 4 + 8 * (i % 2)) % devices) for i in range(devices)])
    q_other = swapped(q_opp)
    sel_all = q_all[:, TOK, :2 * WIN].astype(jnp.int32)

    mine = pl.pallas_call(
        plane_kernel,
        out_shape=bf16(PLANE, TOK, 256),
        in_specs=[SMEM_SPEC] + [VMEM_SPEC] * 4,
        out_specs=VMEM_SPEC,
        scratch_shapes=scratch(SLOTS),
        compiler_params=pltpu.CompilerParams(vmem_limit_bytes=16 * MIB),
        cost_estimate=cost(PLANE),
        name="plane",
    )(sel_all, q_all, main, up, dn)
    mine, b2, a1, b1, far, q_other = lax.optimization_barrier((mine, b2, a1, b1, far, q_other))
    back = exchange(mine)

    own, other = pl.pallas_call(
        pair_kernel,
        out_shape=(bf16(TOK, 256), bf16(TOK, 256)),
        in_specs=[SMEM_SPEC] * 2 + [VMEM_SPEC] * 10,
        out_specs=(VMEM_SPEC,) * 2,
        scratch_shapes=scratch(2 + 2 * REACH),
        compiler_params=pltpu.CompilerParams(vmem_limit_bytes=12 * MIB),
        cost_estimate=cost(2),
        name="pair",
    )(row, sel_all, q_same, q_other, a3, a2, a1, kv_same, b1, b2, b3, far)
    partner = swapped(other)

    return pl.pallas_call(
        unpack_kernel,
        out_shape=(bf16(TOK, HEADS * HEAD_DIM), bf16(TOK, HEADS * HEAD_DIM)),
        in_specs=[SMEM_SPEC] + [VMEM_SPEC] * 3,
        out_specs=(VMEM_SPEC,) * 2,
        compiler_params=pltpu.CompilerParams(vmem_limit_bytes=12 * MIB),
        name="unpack",
    )(row, back, own, partner)


def solution(mesh):
    wide = P("ctx", "head")
    return jax.shard_map(
        body,
        mesh=mesh,
        in_specs=(wide,) * 6 + (P("ctx", None),),
        out_specs=(wide, wide),
        check_vma=False,
    )
```

```python
import jax
import jax.numpy as jnp
from jax import lax
from jax.experimental import pallas as pl
from jax.experimental.pallas import tpu as pltpu
from jax.sharding import PartitionSpec as P

HEADS = 10
HEAD_DIM = 128
BLK = 128
REACH = 3
TOK = 256
WIN = 14
PLANE = 8
CHUNKS = 2 * REACH + 1
NEG = -1.0e30
LOG2E = 1.4426950408889634
SCALE = HEAD_DIM ** -0.5
FACTOR = SCALE * LOG2E
MIB = 1 << 20

VMEM_SPEC = pl.BlockSpec(memory_space=pltpu.VMEM)
HBM_SPEC = pl.BlockSpec(memory_space=pltpu.HBM)
ANY_SPEC = pl.BlockSpec(memory_space=pl.ANY)
SMEM_SPEC = pl.BlockSpec(memory_space=pltpu.SMEM)


def run_copies(pairs, sem):
    copies = [pltpu.make_async_copy(source, target, sem.at[n]) for n, (source, target) in enumerate(pairs)]
    for copy in copies:
        copy.start()
    for copy in copies:
        copy.wait()


def lanes(n):
    return pl.ds(n * HEAD_DIM, HEAD_DIM)


def cut_keys_kernel(k, kt, v, vt, out, sem):
    run_copies([(ref.at[:, lanes(j)], out.at[j, :, lanes(n)])
                for j in range(PLANE) for n, ref in enumerate((k, kt, v, vt))], sem)


def cut_rest_kernel(row_ref, sel, q, qt, k, kt, v, vt, q_out, same, opp, sem):
    pairs = [(ref.at[:, lanes(j)], q_out.at[j, 0:TOK, lanes(n)]) for j in range(PLANE) for n, ref in enumerate((qt, q))]
    par = row_ref[0] % 2
    for which, target in ((par, same), (1 - par, opp)):
        cols = pl.ds(pl.multiple_of((PLANE + which) * HEAD_DIM, HEAD_DIM), HEAD_DIM)
        pairs += [(ref.at[:, cols], target.at[:, lanes(n)]) for n, ref in enumerate((k, kt, v, vt, qt, q))]
    for j in range(PLANE):
        q_out[j, TOK:, :] = sel[...]
    run_copies(pairs, sem)


def weigh(sel_ref, row, first, count, chunk, qcat, floor, s_scr, p_scr, t_scr):
    dims = (((1,), (1,)), ((), ()))
    query = qcat[:, HEAD_DIM:]
    peak = [None, None]
    for u in range(count):
        s = lax.dot_general(query, chunk(u)[:, :HEAD_DIM], dims, preferred_element_type=jnp.float32)
        for qb in range(2):
            for kb in range(2):
                listed = sel_ref[row, qb * WIN + 2 * (first + u) + kb]
                piece = s[qb * BLK:(qb + 1) * BLK, kb * BLK:(kb + 1) * BLK] + jnp.where(listed != 0, 0.0, NEG)
                s_scr[qb * BLK:(qb + 1) * BLK, u * TOK + kb * BLK:u * TOK + (kb + 1) * BLK] = piece
                peak[qb] = piece if peak[qb] is None else jnp.maximum(peak[qb], piece)
    top = jnp.concatenate([jnp.max(p, axis=1, keepdims=True) for p in peak], axis=0) * FACTOR
    if floor is not None:
        top = jnp.maximum(top, floor)
    total = jnp.zeros((TOK, BLK), jnp.float32)
    tangent_total = jnp.zeros((TOK, BLK), jnp.float32)
    for u in range(count):
        st = lax.dot_general(qcat, chunk(u), dims, preferred_element_type=jnp.float32)
        weights = jnp.exp2(s_scr[:, u * TOK:(u + 1) * TOK] * FACTOR - top)
        weighted = weights * st
        total += weights[:, :BLK] + weights[:, BLK:]
        tangent_total += weighted[:, :BLK] + weighted[:, BLK:]
        p_scr[:, u * TOK:(u + 1) * TOK] = weights.astype(jnp.bfloat16)
        t_scr[:, u * TOK:(u + 1) * TOK] = weighted.astype(jnp.bfloat16)
    return top, total, tangent_total


def finish(total, tangent_total, first, second):
    inverse = 1.0 / jnp.sum(total, axis=1, keepdims=True)
    out = first[:, :HEAD_DIM] * inverse
    tangent_sum = jnp.sum(tangent_total, axis=1, keepdims=True)
    tangent = ((second - out * tangent_sum) * SCALE + first[:, HEAD_DIM:]) * inverse
    return jnp.concatenate([out.astype(jnp.bfloat16), tangent.astype(jnp.bfloat16)], axis=1)


def mix(p_scr, t_scr, width, values):
    first = jnp.dot(p_scr[:, :width], values, preferred_element_type=jnp.float32)
    second = jnp.dot(t_scr[:, :width], values[:, :HEAD_DIM], preferred_element_type=jnp.float32)
    return first, second


def inner_kernel(sel_ref, q_ref, main, gate, o_ref, stats, first_ref, second_ref, s_scr, p_scr, t_scr):
    del gate

    def position(i, count, final):
        base = pl.multiple_of(jnp.maximum(i - REACH, 0) * TOK, TOK)
        top, total, tangent_total = weigh(
            sel_ref, i, jnp.maximum(REACH - i, 0), count,
            lambda u: main[pl.ds(base + u * TOK, TOK), :2 * HEAD_DIM], q_ref[i, :TOK, :], None, s_scr, p_scr, t_scr)
        first, second = mix(p_scr, t_scr, count * TOK, main[pl.ds(base, count * TOK), 2 * HEAD_DIM:])
        if final:
            o_ref[i - REACH] = finish(total, tangent_total, first, second)
        else:
            stats[i, 0] = jnp.broadcast_to(top, (TOK, BLK))
            stats[i, 1] = total
            stats[i, 2] = tangent_total
            first_ref[i] = first
            second_ref[i] = second

    def step(n, carry):
        for low in range(REACH + 1):
            position(low + n * (PLANE - 1 - 2 * low), low + REACH + 1, low == REACH)
        return carry

    lax.fori_loop(0, 2, step, 0)


def outer_kernel(sel_ref, q_ref, up, dn, mid, stats, first_ref, second_ref, gate_a, gate_b, o_ref, s_scr, p_scr, t_scr):
    del gate_a, gate_b
    for i in (3, 4):
        o_ref[i] = mid[i - REACH]
    for i in (0, 1, 2, 5, 6, 7):
        low = i < REACH
        halo, skip, at = (up, i, 0) if low else (dn, 0, PLANE + REACH - i)
        count = REACH - i if low else i - REACH - 1
        before = stats[i, 0][:, :1]
        top, total, tangent_total = weigh(
            sel_ref, i, at, count, lambda u: halo[skip + u, :, :2 * HEAD_DIM], q_ref[i, :TOK, :], before,
            s_scr, p_scr, t_scr)
        shrink = jnp.exp2(before - top)
        first, second = first_ref[i] * shrink, second_ref[i] * shrink
        for u in range(count):
            more = mix(p_scr.at[:, u * TOK:(u + 1) * TOK], t_scr.at[:, u * TOK:(u + 1) * TOK], TOK,
                       halo[skip + u, :, 2 * HEAD_DIM:])
            first, second = first + more[0], second + more[1]
        o_ref[i] = finish(stats[i, 1] * shrink + total, stats[i, 2] * shrink + tangent_total, first, second)


def join_kernel(row_ref, same, other, gate, both, even, odd):
    del gate
    par = row_ref[0] % 2
    both[par] = same[:, :4 * HEAD_DIM]
    both[1 - par] = other[:, :4 * HEAD_DIM]
    even[...] = both[0]
    odd[...] = both[1]


def pair_kernel(row_ref, sel_ref, same, other, a4, a2, both, b2, b4, o_own, o_other, kv, s_scr, p_scr, t_scr):
    row = row_ref[0]
    par = row % 2
    places = [a4] + [ref.at[n] for ref in (a2, both, b2) for n in range(2)] + [b4]
    for n, ref in enumerate(places):
        kv[n * TOK:(n + 1) * TOK, :] = ref[...]
    for ref, at, place, o_ref in ((same, row, par, o_own), (other, row + 1 - 2 * par, 1 - par, o_other)):
        base = pl.multiple_of(place * TOK, TOK)
        _, total, tangent_total = weigh(
            sel_ref, at, 0, CHUNKS, lambda u: kv[pl.ds(base + u * TOK, TOK), :2 * HEAD_DIM],
            ref[:, 4 * HEAD_DIM:], None, s_scr, p_scr, t_scr)
        first, second = mix(p_scr, t_scr, CHUNKS * TOK, kv[pl.ds(base, CHUNKS * TOK), 2 * HEAD_DIM:])
        o_ref[...] = finish(total, tangent_total, first, second)


def unpack_kernel(par_ref, mine, own, other, o_ref, t_ref):
    par = par_ref[0] % 2
    for j in range(PLANE):
        cols = pl.ds(j * HEAD_DIM, HEAD_DIM)
        o_ref[:, cols] = mine[j, :, :HEAD_DIM]
        t_ref[:, cols] = mine[j, :, HEAD_DIM:]
    for which, piece in ((par, own), (1 - par, other)):
        cols = pl.ds(pl.multiple_of((PLANE + which) * HEAD_DIM, HEAD_DIM), HEAD_DIM)
        o_ref[:, cols] = piece[:, :HEAD_DIM]
        t_ref[:, cols] = piece[:, HEAD_DIM:]


def bf16(*shape):
    return jax.ShapeDtypeStruct(shape, jnp.bfloat16)


def f32(*shape):
    return jax.ShapeDtypeStruct(shape, jnp.float32)


def scratch(chunks):
    return [
        pltpu.VMEM((TOK, chunks * TOK), jnp.float32),
        pltpu.VMEM((TOK, chunks * TOK), jnp.bfloat16),
        pltpu.VMEM((TOK, chunks * TOK), jnp.bfloat16),
    ]


def cost(chunks):
    products = chunks * TOK * TOK
    return pl.CostEstimate(flops=10 * HEAD_DIM * products, bytes_accessed=chunks * 2 * TOK * 4 * HEAD_DIM,
                           transcendentals=products)


def params(mib):
    return pltpu.CompilerParams(vmem_limit_bytes=mib * MIB)


def body(queries, query_tangents, keys, key_tangents, values, value_tangents, selection):
    devices = lax.axis_size("ctx")
    row = (lax.axis_index("ctx") % PLANE).astype(jnp.int32)[None]
    planes = [[z * PLANE + i for i in range(PLANE)] for z in range(devices // PLANE)]

    def send(array, by):
        return lax.ppermute(array, "ctx", [(i, (i + by) % devices) for i in range(devices)])

    def swapped(array):
        return lax.ppermute(array, "ctx", [(i, i ^ 1) for i in range(devices)])

    def exchange(array):
        return lax.all_to_all(array, "ctx", 0, 0, axis_index_groups=planes, tiled=True)

    wide = [pltpu.with_memory_space_constraint(array, pltpu.HBM) for array in
            (queries, query_tangents, keys, key_tangents, values, value_tangents)]
    kv_out = pl.pallas_call(
        cut_keys_kernel,
        out_shape=bf16(PLANE, TOK, 512),
        in_specs=[HBM_SPEC] * 4,
        out_specs=ANY_SPEC,
        scratch_shapes=[pltpu.SemaphoreType.DMA((4 * PLANE,))],
        compiler_params=params(4),
        name="cut_keys",
    )(*wide[2:])
    sel_rows = jnp.pad(selection.astype(jnp.bfloat16).reshape(1, 2 * WIN), ((0, 15), (0, 256 - 2 * WIN)))
    q_out, same, opp = pl.pallas_call(
        cut_rest_kernel,
        out_shape=(bf16(PLANE, TOK + 16, 256), bf16(TOK, 768), bf16(TOK, 768)),
        in_specs=[SMEM_SPEC, VMEM_SPEC] + [HBM_SPEC] * 6,
        out_specs=(VMEM_SPEC,) * 3,
        scratch_shapes=[pltpu.SemaphoreType.DMA((2 * PLANE + 12,))],
        compiler_params=params(8),
        name="cut_rest",
    )(row, sel_rows, *wide)

    other = swapped(opp)
    main = exchange(kv_out)
    up, dn = send(main[PLANE - REACH:], PLANE), send(main[:REACH], -PLANE)
    q_all = exchange(q_out)
    sel_all = q_all[:, TOK, :2 * WIN].astype(jnp.int32)

    both, even, odd = pl.pallas_call(
        join_kernel,
        out_shape=(bf16(2, TOK, 512), bf16(TOK, 512), bf16(TOK, 512)),
        in_specs=[SMEM_SPEC] + [VMEM_SPEC] * 2 + [ANY_SPEC],
        out_specs=(VMEM_SPEC,) * 3,
        compiler_params=params(4),
        name="join",
    )(row, same, other, q_all)
    a2, b2, a4, b4 = send(both, 2), send(both, -2), send(odd, 4), send(even, -4)

    mid, stats, first, second = pl.pallas_call(
        inner_kernel,
        out_shape=(bf16(2, TOK, 256), f32(PLANE, 3, TOK, BLK), f32(PLANE, TOK, 256), f32(PLANE, TOK, BLK)),
        in_specs=[SMEM_SPEC] + [VMEM_SPEC] * 2 + [ANY_SPEC],
        out_specs=(VMEM_SPEC,) * 4,
        scratch_shapes=scratch(CHUNKS),
        compiler_params=params(20),
        cost_estimate=cost(44),
        name="inner",
    )(sel_all, q_all, main.reshape(PLANE * TOK, 512), both)
    mine = pl.pallas_call(
        outer_kernel,
        out_shape=bf16(PLANE, TOK, 256),
        in_specs=[SMEM_SPEC] + [VMEM_SPEC] * 7 + [ANY_SPEC] * 2,
        out_specs=VMEM_SPEC,
        scratch_shapes=scratch(REACH),
        compiler_params=params(20),
        cost_estimate=cost(12),
        name="outer",
    )(sel_all, q_all, up, dn, mid, stats, first, second, a2, b2)
    back = exchange(mine)

    own, lent = pl.pallas_call(
        pair_kernel,
        out_shape=(bf16(TOK, 256), bf16(TOK, 256)),
        in_specs=[SMEM_SPEC] * 2 + [VMEM_SPEC] * 7,
        out_specs=(VMEM_SPEC,) * 2,
        scratch_shapes=[pltpu.VMEM((8 * TOK, 512), jnp.bfloat16)] + scratch(CHUNKS),
        compiler_params=params(12),
        cost_estimate=cost(14),
        name="pair",
    )(row, sel_all, same, other, a4, a2, both, b2, b4)
    partner = swapped(lent)

    return pl.pallas_call(
        unpack_kernel,
        out_shape=(bf16(TOK, HEADS * HEAD_DIM), bf16(TOK, HEADS * HEAD_DIM)),
        in_specs=[SMEM_SPEC] + [VMEM_SPEC] * 3,
        out_specs=(VMEM_SPEC,) * 2,
        compiler_params=params(6),
        name="unpack",
    )(row, back, own, partner)


def solution(mesh):
    wide = P("ctx", "head")
    return jax.shard_map(
        body,
        mesh=mesh,
        in_specs=(wide,) * 6 + (P("ctx", None),),
        out_specs=(wide, wide),
        check_vma=False,
    )
```

```python
import jax
import jax.numpy as jnp
from jax import lax
from jax.experimental import pallas as pl
from jax.experimental.pallas import tpu as pltpu
from jax.sharding import PartitionSpec as P

HEADS = 10
HEAD_DIM = 128
BLK = 128
REACH = 3
TOK = 256
WIN = 14
PLANE = 8
CHUNKS = 2 * REACH + 1
EXTRA = 8
NEG = -1.0e30
LOG2E = 1.4426950408889634
SCALE = HEAD_DIM ** -0.5
FACTOR = SCALE * LOG2E
MIB = 1 << 20

VMEM_SPEC = pl.BlockSpec(memory_space=pltpu.VMEM)
HBM_SPEC = pl.BlockSpec(memory_space=pltpu.HBM)
ANY_SPEC = pl.BlockSpec(memory_space=pl.ANY)
SMEM_SPEC = pl.BlockSpec(memory_space=pltpu.SMEM)


def run_copies(pairs, sem):
    copies = [pltpu.make_async_copy(source, target, sem.at[n]) for n, (source, target) in enumerate(pairs)]
    for copy in copies:
        copy.start()
    for copy in copies:
        copy.wait()


def lanes(n):
    return pl.ds(n * HEAD_DIM, HEAD_DIM)


def cut_keys_kernel(k, kt, v, vt, out):
    for n, ref in enumerate((k, kt, v, vt)):
        out[0, :, n * HEAD_DIM:(n + 1) * HEAD_DIM] = ref[...]


def cut_rest_kernel(row_ref, sel, q, qt, k, kt, v, vt, q_out, kv_same, kv_opp, near, q_same, sem):
    pairs = [(ref.at[:, lanes(j)], q_out.at[j, 0:TOK, lanes(n)]) for j in range(PLANE) for n, ref in enumerate((qt, q))]
    par = row_ref[0] % 2
    own, opp = [pl.ds(pl.multiple_of((PLANE + which) * HEAD_DIM, HEAD_DIM), HEAD_DIM) for which in (par, 1 - par)]
    for n, ref in enumerate((k, kt, v, vt)):
        pairs += [(ref.at[:, own], kv_same.at[:, lanes(n)]), (ref.at[:, opp], kv_opp.at[:, lanes(n)]),
                  (ref.at[:, opp], near.at[:, lanes(n)])]
    for n, ref in enumerate((qt, q)):
        pairs += [(ref.at[:, own], q_same.at[:, lanes(n)]), (ref.at[:, opp], near.at[:, lanes(n + 4)])]
    for j in range(PLANE):
        q_out[j, TOK:, :] = sel[...]
    run_copies(pairs, sem)


def weigh(sel_ref, row, first, count, chunk, qcat, floor, s_scr, p_scr, t_scr):
    dims = (((1,), (1,)), ((), ()))
    query = qcat[:, HEAD_DIM:]
    peak = [None, None]
    for u in range(count):
        s = lax.dot_general(query, chunk(u)[:, :HEAD_DIM], dims, preferred_element_type=jnp.float32)
        for qb in range(2):
            for kb in range(2):
                listed = sel_ref[row, qb * WIN + 2 * (first + u) + kb]
                piece = s[qb * BLK:(qb + 1) * BLK, kb * BLK:(kb + 1) * BLK] + jnp.where(listed != 0, 0.0, NEG)
                s_scr[qb * BLK:(qb + 1) * BLK, u * TOK + kb * BLK:u * TOK + (kb + 1) * BLK] = piece
                peak[qb] = piece if peak[qb] is None else jnp.maximum(peak[qb], piece)
    top = jnp.concatenate([jnp.max(p, axis=1, keepdims=True) for p in peak], axis=0) * FACTOR
    if floor is not None:
        top = jnp.maximum(top, floor)
    total = jnp.zeros((TOK, BLK), jnp.float32)
    tangent_total = jnp.zeros((TOK, BLK), jnp.float32)
    for u in range(count):
        st = lax.dot_general(qcat, chunk(u), dims, preferred_element_type=jnp.float32)
        weights = jnp.exp2(s_scr[:, u * TOK:(u + 1) * TOK] * FACTOR - top)
        weighted = weights * st
        total += weights[:, :BLK] + weights[:, BLK:]
        tangent_total += weighted[:, :BLK] + weighted[:, BLK:]
        p_scr[:, u * TOK:(u + 1) * TOK] = weights.astype(jnp.bfloat16)
        t_scr[:, u * TOK:(u + 1) * TOK] = weighted.astype(jnp.bfloat16)
    return top, total, tangent_total


def finish(total, tangent_total, first, second):
    inverse = 1.0 / jnp.sum(total, axis=1, keepdims=True)
    out = first[:, :HEAD_DIM] * inverse
    tangent_sum = jnp.sum(tangent_total, axis=1, keepdims=True)
    tangent = ((second - out * tangent_sum) * SCALE + first[:, HEAD_DIM:]) * inverse
    return jnp.concatenate([out.astype(jnp.bfloat16), tangent.astype(jnp.bfloat16)], axis=1)


def mix(p_scr, t_scr, width, values):
    first = jnp.dot(p_scr[:, :width], values, preferred_element_type=jnp.float32)
    second = jnp.dot(t_scr[:, :width], values[:, :HEAD_DIM], preferred_element_type=jnp.float32)
    return first, second


def whole(sel_ref, row, base, qcat, kv, s_scr, p_scr, t_scr):
    _, total, tangent_total = weigh(
        sel_ref, row, 0, CHUNKS, lambda u: kv[pl.ds(base + u * TOK, TOK), :2 * HEAD_DIM], qcat, None,
        s_scr, p_scr, t_scr)
    first, second = mix(p_scr, t_scr, CHUNKS * TOK, kv[pl.ds(base, CHUNKS * TOK), 2 * HEAD_DIM:])
    return finish(total, tangent_total, first, second)


def plane_kernel(sel_ref, q_ref, main, up, dn, o_ref, kv, s_scr, p_scr, t_scr):
    for slot in range(PLANE + 2 * REACH):
        if slot < REACH:
            piece = up.at[slot]
        elif slot < REACH + PLANE:
            piece = main.at[slot - REACH]
        else:
            piece = dn.at[slot - REACH - PLANE]
        kv[slot * TOK:(slot + 1) * TOK, :] = piece[...]

    def step(i, carry):
        base = pl.multiple_of(i * TOK, TOK)
        o_ref[i] = whole(sel_ref, i, base, q_ref[i, :TOK, :], kv, s_scr, p_scr, t_scr)
        return carry

    lax.fori_loop(0, PLANE, step, 0)


def pair_kernel(row_ref, sel_ref, q_own, a3, a2, a1, own, b1, b2, b3, far, gate, o_own, o_other,
                kv, s_scr, p_scr, t_scr):
    del gate
    row = row_ref[0]
    par = row % 2
    for place, piece in enumerate((a3, a2, a1, own, b1, b2, b3)):
        kv[pl.ds(pl.multiple_of((place + par) * TOK, TOK), TOK), :] = piece[:, :512]
    kv[pl.ds(pl.multiple_of((1 - par) * CHUNKS * TOK, TOK), TOK), :] = far[...]
    q_other = jnp.where(par == 1, a1[:, 512:], b1[:, 512:])
    for qcat, at, place, o_ref in ((q_own[...], row, par, o_own), (q_other, row + 1 - 2 * par, 1 - par, o_other)):
        base = pl.multiple_of(place * TOK, TOK)
        o_ref[...] = whole(sel_ref, at, base, qcat, kv, s_scr, p_scr, t_scr)


def after_kernel(*refs):
    del refs


def after(array, *others):
    return pl.pallas_call(
        after_kernel,
        out_shape=jax.ShapeDtypeStruct(array.shape, array.dtype),
        in_specs=[ANY_SPEC] + [VMEM_SPEC] * len(others),
        out_specs=ANY_SPEC,
        input_output_aliases={0: 0},
        compiler_params=params(1),
        name="after",
    )(array, *others)


def unpack_kernel(par_ref, mine, own, other, o_ref, t_ref):
    par = par_ref[0] % 2
    for j in range(PLANE):
        cols = pl.ds(j * HEAD_DIM, HEAD_DIM)
        o_ref[:, cols] = mine[j, :, :HEAD_DIM]
        t_ref[:, cols] = mine[j, :, HEAD_DIM:]
    for which, piece in ((par, own), (1 - par, other)):
        cols = pl.ds(pl.multiple_of((PLANE + which) * HEAD_DIM, HEAD_DIM), HEAD_DIM)
        o_ref[:, cols] = piece[:, :HEAD_DIM]
        t_ref[:, cols] = piece[:, HEAD_DIM:]


def bf16(*shape):
    return jax.ShapeDtypeStruct(shape, jnp.bfloat16)


def f32(*shape):
    return jax.ShapeDtypeStruct(shape, jnp.float32)


def scratch(chunks):
    return [
        pltpu.VMEM((TOK, chunks * TOK), jnp.float32),
        pltpu.VMEM((TOK, chunks * TOK), jnp.bfloat16),
        pltpu.VMEM((TOK, chunks * TOK), jnp.bfloat16),
    ]


def cost(chunks):
    products = chunks * TOK * TOK
    return pl.CostEstimate(flops=10 * HEAD_DIM * products, bytes_accessed=chunks * 2 * TOK * 4 * HEAD_DIM,
                           transcendentals=products)


def params(mib):
    return pltpu.CompilerParams(vmem_limit_bytes=mib * MIB)


def body(queries, query_tangents, keys, key_tangents, values, value_tangents, selection):
    devices = lax.axis_size("ctx")
    row = (lax.axis_index("ctx") % PLANE).astype(jnp.int32)[None]
    planes = [[z * PLANE + i for i in range(PLANE)] for z in range(devices // PLANE)]

    def send(array, by):
        return lax.ppermute(array, "ctx", [(i, (i + by) % devices) for i in range(devices)])

    def swapped(array):
        return lax.ppermute(array, "ctx", [(i, i ^ 1) for i in range(devices)])

    def exchange(array):
        return lax.all_to_all(array, "ctx", 0, 0, axis_index_groups=planes, tiled=True)

    wide = [pltpu.with_memory_space_constraint(array, pltpu.HBM) for array in
            (queries, query_tangents, keys, key_tangents, values, value_tangents)]
    kv_out = pl.pallas_call(
        cut_keys_kernel,
        grid=(PLANE,),
        out_shape=pltpu.HBM((PLANE, TOK, 512), jnp.bfloat16),
        in_specs=[pl.BlockSpec((TOK, HEAD_DIM), lambda j: (0, j))] * 4,
        out_specs=pl.BlockSpec((1, TOK, 512), lambda j: (j, 0, 0)),
        compiler_params=params(8),
        name="cut_keys",
    )(*wide[2:])
    sel_rows = jnp.pad(selection.astype(jnp.bfloat16).reshape(1, 2 * WIN), ((0, EXTRA - 1), (0, 256 - 2 * WIN)))
    q_out, kv_same, kv_opp, near, q_same = pl.pallas_call(
        cut_rest_kernel,
        out_shape=(bf16(PLANE, TOK + EXTRA, 256), bf16(TOK, 512), bf16(TOK, 512), bf16(TOK, 768), bf16(TOK, 256)),
        in_specs=[SMEM_SPEC, VMEM_SPEC] + [HBM_SPEC] * 6,
        out_specs=(VMEM_SPEC,) * 5,
        scratch_shapes=[pltpu.SemaphoreType.DMA((2 * PLANE + 16,))],
        compiler_params=params(8),
        name="cut_rest",
    )(row, sel_rows, *wide)

    main = exchange(kv_out)
    up, dn = send(main[PLANE - REACH:], PLANE), send(main[:REACH], -PLANE)
    q_all = exchange(after(q_out, main))
    sel_all = q_all[:, TOK, :2 * WIN].astype(jnp.int32)

    near = after(near, main)
    a1, b1 = send(near, 1), send(near, -1)
    kv_same, kv_opp = after(kv_same, sel_all, a1, b1), after(kv_opp, sel_all, a1, b1)
    a2, b2, a3, b3 = send(kv_same, 2), send(kv_same, -2), send(kv_opp, 3), send(kv_opp, -3)
    far = lax.ppermute(kv_same, "ctx", [(i, (i - 4 + 8 * (i % 2)) % devices) for i in range(devices)])

    mine = pl.pallas_call(
        plane_kernel,
        out_shape=bf16(PLANE, TOK, 256),
        in_specs=[SMEM_SPEC] + [VMEM_SPEC] * 4,
        out_specs=VMEM_SPEC,
        scratch_shapes=[pltpu.VMEM(((PLANE + 2 * REACH) * TOK, 512), jnp.bfloat16)] + scratch(CHUNKS),
        compiler_params=params(16),
        cost_estimate=cost(56),
        name="plane",
    )(sel_all, q_all, main, up, dn)
    own, other = pl.pallas_call(
        pair_kernel,
        out_shape=(bf16(TOK, 256), bf16(TOK, 256)),
        in_specs=[SMEM_SPEC] * 2 + [VMEM_SPEC] * 10,
        out_specs=(VMEM_SPEC,) * 2,
        scratch_shapes=[pltpu.VMEM((8 * TOK, 512), jnp.bfloat16)] + scratch(CHUNKS),
        compiler_params=params(12),
        cost_estimate=cost(14),
        name="pair",
    )(row, sel_all, q_same, a3, a2, a1, kv_same, b1, b2, b3, far, mine)
    partner = swapped(other)
    back = exchange(after(mine, other))

    return pl.pallas_call(
        unpack_kernel,
        out_shape=(bf16(TOK, HEADS * HEAD_DIM), bf16(TOK, HEADS * HEAD_DIM)),
        in_specs=[SMEM_SPEC] + [VMEM_SPEC] * 3,
        out_specs=(VMEM_SPEC,) * 2,
        compiler_params=params(6),
        name="unpack",
    )(row, back, own, partner)


def solution(mesh):
    wide = P("ctx", "head")
    return jax.shard_map(
        body,
        mesh=mesh,
        in_specs=(wide,) * 6 + (P("ctx", None),),
        out_specs=(wide, wide),
        check_vma=False,
    )
```

```python
import jax
import jax.numpy as jnp
from jax import lax
from jax.experimental import pallas as pl
from jax.experimental.pallas import tpu as pltpu
from jax.sharding import PartitionSpec as P

HEADS = 10
HEAD_DIM = 128
BLK = 128
REACH = 3
TOK = 256
WIN = 14
PLANE = 8
CHUNKS = 2 * REACH + 1
EXTRA = 8
KV = 4 * HEAD_DIM
ALL = 6 * HEAD_DIM
CROSSING = (((7, 2), (6, 0), (5, 1)), ((7, 3), (6, 1), (5, 0)), ((7, 0),), ((7, 1),))
NEG = -1.0e30
LOG2E = 1.4426950408889634
SCALE = HEAD_DIM ** -0.5
FACTOR = SCALE * LOG2E
MIB = 1 << 20

VMEM_SPEC = pl.BlockSpec(memory_space=pltpu.VMEM)
HBM_SPEC = pl.BlockSpec(memory_space=pltpu.HBM)
ANY_SPEC = pl.BlockSpec(memory_space=pl.ANY)
SMEM_SPEC = pl.BlockSpec(memory_space=pltpu.SMEM)


def run_copies(pairs, sem):
    copies = [pltpu.make_async_copy(source, target, sem.at[n]) for n, (source, target) in enumerate(pairs)]
    for copy in copies:
        copy.start()
    for copy in copies:
        copy.wait()


def lanes(n):
    return pl.ds(n * HEAD_DIM, HEAD_DIM)


def cut_plane_kernel(sel, q, qt, k, kt, v, vt, out, buf, in_sem, out_sem):
    arrays = (k, kt, v, vt, qt, q)
    ins = [[pltpu.make_async_copy(ref.at[:, lanes(j)], buf.at[j, 0:TOK, lanes(n)], in_sem.at[j, n])
            for n, ref in enumerate(arrays)] for j in range(PLANE)]
    outs = [pltpu.make_async_copy(buf.at[j], out.at[j], out_sem.at[j]) for j in range(PLANE)]
    for chunk in ins:
        for copy in chunk:
            copy.start()
    for j in range(PLANE):
        buf[j, TOK:, :] = sel[...]
        for copy in ins[j]:
            copy.wait()
        outs[j].start()
    for copy in outs:
        copy.wait()


def cut_pair_kernel(row_ref, q, qt, k, kt, v, vt, rest, first, second, q_same, q_opp, buf, in_sem, out_sem):
    arrays = (k, kt, v, vt, qt, q)
    ins = [pltpu.make_async_copy(ref.at[:, lanes(PLANE + h)], buf.at[h, :, lanes(n)], in_sem.at[h, n])
           for h in range(2) for n, ref in enumerate(arrays)]
    outs = [pltpu.make_async_copy(buf.at[j % 2, :, 0:KV], rest.at[j], out_sem.at[j]) for j in range(PLANE)]
    for copy in ins:
        copy.start()
    for copy in ins:
        copy.wait()
    for copy in outs:
        copy.start()
    row = row_ref[0]
    par = row % 2
    bit = jnp.where(jnp.logical_or(row < 2, row == 5), 1, 0)
    first[...] = buf[bit, :, :KV]
    second[...] = buf[1 - bit, :, :KV]
    q_same[...] = buf[par, :, KV:]
    q_opp[...] = buf[1 - par, :, KV:]
    for copy in outs:
        copy.wait()


def weigh(sel_ref, row, first, count, chunk, qcat, floor, s_scr, p_scr, t_scr):
    dims = (((1,), (1,)), ((), ()))
    query = qcat[:, HEAD_DIM:]
    peak = [None, None]
    for u in range(count):
        s = lax.dot_general(query, chunk(u)[:, :HEAD_DIM], dims, preferred_element_type=jnp.float32)
        for qb in range(2):
            for kb in range(2):
                listed = sel_ref[row, qb * WIN + 2 * (first + u) + kb]
                piece = s[qb * BLK:(qb + 1) * BLK, kb * BLK:(kb + 1) * BLK] + jnp.where(listed != 0, 0.0, NEG)
                s_scr[qb * BLK:(qb + 1) * BLK, u * TOK + kb * BLK:u * TOK + (kb + 1) * BLK] = piece
                peak[qb] = piece if peak[qb] is None else jnp.maximum(peak[qb], piece)
    top = jnp.concatenate([jnp.max(p, axis=1, keepdims=True) for p in peak], axis=0) * FACTOR
    if floor is not None:
        top = jnp.maximum(top, floor)
    total = jnp.zeros((TOK, BLK), jnp.float32)
    tangent_total = jnp.zeros((TOK, BLK), jnp.float32)
    for u in range(count):
        st = lax.dot_general(qcat, chunk(u), dims, preferred_element_type=jnp.float32)
        weights = jnp.exp2(s_scr[:, u * TOK:(u + 1) * TOK] * FACTOR - top)
        weighted = weights * st
        total += weights[:, :BLK] + weights[:, BLK:]
        tangent_total += weighted[:, :BLK] + weighted[:, BLK:]
        p_scr[:, u * TOK:(u + 1) * TOK] = weights.astype(jnp.bfloat16)
        t_scr[:, u * TOK:(u + 1) * TOK] = weighted.astype(jnp.bfloat16)
    return top, total, tangent_total


def finish(total, tangent_total, first, second):
    inverse = 1.0 / jnp.sum(total, axis=1, keepdims=True)
    out = first[:, :HEAD_DIM] * inverse
    tangent_sum = jnp.sum(tangent_total, axis=1, keepdims=True)
    tangent = ((second - out * tangent_sum) * SCALE + first[:, HEAD_DIM:]) * inverse
    return jnp.concatenate([out.astype(jnp.bfloat16), tangent.astype(jnp.bfloat16)], axis=1)


def mix(p_scr, t_scr, width, values):
    first = jnp.dot(p_scr[:, :width], values, preferred_element_type=jnp.float32)
    second = jnp.dot(t_scr[:, :width], values[:, :HEAD_DIM], preferred_element_type=jnp.float32)
    return first, second


def inner_kernel(sel_ref, main, o_ref, stats, first_ref, second_ref, vv, s_scr, p_scr, t_scr):
    for c in range(PLANE):
        vv[c * TOK:(c + 1) * TOK, :] = main[c, :TOK, 2 * HEAD_DIM:KV]

    def position(i, count, final):
        begin = jnp.maximum(i - REACH, 0)
        base = pl.multiple_of(begin * TOK, TOK)
        top, total, tangent_total = weigh(
            sel_ref, i, jnp.maximum(REACH - i, 0), count, lambda u: main[begin + u, :TOK, :2 * HEAD_DIM],
            main[i, :TOK, KV:], None, s_scr, p_scr, t_scr)
        first, second = mix(p_scr, t_scr, count * TOK, vv[pl.ds(base, count * TOK), :])
        if final:
            o_ref[i - REACH] = finish(total, tangent_total, first, second)
        else:
            stats[i, 0] = jnp.broadcast_to(top, (TOK, BLK))
            stats[i, 1] = total
            stats[i, 2] = tangent_total
            first_ref[i] = first
            second_ref[i] = second

    def step(n, carry):
        for low in range(REACH + 1):
            position(low + n * (PLANE - 1 - 2 * low), low + REACH + 1, low == REACH)
        return carry

    lax.fori_loop(0, 2, step, 0)


def outer_kernel(sel_ref, main, up, dn, mid, stats, first_ref, second_ref, o_ref, s_scr, p_scr, t_scr):
    for i in (3, 4):
        o_ref[i] = mid[i - REACH]
    for i in (0, 1, 2, 5, 6, 7):
        low = i < REACH
        halo, skip, at = (up, i, 0) if low else (dn, 0, PLANE + REACH - i)
        count = REACH - i if low else i - REACH - 1
        before = stats[i, 0][:, :1]
        top, total, tangent_total = weigh(
            sel_ref, i, at, count, lambda u: halo[skip + u, :, :2 * HEAD_DIM], main[i, :TOK, KV:], before,
            s_scr, p_scr, t_scr)
        shrink = jnp.exp2(before - top)
        first, second = first_ref[i] * shrink, second_ref[i] * shrink
        for u in range(count):
            more = mix(p_scr.at[:, u * TOK:(u + 1) * TOK], t_scr.at[:, u * TOK:(u + 1) * TOK], TOK,
                       halo[skip + u, :, 2 * HEAD_DIM:])
            first, second = first + more[0], second + more[1]
        o_ref[i] = finish(stats[i, 1] * shrink + total, stats[i, 2] * shrink + tangent_total, first, second)


def crossing_places():
    unused = PLANE + 2 * REACH
    tables = []
    for pairs in CROSSING:
        table = [unused] * PLANE
        for source, target in pairs:
            table[target] = source - (PLANE - REACH)
            table[PLANE - 1 - target] = PLANE + REACH + PLANE - 1 - source
        tables.append(table)
    return tables


def pair_kernel(row_ref, sel_ref, q_own, q_other, main, c0, c1, c2, c3, o_own, o_other, kv, s_scr, p_scr, t_scr):
    row = row_ref[0]
    for c in range(PLANE):
        kv[(c + REACH) * TOK:(c + REACH + 1) * TOK, :] = main[c]
    for ref, table in zip((c0, c1, c2, c3), crossing_places()):
        place = jnp.int32(table[0])
        for d in range(1, PLANE):
            place = jnp.where(row == d, table[d], place)
        kv[pl.ds(pl.multiple_of(place * TOK, TOK), TOK), :] = ref[...]
    for ref, at, o_ref in ((q_own, row, o_own), (q_other, row + 1 - 2 * (row % 2), o_other)):
        base = pl.multiple_of(at * TOK, TOK)
        _, total, tangent_total = weigh(
            sel_ref, at, 0, CHUNKS, lambda u: kv[pl.ds(base + u * TOK, TOK), :2 * HEAD_DIM], ref[...], None,
            s_scr, p_scr, t_scr)
        first, second = mix(p_scr, t_scr, CHUNKS * TOK, kv[pl.ds(base, CHUNKS * TOK), 2 * HEAD_DIM:])
        o_ref[...] = finish(total, tangent_total, first, second)


def after_kernel(*refs):
    del refs


def after(array, *others):
    return pl.pallas_call(
        after_kernel,
        out_shape=pltpu.HBM(array.shape, array.dtype),
        in_specs=[HBM_SPEC] + [ANY_SPEC] * len(others),
        out_specs=HBM_SPEC,
        input_output_aliases={0: 0},
        compiler_params=params(1),
        name="after",
    )(pltpu.with_memory_space_constraint(array, pltpu.HBM), *others)


def unpack_kernel(par_ref, mine, own, other, o_ref, t_ref):
    par = par_ref[0] % 2
    for j in range(PLANE):
        cols = pl.ds(j * HEAD_DIM, HEAD_DIM)
        o_ref[:, cols] = mine[j, :, :HEAD_DIM]
        t_ref[:, cols] = mine[j, :, HEAD_DIM:]
    for which, piece in ((par, own), (1 - par, other)):
        cols = pl.ds(pl.multiple_of((PLANE + which) * HEAD_DIM, HEAD_DIM), HEAD_DIM)
        o_ref[:, cols] = piece[:, :HEAD_DIM]
        t_ref[:, cols] = piece[:, HEAD_DIM:]


def bf16(*shape):
    return jax.ShapeDtypeStruct(shape, jnp.bfloat16)


def f32(*shape):
    return jax.ShapeDtypeStruct(shape, jnp.float32)


def scratch(chunks):
    return [
        pltpu.VMEM((TOK, chunks * TOK), jnp.float32),
        pltpu.VMEM((TOK, chunks * TOK), jnp.bfloat16),
        pltpu.VMEM((TOK, chunks * TOK), jnp.bfloat16),
    ]


def cost(chunks):
    products = chunks * TOK * TOK
    return pl.CostEstimate(flops=10 * HEAD_DIM * products, bytes_accessed=chunks * 2 * TOK * 4 * HEAD_DIM,
                           transcendentals=products)


def params(mib):
    return pltpu.CompilerParams(vmem_limit_bytes=mib * MIB)


def body(queries, query_tangents, keys, key_tangents, values, value_tangents, selection):
    devices = lax.axis_size("ctx")
    row = (lax.axis_index("ctx") % PLANE).astype(jnp.int32)[None]
    planes = [[z * PLANE + i for i in range(PLANE)] for z in range(devices // PLANE)]

    def send(array, by):
        return lax.ppermute(array, "ctx", [(i, (i + by) % devices) for i in range(devices)])

    def swapped(array):
        return lax.ppermute(array, "ctx", [(i, i ^ 1) for i in range(devices)])

    def cross(array, pairs):
        last = PLANE - 1
        moves = [(z * PLANE + a, (z * PLANE + PLANE + b) % devices) for z in range(devices // PLANE) for a, b in pairs]
        moves += [(z * PLANE + last - a, (z * PLANE - PLANE + last - b) % devices)
                  for z in range(devices // PLANE) for a, b in pairs]
        return lax.ppermute(array, "ctx", moves)

    def exchange(array):
        return lax.all_to_all(array, "ctx", 0, 0, axis_index_groups=planes, tiled=True)

    wide = [pltpu.with_memory_space_constraint(array, pltpu.HBM) for array in
            (queries, query_tangents, keys, key_tangents, values, value_tangents)]
    sel_rows = jnp.pad(selection.astype(jnp.bfloat16).reshape(1, 2 * WIN), ((0, EXTRA - 1), (0, ALL - 2 * WIN)))
    plane_out = pl.pallas_call(
        cut_plane_kernel,
        out_shape=pltpu.HBM((PLANE, TOK + EXTRA, ALL), jnp.bfloat16),
        in_specs=[VMEM_SPEC] + [HBM_SPEC] * 6,
        out_specs=ANY_SPEC,
        scratch_shapes=[pltpu.VMEM((PLANE, TOK + EXTRA, ALL), jnp.bfloat16),
                        pltpu.SemaphoreType.DMA((PLANE, 6)), pltpu.SemaphoreType.DMA((PLANE,))],
        compiler_params=params(8),
        name="cut_plane",
    )(sel_rows, *wide)
    rest_out, first_out, second_out, q_same, q_opp = pl.pallas_call(
        cut_pair_kernel,
        out_shape=(pltpu.HBM((PLANE, TOK, KV), jnp.bfloat16), bf16(TOK, KV), bf16(TOK, KV), bf16(TOK, 256), bf16(TOK, 256)),
        in_specs=[SMEM_SPEC] + [HBM_SPEC] * 6,
        out_specs=(ANY_SPEC,) + (VMEM_SPEC,) * 4,
        scratch_shapes=[pltpu.VMEM((2, TOK, ALL), jnp.bfloat16),
                        pltpu.SemaphoreType.DMA((2, 6)), pltpu.SemaphoreType.DMA((PLANE,))],
        compiler_params=params(8),
        name="cut_pair",
    )(row, *wide)

    crossed = [cross(array, pairs) for array, pairs in zip((first_out, second_out) * 2, CROSSING)]
    q_other = swapped(q_opp)

    main = exchange(plane_out)
    sel_all = main[:, TOK, :2 * WIN].astype(jnp.int32)
    edge_up, edge_dn = main[PLANE - REACH:, :TOK, :KV], main[:REACH, :TOK, :KV]
    up, dn = send(edge_up, PLANE), send(edge_dn, -PLANE)
    rest = exchange(after(rest_out, sel_all, q_other, *crossed))

    mid, stats, first, second = pl.pallas_call(
        inner_kernel,
        out_shape=(bf16(2, TOK, 256), f32(PLANE, 3, TOK, BLK), f32(PLANE, TOK, 256), f32(PLANE, TOK, BLK)),
        in_specs=[SMEM_SPEC, VMEM_SPEC],
        out_specs=(VMEM_SPEC,) * 4,
        scratch_shapes=[pltpu.VMEM((PLANE * TOK, 2 * HEAD_DIM), jnp.bfloat16)] + scratch(CHUNKS),
        compiler_params=params(16),
        cost_estimate=cost(44),
        name="inner",
    )(sel_all, main)
    mine = pl.pallas_call(
        outer_kernel,
        out_shape=bf16(PLANE, TOK, 256),
        in_specs=[SMEM_SPEC] + [VMEM_SPEC] * 7,
        out_specs=VMEM_SPEC,
        scratch_shapes=scratch(REACH),
        compiler_params=params(16),
        cost_estimate=cost(12),
        name="outer",
    )(sel_all, main, up, dn, mid, stats, first, second)
    back = exchange(after(mine, rest))

    own, lent = pl.pallas_call(
        pair_kernel,
        out_shape=(bf16(TOK, 256), bf16(TOK, 256)),
        in_specs=[SMEM_SPEC] * 2 + [VMEM_SPEC] * 7,
        out_specs=(VMEM_SPEC,) * 2,
        scratch_shapes=[pltpu.VMEM(((PLANE + 2 * REACH + 1) * TOK, KV), jnp.bfloat16)] + scratch(CHUNKS),
        compiler_params=params(14),
        cost_estimate=cost(14),
        name="pair",
    )(row, sel_all, q_same, q_other, rest, *crossed)
    partner = swapped(lent)

    return pl.pallas_call(
        unpack_kernel,
        out_shape=(bf16(TOK, HEADS * HEAD_DIM), bf16(TOK, HEADS * HEAD_DIM)),
        in_specs=[SMEM_SPEC] + [VMEM_SPEC] * 3,
        out_specs=(VMEM_SPEC,) * 2,
        compiler_params=params(6),
        name="unpack",
    )(row, back, own, partner)


def solution(mesh):
    wide = P("ctx", "head")
    return jax.shard_map(
        body,
        mesh=mesh,
        in_specs=(wide,) * 6 + (P("ctx", None),),
        out_specs=(wide, wide),
        check_vma=False,
    )
```

```python
import jax
import jax.numpy as jnp
from jax import lax
from jax.experimental import pallas as pl
from jax.experimental.pallas import tpu as pltpu
from jax.sharding import PartitionSpec as P

HEADS = 10
HEAD_DIM = 128
BLK = 128
REACH = 3
TOK = 256
WIN = 14
PLANE = 8
CHUNKS = 2 * REACH + 1
EXTRA = 8
KV = 4 * HEAD_DIM
ALL = 6 * HEAD_DIM
NEG = -1.0e30
LOG2E = 1.4426950408889634
SCALE = HEAD_DIM ** -0.5
FACTOR = SCALE * LOG2E
MIB = 1 << 20

VMEM_SPEC = pl.BlockSpec(memory_space=pltpu.VMEM)
HBM_SPEC = pl.BlockSpec(memory_space=pltpu.HBM)
ANY_SPEC = pl.BlockSpec(memory_space=pl.ANY)
SMEM_SPEC = pl.BlockSpec(memory_space=pltpu.SMEM)


def run_copies(pairs, sem):
    copies = [pltpu.make_async_copy(source, target, sem.at[n]) for n, (source, target) in enumerate(pairs)]
    for copy in copies:
        copy.start()
    for copy in copies:
        copy.wait()


def lanes(n):
    return pl.ds(n * HEAD_DIM, HEAD_DIM)


def cut_plane_kernel(sel, q, qt, k, kt, v, vt, out, buf, in_sem, out_sem):
    arrays = (k, kt, v, vt, qt, q)
    ins = [[pltpu.make_async_copy(ref.at[:, lanes(j)], buf.at[j, 0:TOK, lanes(n)], in_sem.at[j, n])
            for n, ref in enumerate(arrays)] for j in range(PLANE)]
    outs = [pltpu.make_async_copy(buf.at[j], out.at[j], out_sem.at[j]) for j in range(PLANE)]
    for chunk in ins:
        for copy in chunk:
            copy.start()
    for j in range(PLANE):
        buf[j, TOK:, :] = sel[...]
        for copy in ins[j]:
            copy.wait()
        outs[j].start()
    for copy in outs:
        copy.wait()


def cut_pair_kernel(row_ref, q, qt, k, kt, v, vt, rest, q_same, q_opp, buf, in_sem, out_sem):
    arrays = (k, kt, v, vt, qt, q)
    ins = [pltpu.make_async_copy(ref.at[:, lanes(PLANE + h)], buf.at[h, :, lanes(n)], in_sem.at[h, n])
           for h in range(2) for n, ref in enumerate(arrays)]
    outs = [pltpu.make_async_copy(buf.at[j % 2, :, 0:KV], rest.at[j], out_sem.at[j]) for j in range(PLANE)]
    for copy in ins:
        copy.start()
    for copy in ins:
        copy.wait()
    for copy in outs:
        copy.start()
    par = row_ref[0] % 2
    q_same[...] = buf[par, :, KV:]
    q_opp[...] = buf[1 - par, :, KV:]
    for copy in outs:
        copy.wait()


def weigh(sel_ref, row, first, count, chunk, qcat, floor, s_scr, p_scr, t_scr):
    dims = (((1,), (1,)), ((), ()))
    query = qcat[:, HEAD_DIM:]
    peak = [None, None]
    for u in range(count):
        s = lax.dot_general(query, chunk(u)[:, :HEAD_DIM], dims, preferred_element_type=jnp.float32)
        for qb in range(2):
            for kb in range(2):
                listed = sel_ref[row, qb * WIN + 2 * (first + u) + kb]
                piece = s[qb * BLK:(qb + 1) * BLK, kb * BLK:(kb + 1) * BLK] + jnp.where(listed != 0, 0.0, NEG)
                s_scr[qb * BLK:(qb + 1) * BLK, u * TOK + kb * BLK:u * TOK + (kb + 1) * BLK] = piece
                peak[qb] = piece if peak[qb] is None else jnp.maximum(peak[qb], piece)
    top = jnp.concatenate([jnp.max(p, axis=1, keepdims=True) for p in peak], axis=0) * FACTOR
    if floor is not None:
        top = jnp.maximum(top, floor)
    total = jnp.zeros((TOK, BLK), jnp.float32)
    tangent_total = jnp.zeros((TOK, BLK), jnp.float32)
    for u in range(count):
        st = lax.dot_general(qcat, chunk(u), dims, preferred_element_type=jnp.float32)
        weights = jnp.exp2(s_scr[:, u * TOK:(u + 1) * TOK] * FACTOR - top)
        weighted = weights * st
        total += weights[:, :BLK] + weights[:, BLK:]
        tangent_total += weighted[:, :BLK] + weighted[:, BLK:]
        p_scr[:, u * TOK:(u + 1) * TOK] = weights.astype(jnp.bfloat16)
        t_scr[:, u * TOK:(u + 1) * TOK] = weighted.astype(jnp.bfloat16)
    return top, total, tangent_total


def finish(total, tangent_total, first, second):
    inverse = 1.0 / jnp.sum(total, axis=1, keepdims=True)
    out = first[:, :HEAD_DIM] * inverse
    tangent_sum = jnp.sum(tangent_total, axis=1, keepdims=True)
    tangent = ((second - out * tangent_sum) * SCALE + first[:, HEAD_DIM:]) * inverse
    return jnp.concatenate([out.astype(jnp.bfloat16), tangent.astype(jnp.bfloat16)], axis=1)


def mix(p_scr, t_scr, width, values):
    first = jnp.dot(p_scr[:, :width], values, preferred_element_type=jnp.float32)
    second = jnp.dot(t_scr[:, :width], values[:, :HEAD_DIM], preferred_element_type=jnp.float32)
    return first, second


def inner_kernel(sel_ref, main, o_ref, stats, first_ref, second_ref, vv, s_scr, p_scr, t_scr):
    for c in range(PLANE):
        vv[c * TOK:(c + 1) * TOK, :] = main[c, :TOK, 2 * HEAD_DIM:KV]

    def position(i, count, final):
        begin = jnp.maximum(i - REACH, 0)
        base = pl.multiple_of(begin * TOK, TOK)
        top, total, tangent_total = weigh(
            sel_ref, i, jnp.maximum(REACH - i, 0), count, lambda u: main[begin + u, :TOK, :2 * HEAD_DIM],
            main[i, :TOK, KV:], None, s_scr, p_scr, t_scr)
        first, second = mix(p_scr, t_scr, count * TOK, vv[pl.ds(base, count * TOK), :])
        if final:
            o_ref[i - REACH] = finish(total, tangent_total, first, second)
        else:
            stats[i, 0] = jnp.broadcast_to(top, (TOK, BLK))
            stats[i, 1] = total
            stats[i, 2] = tangent_total
            first_ref[i] = first
            second_ref[i] = second

    def step(n, carry):
        for low in range(REACH + 1):
            position(low + n * (PLANE - 1 - 2 * low), low + REACH + 1, low == REACH)
        return carry

    lax.fori_loop(0, 2, step, 0)


def outer_kernel(sel_ref, main, up, dn, mid, stats, first_ref, second_ref, o_ref, done, s_scr, p_scr, t_scr):
    done[...] = jnp.zeros_like(done)
    for i in (3, 4):
        o_ref[i] = mid[i - REACH]
    for i in (0, 1, 2, 5, 6, 7):
        low = i < REACH
        halo, skip, at = (up, i, 0) if low else (dn, 0, PLANE + REACH - i)
        count = REACH - i if low else i - REACH - 1
        before = stats[i, 0][:, :1]
        top, total, tangent_total = weigh(
            sel_ref, i, at, count, lambda u: halo[skip + u, :, :2 * HEAD_DIM], main[i, :TOK, KV:], before,
            s_scr, p_scr, t_scr)
        shrink = jnp.exp2(before - top)
        first, second = first_ref[i] * shrink, second_ref[i] * shrink
        for u in range(count):
            more = mix(p_scr.at[:, u * TOK:(u + 1) * TOK], t_scr.at[:, u * TOK:(u + 1) * TOK], TOK,
                       halo[skip + u, :, 2 * HEAD_DIM:])
            first, second = first + more[0], second + more[1]
        o_ref[i] = finish(stats[i, 1] * shrink + total, stats[i, 2] * shrink + tangent_total, first, second)


def edge_kernel(task_ref, main, gate, edge):
    del gate
    begin = jnp.where(task_ref[0] < PLANE // 2, PLANE - REACH, 0)
    for n in range(REACH):
        edge[n] = main[begin + n]


def pair_kernel(task_ref, sel_ref, q_first, q_second, main, halo, o_first, o_second, kv, s_scr, p_scr, t_scr):
    task = task_ref[0]
    for c in range(PLANE):
        kv[(c + REACH) * TOK:(c + REACH + 1) * TOK, :] = main[c]
    begin = jnp.where(task < PLANE // 2, 0, REACH + PLANE)
    for n in range(REACH):
        kv[pl.ds(pl.multiple_of((begin + n) * TOK, TOK), TOK), :] = halo[n]
    for ref, at, o_ref in ((q_first, task, o_first), (q_second, task + 1 - 2 * (task % 2), o_second)):
        base = pl.multiple_of(at * TOK, TOK)
        _, total, tangent_total = weigh(
            sel_ref, at, 0, CHUNKS, lambda u: kv[pl.ds(base + u * TOK, TOK), :2 * HEAD_DIM], ref[...], None,
            s_scr, p_scr, t_scr)
        first, second = mix(p_scr, t_scr, CHUNKS * TOK, kv[pl.ds(base, CHUNKS * TOK), 2 * HEAD_DIM:])
        o_ref[...] = finish(total, tangent_total, first, second)


def after_kernel(*refs):
    del refs


def after(array, *others):
    return pl.pallas_call(
        after_kernel,
        out_shape=pltpu.HBM(array.shape, array.dtype),
        in_specs=[HBM_SPEC] + [ANY_SPEC] * len(others),
        out_specs=HBM_SPEC,
        input_output_aliases={0: 0},
        compiler_params=params(1),
        name="after",
    )(pltpu.with_memory_space_constraint(array, pltpu.HBM), *others)


def unpack_kernel(par_ref, mine, own, other, o_ref, t_ref):
    par = par_ref[0] % 2
    for j in range(PLANE):
        cols = pl.ds(j * HEAD_DIM, HEAD_DIM)
        o_ref[:, cols] = mine[j, :, :HEAD_DIM]
        t_ref[:, cols] = mine[j, :, HEAD_DIM:]
    for which, piece in ((par, own), (1 - par, other)):
        cols = pl.ds(pl.multiple_of((PLANE + which) * HEAD_DIM, HEAD_DIM), HEAD_DIM)
        o_ref[:, cols] = piece[:, :HEAD_DIM]
        t_ref[:, cols] = piece[:, HEAD_DIM:]


def bf16(*shape):
    return jax.ShapeDtypeStruct(shape, jnp.bfloat16)


def f32(*shape):
    return jax.ShapeDtypeStruct(shape, jnp.float32)


def scratch(chunks):
    return [
        pltpu.VMEM((TOK, chunks * TOK), jnp.float32),
        pltpu.VMEM((TOK, chunks * TOK), jnp.bfloat16),
        pltpu.VMEM((TOK, chunks * TOK), jnp.bfloat16),
    ]


def cost(chunks):
    products = chunks * TOK * TOK
    return pl.CostEstimate(flops=10 * HEAD_DIM * products, bytes_accessed=chunks * 2 * TOK * 4 * HEAD_DIM,
                           transcendentals=products)


def params(mib):
    return pltpu.CompilerParams(vmem_limit_bytes=mib * MIB)


def body(queries, query_tangents, keys, key_tangents, values, value_tangents, selection):
    devices = lax.axis_size("ctx")
    columns = lax.axis_size("head")
    row = (lax.axis_index("ctx") % PLANE).astype(jnp.int32)[None]
    task = row ^ (4 * (lax.axis_index("head") % 2).astype(jnp.int32))
    planes = [[z * PLANE + i for i in range(PLANE)] for z in range(devices // PLANE)]

    def send(array, by):
        return lax.ppermute(array, "ctx", [(i, (i + by) % devices) for i in range(devices)])

    def spread(array, target):
        pairs = [(i * columns + h, target(i, h % 2) * columns + h) for i in range(devices) for h in range(columns)]
        return lax.ppermute(array, ("ctx", "head"), pairs)

    def to_first(array):
        return spread(array, lambda i, core: i ^ (4 * core))

    def to_second(array):
        return spread(array, lambda i, core: i ^ (4 * core) ^ 1)

    def exchange(array):
        return lax.all_to_all(array, "ctx", 0, 0, axis_index_groups=planes, tiled=True)

    wide = [pltpu.with_memory_space_constraint(array, pltpu.HBM) for array in
            (queries, query_tangents, keys, key_tangents, values, value_tangents)]
    sel_rows = jnp.pad(selection.astype(jnp.bfloat16).reshape(1, 2 * WIN), ((0, EXTRA - 1), (0, ALL - 2 * WIN)))
    plane_out = pl.pallas_call(
        cut_plane_kernel,
        out_shape=pltpu.HBM((PLANE, TOK + EXTRA, ALL), jnp.bfloat16),
        in_specs=[VMEM_SPEC] + [HBM_SPEC] * 6,
        out_specs=ANY_SPEC,
        scratch_shapes=[pltpu.VMEM((PLANE, TOK + EXTRA, ALL), jnp.bfloat16),
                        pltpu.SemaphoreType.DMA((PLANE, 6)), pltpu.SemaphoreType.DMA((PLANE,))],
        compiler_params=params(8),
        name="cut_plane",
    )(sel_rows, *wide)
    rest_out, q_same, q_opp = pl.pallas_call(
        cut_pair_kernel,
        out_shape=(pltpu.HBM((PLANE, TOK, KV), jnp.bfloat16), bf16(TOK, 256), bf16(TOK, 256)),
        in_specs=[SMEM_SPEC] + [HBM_SPEC] * 6,
        out_specs=(ANY_SPEC,) + (VMEM_SPEC,) * 2,
        scratch_shapes=[pltpu.VMEM((2, TOK, ALL), jnp.bfloat16),
                        pltpu.SemaphoreType.DMA((2, 6)), pltpu.SemaphoreType.DMA((PLANE,))],
        compiler_params=params(8),
        name="cut_pair",
    )(row, *wide)

    q_first, q_second = to_first(q_same), to_second(q_opp)

    main = exchange(plane_out)
    sel_all = main[:, TOK, :2 * WIN].astype(jnp.int32)
    edge_up, edge_dn = main[PLANE - REACH:, :TOK, :KV], main[:REACH, :TOK, :KV]
    up, dn = send(edge_up, PLANE), send(edge_dn, -PLANE)
    rest = exchange(after(rest_out, sel_all, q_first, q_second))

    mid, stats, first, second = pl.pallas_call(
        inner_kernel,
        out_shape=(bf16(2, TOK, 256), f32(PLANE, 3, TOK, BLK), f32(PLANE, TOK, 256), f32(PLANE, TOK, BLK)),
        in_specs=[SMEM_SPEC, VMEM_SPEC],
        out_specs=(VMEM_SPEC,) * 4,
        scratch_shapes=[pltpu.VMEM((PLANE * TOK, 2 * HEAD_DIM), jnp.bfloat16)] + scratch(CHUNKS),
        compiler_params=params(16),
        cost_estimate=cost(44),
        name="inner",
    )(sel_all, main)
    mine, done = pl.pallas_call(
        outer_kernel,
        out_shape=(bf16(PLANE, TOK, 256), f32(8, BLK)),
        in_specs=[SMEM_SPEC] + [VMEM_SPEC] * 7,
        out_specs=(VMEM_SPEC,) * 2,
        scratch_shapes=scratch(REACH),
        compiler_params=params(16),
        cost_estimate=cost(12),
        name="outer",
    )(sel_all, main, up, dn, mid, stats, first, second)
    edge = pl.pallas_call(
        edge_kernel,
        out_shape=bf16(REACH, TOK, KV),
        in_specs=[SMEM_SPEC, VMEM_SPEC, ANY_SPEC],
        out_specs=VMEM_SPEC,
        compiler_params=params(4),
        name="edge",
    )(task, rest, done)
    halo = spread(edge, lambda i, core: (i + (PLANE if (i ^ (4 * core)) % PLANE < PLANE // 2 else -PLANE)) % devices)
    back = exchange(after(mine, edge))

    own, lent = pl.pallas_call(
        pair_kernel,
        out_shape=(bf16(TOK, 256), bf16(TOK, 256)),
        in_specs=[SMEM_SPEC] * 2 + [VMEM_SPEC] * 4,
        out_specs=(VMEM_SPEC,) * 2,
        scratch_shapes=[pltpu.VMEM(((PLANE + 2 * REACH) * TOK, KV), jnp.bfloat16)] + scratch(CHUNKS),
        compiler_params=params(14),
        cost_estimate=cost(14),
        name="pair",
    )(task, sel_all, q_first, q_second, rest, halo)
    own, partner = to_first(own), to_second(lent)

    return pl.pallas_call(
        unpack_kernel,
        out_shape=(bf16(TOK, HEADS * HEAD_DIM), bf16(TOK, HEADS * HEAD_DIM)),
        in_specs=[SMEM_SPEC] + [VMEM_SPEC] * 3,
        out_specs=(VMEM_SPEC,) * 2,
        compiler_params=params(6),
        name="unpack",
    )(row, back, own, partner)


def solution(mesh):
    wide = P("ctx", "head")
    return jax.shard_map(
        body,
        mesh=mesh,
        in_specs=(wide,) * 6 + (P("ctx", None),),
        out_specs=(wide, wide),
        check_vma=False,
    )
```

```python
import jax
import jax.numpy as jnp
from jax import lax
from jax.experimental import pallas as pl
from jax.experimental.pallas import tpu as pltpu
from jax.sharding import PartitionSpec as P

HEADS = 10
HEAD_DIM = 128
BLK = 128
REACH = 3
TOK = 256
WIN = 14
PLANE = 8
CHUNKS = 2 * REACH + 1
EXTRA = 8
KV = 4 * HEAD_DIM
ALL = 6 * HEAD_DIM
NEG = -1.0e30
LOG2E = 1.4426950408889634
SCALE = HEAD_DIM ** -0.5
FACTOR = SCALE * LOG2E
MIB = 1 << 20

VMEM_SPEC = pl.BlockSpec(memory_space=pltpu.VMEM)
HBM_SPEC = pl.BlockSpec(memory_space=pltpu.HBM)
ANY_SPEC = pl.BlockSpec(memory_space=pl.ANY)
SMEM_SPEC = pl.BlockSpec(memory_space=pltpu.SMEM)


def run_copies(pairs, sem):
    copies = [pltpu.make_async_copy(source, target, sem.at[n]) for n, (source, target) in enumerate(pairs)]
    for copy in copies:
        copy.start()
    for copy in copies:
        copy.wait()


def lanes(n):
    return pl.ds(n * HEAD_DIM, HEAD_DIM)


def cut_plane_kernel(sel, q, qt, k, kt, v, vt, out, buf, in_sem, out_sem):
    arrays = (k, kt, v, vt, qt, q)
    ins = [[pltpu.make_async_copy(ref.at[:, lanes(j)], buf.at[j, 0:TOK, lanes(n)], in_sem.at[j, n])
            for n, ref in enumerate(arrays)] for j in range(PLANE)]
    outs = [pltpu.make_async_copy(buf.at[j], out.at[j], out_sem.at[j]) for j in range(PLANE)]
    for chunk in ins:
        for copy in chunk:
            copy.start()
    listed = sel[...].astype(jnp.float32).astype(jnp.bfloat16)
    for j in range(PLANE):
        buf[j, TOK:TOK + 2, :WIN] = listed
        for copy in ins[j]:
            copy.wait()
        outs[j].start()
    for copy in outs:
        copy.wait()


def cut_pair_kernel(row_ref, q, qt, k, kt, v, vt, rest, q_same, q_opp, buf, in_sem, out_sem):
    arrays = (k, kt, v, vt, qt, q)
    ins = [pltpu.make_async_copy(ref.at[:, lanes(PLANE + h)], buf.at[h, :, lanes(n)], in_sem.at[h, n])
           for h in range(2) for n, ref in enumerate(arrays)]
    outs = [pltpu.make_async_copy(buf.at[j % 2, :, 0:KV], rest.at[j], out_sem.at[j]) for j in range(PLANE)]
    for copy in ins:
        copy.start()
    for copy in ins:
        copy.wait()
    for copy in outs:
        copy.start()
    par = row_ref[0] % 2
    q_same[...] = buf[par, :, KV:]
    q_opp[...] = buf[1 - par, :, KV:]
    for copy in outs:
        copy.wait()


def weigh(sel_ref, row, first, count, chunk, qcat, floor, s_scr, p_scr, t_scr):
    dims = (((1,), (1,)), ((), ()))
    query = qcat[:, HEAD_DIM:]
    peak = [None, None]
    for u in range(count):
        s = lax.dot_general(query, chunk(u)[:, :HEAD_DIM], dims, preferred_element_type=jnp.float32)
        for qb in range(2):
            for kb in range(2):
                listed = sel_ref[row, qb * WIN + 2 * (first + u) + kb]
                piece = s[qb * BLK:(qb + 1) * BLK, kb * BLK:(kb + 1) * BLK] + jnp.where(listed != 0, 0.0, NEG)
                s_scr[qb * BLK:(qb + 1) * BLK, u * TOK + kb * BLK:u * TOK + (kb + 1) * BLK] = piece
                peak[qb] = piece if peak[qb] is None else jnp.maximum(peak[qb], piece)
    top = jnp.concatenate([jnp.max(p, axis=1, keepdims=True) for p in peak], axis=0) * FACTOR
    if floor is not None:
        top = jnp.maximum(top, floor)
    total = jnp.zeros((TOK, BLK), jnp.float32)
    tangent_total = jnp.zeros((TOK, BLK), jnp.float32)
    for u in range(count):
        st = lax.dot_general(qcat, chunk(u), dims, preferred_element_type=jnp.float32)
        weights = jnp.exp2(s_scr[:, u * TOK:(u + 1) * TOK] * FACTOR - top)
        weighted = weights * st
        total += weights[:, :BLK] + weights[:, BLK:]
        tangent_total += weighted[:, :BLK] + weighted[:, BLK:]
        p_scr[:, u * TOK:(u + 1) * TOK] = weights.astype(jnp.bfloat16)
        t_scr[:, u * TOK:(u + 1) * TOK] = weighted.astype(jnp.bfloat16)
    return top, total, tangent_total


def finish(total, tangent_total, first, second):
    inverse = 1.0 / jnp.sum(total, axis=1, keepdims=True)
    out = first[:, :HEAD_DIM] * inverse
    tangent_sum = jnp.sum(tangent_total, axis=1, keepdims=True)
    tangent = ((second - out * tangent_sum) * SCALE + first[:, HEAD_DIM:]) * inverse
    return jnp.concatenate([out.astype(jnp.bfloat16), tangent.astype(jnp.bfloat16)], axis=1)


def mix(p_scr, t_scr, width, values):
    first = jnp.dot(p_scr[:, :width], values, preferred_element_type=jnp.float32)
    second = jnp.dot(t_scr[:, :width], values[:, :HEAD_DIM], preferred_element_type=jnp.float32)
    return first, second


def inner_kernel(sel_ref, main, o_ref, stats, first_ref, second_ref, vv, s_scr, p_scr, t_scr):
    for c in range(PLANE):
        vv[c * TOK:(c + 1) * TOK, :] = main[c, :TOK, 2 * HEAD_DIM:KV]

    def position(i, count, final):
        begin = jnp.maximum(i - REACH, 0)
        base = pl.multiple_of(begin * TOK, TOK)
        top, total, tangent_total = weigh(
            sel_ref, i, jnp.maximum(REACH - i, 0), count, lambda u: main[begin + u, :TOK, :2 * HEAD_DIM],
            main[i, :TOK, KV:], None, s_scr, p_scr, t_scr)
        first, second = mix(p_scr, t_scr, count * TOK, vv[pl.ds(base, count * TOK), :])
        if final:
            o_ref[i - REACH] = finish(total, tangent_total, first, second)
        else:
            stats[i, 0] = jnp.broadcast_to(top, (TOK, BLK))
            stats[i, 1] = total
            stats[i, 2] = tangent_total
            first_ref[i] = first
            second_ref[i] = second

    def step(n, carry):
        for low in range(REACH + 1):
            position(low + n * (PLANE - 1 - 2 * low), low + REACH + 1, low == REACH)
        return carry

    lax.fori_loop(0, 2, step, 0)


def outer_kernel(sel_ref, main, up, dn, mid, stats, first_ref, second_ref, o_ref, done, buf, sem, s_scr, p_scr, t_scr):
    done[...] = jnp.zeros_like(done)
    copies = []

    def leave(i, value):
        buf[i] = value
        copies.append(pltpu.make_async_copy(buf.at[i], o_ref.at[i], sem.at[i]))
        copies[-1].start()

    for i in (3, 4):
        leave(i, mid[i - REACH])
    for i in (0, 1, 2, 5, 6, 7):
        low = i < REACH
        halo, skip, at = (up, i, 0) if low else (dn, 0, PLANE + REACH - i)
        count = REACH - i if low else i - REACH - 1
        before = stats[i, 0][:, :1]
        top, total, tangent_total = weigh(
            sel_ref, i, at, count, lambda u: halo[skip + u, :, :2 * HEAD_DIM], main[i, :TOK, KV:], before,
            s_scr, p_scr, t_scr)
        shrink = jnp.exp2(before - top)
        first, second = first_ref[i] * shrink, second_ref[i] * shrink
        for u in range(count):
            more = mix(p_scr.at[:, u * TOK:(u + 1) * TOK], t_scr.at[:, u * TOK:(u + 1) * TOK], TOK,
                       halo[skip + u, :, 2 * HEAD_DIM:])
            first, second = first + more[0], second + more[1]
        leave(i, finish(stats[i, 1] * shrink + total, stats[i, 2] * shrink + tangent_total, first, second))
    for copy in copies:
        copy.wait()


def edges_kernel(main, gate_a, gate_b, up, dn):
    del gate_a, gate_b
    for n in range(REACH):
        up[n] = main[PLANE - REACH + n, :TOK, :KV]
        dn[n] = main[n, :TOK, :KV]


def edge_kernel(task_ref, main, gate, edge):
    del gate
    begin = jnp.where(task_ref[0] < PLANE // 2, PLANE - REACH, 0)
    for n in range(REACH):
        edge[n] = main[begin + n]


def pair_kernel(task_ref, sel_ref, q_first, q_second, main, halo, o_first, o_second, kv, s_scr, p_scr, t_scr, sem):
    task = task_ref[0]
    begin = jnp.where(task < PLANE // 2, 0, REACH + PLANE)
    pairs = [(main.at[c], kv.at[pl.ds((c + REACH) * TOK, TOK), :]) for c in range(PLANE)]
    pairs += [(halo.at[n], kv.at[pl.ds(pl.multiple_of((begin + n) * TOK, TOK), TOK), :]) for n in range(REACH)]
    run_copies(pairs, sem)
    for ref, at, o_ref in ((q_first, task, o_first), (q_second, task + 1 - 2 * (task % 2), o_second)):
        base = pl.multiple_of(at * TOK, TOK)
        _, total, tangent_total = weigh(
            sel_ref, at, 0, CHUNKS, lambda u: kv[pl.ds(base + u * TOK, TOK), :2 * HEAD_DIM], ref[...], None,
            s_scr, p_scr, t_scr)
        first, second = mix(p_scr, t_scr, CHUNKS * TOK, kv[pl.ds(base, CHUNKS * TOK), 2 * HEAD_DIM:])
        o_ref[...] = finish(total, tangent_total, first, second)


def after_kernel(*refs):
    del refs


def after(array, *others):
    return pl.pallas_call(
        after_kernel,
        out_shape=pltpu.HBM(array.shape, array.dtype),
        in_specs=[HBM_SPEC] + [ANY_SPEC] * len(others),
        out_specs=HBM_SPEC,
        input_output_aliases={0: 0},
        compiler_params=params(1),
        name="after",
    )(pltpu.with_memory_space_constraint(array, pltpu.HBM), *others)


def unpack_kernel(par_ref, mine, own, other, o_ref, t_ref):
    par = par_ref[0] % 2
    for j in range(PLANE):
        cols = pl.ds(j * HEAD_DIM, HEAD_DIM)
        o_ref[:, cols] = mine[j, :, :HEAD_DIM]
        t_ref[:, cols] = mine[j, :, HEAD_DIM:]
    for which, piece in ((par, own), (1 - par, other)):
        cols = pl.ds(pl.multiple_of((PLANE + which) * HEAD_DIM, HEAD_DIM), HEAD_DIM)
        o_ref[:, cols] = piece[:, :HEAD_DIM]
        t_ref[:, cols] = piece[:, HEAD_DIM:]


def bf16(*shape):
    return jax.ShapeDtypeStruct(shape, jnp.bfloat16)


def f32(*shape):
    return jax.ShapeDtypeStruct(shape, jnp.float32)


def scratch(chunks):
    return [
        pltpu.VMEM((TOK, chunks * TOK), jnp.float32),
        pltpu.VMEM((TOK, chunks * TOK), jnp.bfloat16),
        pltpu.VMEM((TOK, chunks * TOK), jnp.bfloat16),
    ]


def cost(chunks):
    products = chunks * TOK * TOK
    return pl.CostEstimate(flops=10 * HEAD_DIM * products, bytes_accessed=chunks * 2 * TOK * 4 * HEAD_DIM,
                           transcendentals=products)


def params(mib):
    return pltpu.CompilerParams(vmem_limit_bytes=mib * MIB)


def body(queries, query_tangents, keys, key_tangents, values, value_tangents, selection):
    devices = lax.axis_size("ctx")
    columns = lax.axis_size("head")
    row = (lax.axis_index("ctx") % PLANE).astype(jnp.int32)[None]
    task = row ^ (4 * (lax.axis_index("head") % 2).astype(jnp.int32))
    planes = [[z * PLANE + i for i in range(PLANE)] for z in range(devices // PLANE)]

    def send(array, by):
        return lax.ppermute(array, "ctx", [(i, (i + by) % devices) for i in range(devices)])

    def spread(array, target):
        pairs = [(i * columns + h, target(i, h % 2) * columns + h) for i in range(devices) for h in range(columns)]
        return lax.ppermute(array, ("ctx", "head"), pairs)

    def to_first(array):
        return spread(array, lambda i, core: i ^ (4 * core))

    def to_second(array):
        return spread(array, lambda i, core: i ^ (4 * core) ^ 1)

    def exchange(array):
        return lax.all_to_all(array, "ctx", 0, 0, axis_index_groups=planes, tiled=True)

    wide = [pltpu.with_memory_space_constraint(array, pltpu.HBM) for array in
            (queries, query_tangents, keys, key_tangents, values, value_tangents)]
    plane_out = pl.pallas_call(
        cut_plane_kernel,
        out_shape=pltpu.HBM((PLANE, TOK + EXTRA, ALL), jnp.bfloat16),
        in_specs=[VMEM_SPEC] + [HBM_SPEC] * 6,
        out_specs=ANY_SPEC,
        scratch_shapes=[pltpu.VMEM((PLANE, TOK + EXTRA, ALL), jnp.bfloat16),
                        pltpu.SemaphoreType.DMA((PLANE, 6)), pltpu.SemaphoreType.DMA((PLANE,))],
        compiler_params=params(8),
        name="cut_plane",
    )(selection, *wide)
    rest_out, q_same, q_opp = pl.pallas_call(
        cut_pair_kernel,
        out_shape=(pltpu.HBM((PLANE, TOK, KV), jnp.bfloat16), bf16(TOK, 256), bf16(TOK, 256)),
        in_specs=[SMEM_SPEC] + [HBM_SPEC] * 6,
        out_specs=(ANY_SPEC,) + (VMEM_SPEC,) * 2,
        scratch_shapes=[pltpu.VMEM((2, TOK, ALL), jnp.bfloat16),
                        pltpu.SemaphoreType.DMA((2, 6)), pltpu.SemaphoreType.DMA((PLANE,))],
        compiler_params=params(8),
        name="cut_pair",
    )(row, *wide)

    q_first, q_second = to_first(q_same), to_second(q_opp)

    main = exchange(plane_out)
    sel_all = main[:, TOK:TOK + 2, :WIN].astype(jnp.int32).reshape(PLANE, 2 * WIN)
    edge_up, edge_dn = pl.pallas_call(
        edges_kernel,
        out_shape=(bf16(REACH, TOK, KV),) * 2,
        in_specs=[VMEM_SPEC] + [ANY_SPEC] * 2,
        out_specs=(VMEM_SPEC,) * 2,
        compiler_params=params(4),
        name="edges",
    )(main, q_first, q_second)
    up, dn = send(edge_up, PLANE), send(edge_dn, -PLANE)
    rest = exchange(after(rest_out, sel_all, q_first, q_second))

    mid, stats, first, second = pl.pallas_call(
        inner_kernel,
        out_shape=(bf16(2, TOK, 256), f32(PLANE, 3, TOK, BLK), f32(PLANE, TOK, 256), f32(PLANE, TOK, BLK)),
        in_specs=[SMEM_SPEC, VMEM_SPEC],
        out_specs=(VMEM_SPEC,) * 4,
        scratch_shapes=[pltpu.VMEM((PLANE * TOK, 2 * HEAD_DIM), jnp.bfloat16)] + scratch(CHUNKS),
        compiler_params=params(16),
        cost_estimate=cost(2),
        name="inner",
    )(sel_all, main)
    mine, done = pl.pallas_call(
        outer_kernel,
        out_shape=(pltpu.HBM((PLANE, TOK, 256), jnp.bfloat16), f32(8, BLK)),
        in_specs=[SMEM_SPEC] + [VMEM_SPEC] * 7,
        out_specs=(ANY_SPEC, VMEM_SPEC),
        scratch_shapes=[pltpu.VMEM((PLANE, TOK, 256), jnp.bfloat16), pltpu.SemaphoreType.DMA((PLANE,))] + scratch(REACH),
        compiler_params=params(16),
        cost_estimate=cost(276),
        name="outer",
    )(sel_all, main, up, dn, mid, stats, first, second)
    edge = pl.pallas_call(
        edge_kernel,
        out_shape=bf16(REACH, TOK, KV),
        in_specs=[SMEM_SPEC, VMEM_SPEC, ANY_SPEC],
        out_specs=VMEM_SPEC,
        compiler_params=params(4),
        name="edge",
    )(task, rest, done)
    halo = spread(edge, lambda i, core: (i + (PLANE if (i ^ (4 * core)) % PLANE < PLANE // 2 else -PLANE)) % devices)
    back = exchange(after(mine, edge))

    own, lent = pl.pallas_call(
        pair_kernel,
        out_shape=(bf16(TOK, 256), bf16(TOK, 256)),
        in_specs=[SMEM_SPEC] * 2 + [VMEM_SPEC] * 2 + [ANY_SPEC, HBM_SPEC],
        out_specs=(VMEM_SPEC,) * 2,
        scratch_shapes=[pltpu.VMEM(((PLANE + 2 * REACH) * TOK, KV), jnp.bfloat16)] + scratch(CHUNKS) + [pltpu.SemaphoreType.DMA((PLANE + REACH,))],
        compiler_params=params(14),
        cost_estimate=cost(14),
        name="pair",
    )(task, sel_all, q_first, q_second, rest, pltpu.with_memory_space_constraint(halo, pltpu.HBM))
    own, partner = to_first(own), to_second(lent)

    return pl.pallas_call(
        unpack_kernel,
        out_shape=(bf16(TOK, HEADS * HEAD_DIM), bf16(TOK, HEADS * HEAD_DIM)),
        in_specs=[SMEM_SPEC] + [VMEM_SPEC] * 3,
        out_specs=(VMEM_SPEC,) * 2,
        compiler_params=params(6),
        name="unpack",
    )(row, back, own, partner)


def solution(mesh):
    wide = P("ctx", "head")
    return jax.shard_map(
        body,
        mesh=mesh,
        in_specs=(wide,) * 6 + (P("ctx", None),),
        out_specs=(wide, wide),
        check_vma=False,
    )
```

```python
import jax
import jax.numpy as jnp
from jax import lax
from jax.experimental import pallas as pl
from jax.experimental.pallas import tpu as pltpu
from jax.sharding import PartitionSpec as P

HEADS = 10
HEAD_DIM = 128
BLK = 128
REACH = 3
TOK = 256
WIN = 14
PLANE = 8
CHUNKS = 2 * REACH + 1
EXTRA = 8
KV = 4 * HEAD_DIM
EARLY = 4
GATES = 3
ALL = 6 * HEAD_DIM
NEG = -1.0e30
LOG2E = 1.4426950408889634
SCALE = HEAD_DIM ** -0.5
FACTOR = SCALE * LOG2E
MIB = 1 << 20

VMEM_SPEC = pl.BlockSpec(memory_space=pltpu.VMEM)
HBM_SPEC = pl.BlockSpec(memory_space=pltpu.HBM)
ANY_SPEC = pl.BlockSpec(memory_space=pl.ANY)
SMEM_SPEC = pl.BlockSpec(memory_space=pltpu.SMEM)


def run_copies(pairs, sem):
    copies = [pltpu.make_async_copy(source, target, sem.at[n]) for n, (source, target) in enumerate(pairs)]
    for copy in copies:
        copy.start()
    for copy in copies:
        copy.wait()


def lanes(n):
    return pl.ds(n * HEAD_DIM, HEAD_DIM)


def cut_plane_kernel(sel, q, qt, k, kt, v, vt, out, buf, in_sem, out_sem):
    arrays = (k, kt, v, vt, qt, q)
    ins = [[pltpu.make_async_copy(ref.at[:, lanes(j)], buf.at[j, 0:TOK, lanes(n)], in_sem.at[j, n])
            for n, ref in enumerate(arrays)] for j in range(PLANE)]
    outs = [pltpu.make_async_copy(buf.at[j], out.at[j], out_sem.at[j]) for j in range(PLANE)]
    for chunk in ins:
        for copy in chunk:
            copy.start()
    listed = sel[...].astype(jnp.float32).astype(jnp.bfloat16)
    for j in range(PLANE):
        buf[j, TOK:TOK + 2, :WIN] = listed
        for copy in ins[j]:
            copy.wait()
        outs[j].start()
    for copy in outs:
        copy.wait()


def cut_pair_kernel(row_ref, q, qt, k, kt, v, vt, rest, q_same, q_opp, buf, in_sem, out_sem):
    arrays = (k, kt, v, vt, qt, q)
    ins = [pltpu.make_async_copy(ref.at[:, lanes(PLANE + h)], buf.at[h, :, lanes(n)], in_sem.at[h, n])
           for h in range(2) for n, ref in enumerate(arrays)]
    outs = [pltpu.make_async_copy(buf.at[j % 2, :, 0:KV], rest.at[j], out_sem.at[j]) for j in range(PLANE)]
    for copy in ins:
        copy.start()
    for copy in ins:
        copy.wait()
    for copy in outs:
        copy.start()
    par = row_ref[0] % 2
    q_same[...] = buf[par, :, KV:]
    q_opp[...] = buf[1 - par, :, KV:]
    for copy in outs:
        copy.wait()


def weigh(sel_ref, row, first, count, chunk, qcat, floor, s_scr, p_scr, t_scr):
    dims = (((1,), (1,)), ((), ()))
    query = qcat[:, HEAD_DIM:]
    peak = [None, None]
    for u in range(count):
        s = lax.dot_general(query, chunk(u)[:, :HEAD_DIM], dims, preferred_element_type=jnp.float32)
        for qb in range(2):
            for kb in range(2):
                listed = sel_ref[row, qb * WIN + 2 * (first + u) + kb]
                piece = s[qb * BLK:(qb + 1) * BLK, kb * BLK:(kb + 1) * BLK] + jnp.where(listed != 0, 0.0, NEG)
                s_scr[qb * BLK:(qb + 1) * BLK, u * TOK + kb * BLK:u * TOK + (kb + 1) * BLK] = piece
                peak[qb] = piece if peak[qb] is None else jnp.maximum(peak[qb], piece)
    top = jnp.concatenate([jnp.max(p, axis=1, keepdims=True) for p in peak], axis=0) * FACTOR
    if floor is not None:
        top = jnp.maximum(top, floor)
    total = jnp.zeros((TOK, BLK), jnp.float32)
    tangent_total = jnp.zeros((TOK, BLK), jnp.float32)
    for u in range(count):
        st = lax.dot_general(qcat, chunk(u), dims, preferred_element_type=jnp.float32)
        weights = jnp.exp2(s_scr[:, u * TOK:(u + 1) * TOK] * FACTOR - top)
        weighted = weights * st
        total += weights[:, :BLK] + weights[:, BLK:]
        tangent_total += weighted[:, :BLK] + weighted[:, BLK:]
        p_scr[:, u * TOK:(u + 1) * TOK] = weights.astype(jnp.bfloat16)
        t_scr[:, u * TOK:(u + 1) * TOK] = weighted.astype(jnp.bfloat16)
    return top, total, tangent_total


def finish(total, tangent_total, first, second):
    inverse = 1.0 / jnp.sum(total, axis=1, keepdims=True)
    out = first[:, :HEAD_DIM] * inverse
    tangent_sum = jnp.sum(tangent_total, axis=1, keepdims=True)
    tangent = ((second - out * tangent_sum) * SCALE + first[:, HEAD_DIM:]) * inverse
    return jnp.concatenate([out.astype(jnp.bfloat16), tangent.astype(jnp.bfloat16)], axis=1)


def mix(p_scr, t_scr, width, values):
    first = jnp.dot(p_scr[:, :width], values, preferred_element_type=jnp.float32)
    second = jnp.dot(t_scr[:, :width], values[:, :HEAD_DIM], preferred_element_type=jnp.float32)
    return first, second


def inner_kernel(sel_ref, main, o_ref, stats, first_ref, second_ref, vv, s_scr, p_scr, t_scr):
    for c in range(PLANE):
        vv[c * TOK:(c + 1) * TOK, :] = main[c, :TOK, 2 * HEAD_DIM:KV]

    def position(i, count, final):
        begin = jnp.maximum(i - REACH, 0)
        base = pl.multiple_of(begin * TOK, TOK)
        top, total, tangent_total = weigh(
            sel_ref, i, jnp.maximum(REACH - i, 0), count, lambda u: main[begin + u, :TOK, :2 * HEAD_DIM],
            main[i, :TOK, KV:], None, s_scr, p_scr, t_scr)
        first, second = mix(p_scr, t_scr, count * TOK, vv[pl.ds(base, count * TOK), :])
        if final:
            o_ref[i - REACH] = finish(total, tangent_total, first, second)
        else:
            stats[i, 0] = jnp.broadcast_to(top, (TOK, BLK))
            stats[i, 1] = total
            stats[i, 2] = tangent_total
            first_ref[i] = first
            second_ref[i] = second

    def step(n, carry):
        for low in range(REACH + 1):
            position(low + n * (PLANE - 1 - 2 * low), low + REACH + 1, low == REACH)
        return carry

    lax.fori_loop(0, 2, step, 0)


def outer_kernel(row_ref, sel_ref, main, up, dn, mid, stats, first_ref, second_ref, *rest):
    outs, (buf, sem, s_scr, p_scr, t_scr) = rest[:PLANE], rest[PLANE:]
    for i in (3, 4):
        buf[i] = mid[i - REACH]
    for i in (0, 1, 2, 5, 6, 7):
        low = i < REACH
        halo, skip, at = (up, i, 0) if low else (dn, 0, PLANE + REACH - i)
        count = REACH - i if low else i - REACH - 1
        before = stats[i, 0][:, :1]
        top, total, tangent_total = weigh(
            sel_ref, i, at, count, lambda u: halo[skip + u, :, :2 * HEAD_DIM], main[i, :TOK, KV:], before,
            s_scr, p_scr, t_scr)
        shrink = jnp.exp2(before - top)
        first, second = first_ref[i] * shrink, second_ref[i] * shrink
        for u in range(count):
            more = mix(p_scr.at[:, u * TOK:(u + 1) * TOK], t_scr.at[:, u * TOK:(u + 1) * TOK], TOK,
                       halo[skip + u, :, 2 * HEAD_DIM:])
            first, second = first + more[0], second + more[1]
        buf[i] = finish(stats[i, 1] * shrink + total, stats[i, 2] * shrink + tangent_total, first, second)
    run_copies([(buf.at[row_ref[0] ^ k], outs[k]) for k in range(PLANE)], sem)


def edges_kernel(main, gate_a, gate_b, up, dn):
    del gate_a, gate_b
    for n in range(REACH):
        up[n] = main[PLANE - REACH + n, :TOK, :KV]
        dn[n] = main[n, :TOK, :KV]


def edge_kernel(task_ref, main, *rest):
    edge = rest[-1]
    begin = jnp.where(task_ref[0] < PLANE // 2, PLANE - REACH, 0)
    for n in range(REACH):
        edge[n] = main[begin + n]


def pair_kernel(task_ref, sel_ref, q_first, q_second, main, halo, *rest):
    o_first, o_second, kv, s_scr, p_scr, t_scr, sem = rest[GATES:]
    task = task_ref[0]
    begin = jnp.where(task < PLANE // 2, 0, REACH + PLANE)
    pairs = [(main.at[c], kv.at[pl.ds((c + REACH) * TOK, TOK), :]) for c in range(PLANE)]
    pairs += [(halo.at[n], kv.at[pl.ds(pl.multiple_of((begin + n) * TOK, TOK), TOK), :]) for n in range(REACH)]
    run_copies(pairs, sem)
    for ref, at, o_ref in ((q_first, task, o_first), (q_second, task + 1 - 2 * (task % 2), o_second)):
        base = pl.multiple_of(at * TOK, TOK)
        _, total, tangent_total = weigh(
            sel_ref, at, 0, CHUNKS, lambda u: kv[pl.ds(base + u * TOK, TOK), :2 * HEAD_DIM], ref[...], None,
            s_scr, p_scr, t_scr)
        first, second = mix(p_scr, t_scr, CHUNKS * TOK, kv[pl.ds(base, CHUNKS * TOK), 2 * HEAD_DIM:])
        o_ref[...] = finish(total, tangent_total, first, second)


def after_kernel(*refs):
    del refs


def after(array, *others):
    return pl.pallas_call(
        after_kernel,
        out_shape=pltpu.HBM(array.shape, array.dtype),
        in_specs=[HBM_SPEC] + [ANY_SPEC] * len(others),
        out_specs=HBM_SPEC,
        input_output_aliases={0: 0},
        compiler_params=params(1),
        name="after",
    )(pltpu.with_memory_space_constraint(array, pltpu.HBM), *others)


def unpack_kernel(row_ref, *refs):
    pieces, (own, other, o_ref, t_ref) = refs[:PLANE], refs[PLANE:]
    row = row_ref[0]
    heads = [(row ^ k, piece) for k, piece in enumerate(pieces)]
    heads += [(PLANE + row % 2, own), (PLANE + 1 - row % 2, other)]
    for head, piece in heads:
        cols = pl.ds(pl.multiple_of(head * HEAD_DIM, HEAD_DIM), HEAD_DIM)
        o_ref[:, cols] = piece[:, :HEAD_DIM]
        t_ref[:, cols] = piece[:, HEAD_DIM:]


def bf16(*shape):
    return jax.ShapeDtypeStruct(shape, jnp.bfloat16)


def f32(*shape):
    return jax.ShapeDtypeStruct(shape, jnp.float32)


def scratch(chunks):
    return [
        pltpu.VMEM((TOK, chunks * TOK), jnp.float32),
        pltpu.VMEM((TOK, chunks * TOK), jnp.bfloat16),
        pltpu.VMEM((TOK, chunks * TOK), jnp.bfloat16),
    ]


def cost(chunks):
    products = chunks * TOK * TOK
    return pl.CostEstimate(flops=10 * HEAD_DIM * products, bytes_accessed=chunks * 2 * TOK * 4 * HEAD_DIM,
                           transcendentals=products)


def params(mib):
    return pltpu.CompilerParams(vmem_limit_bytes=mib * MIB)


def body(queries, query_tangents, keys, key_tangents, values, value_tangents, selection):
    devices = lax.axis_size("ctx")
    columns = lax.axis_size("head")
    row = (lax.axis_index("ctx") % PLANE).astype(jnp.int32)[None]
    task = row ^ (4 * (lax.axis_index("head") % 2).astype(jnp.int32))
    planes = [[z * PLANE + i for i in range(PLANE)] for z in range(devices // PLANE)]

    def send(array, by):
        return lax.ppermute(array, "ctx", [(i, (i + by) % devices) for i in range(devices)])

    def spread(array, target):
        pairs = [(i * columns + h, target(i, h % 2) * columns + h) for i in range(devices) for h in range(columns)]
        return lax.ppermute(array, ("ctx", "head"), pairs)

    def to_first(array):
        return spread(array, lambda i, core: i ^ (4 * core))

    def to_second(array):
        return spread(array, lambda i, core: i ^ (4 * core) ^ 1)

    def exchange(array):
        return lax.all_to_all(array, "ctx", 0, 0, axis_index_groups=planes, tiled=True)

    wide = [pltpu.with_memory_space_constraint(array, pltpu.HBM) for array in
            (queries, query_tangents, keys, key_tangents, values, value_tangents)]
    plane_out = pl.pallas_call(
        cut_plane_kernel,
        out_shape=pltpu.HBM((PLANE, TOK + EXTRA, ALL), jnp.bfloat16),
        in_specs=[VMEM_SPEC] + [HBM_SPEC] * 6,
        out_specs=ANY_SPEC,
        scratch_shapes=[pltpu.VMEM((PLANE, TOK + EXTRA, ALL), jnp.bfloat16),
                        pltpu.SemaphoreType.DMA((PLANE, 6)), pltpu.SemaphoreType.DMA((PLANE,))],
        compiler_params=params(8),
        name="cut_plane",
    )(selection, *wide)
    rest_out, q_same, q_opp = pl.pallas_call(
        cut_pair_kernel,
        out_shape=(pltpu.HBM((PLANE, TOK, KV), jnp.bfloat16), bf16(TOK, 256), bf16(TOK, 256)),
        in_specs=[SMEM_SPEC] + [HBM_SPEC] * 6,
        out_specs=(ANY_SPEC,) + (VMEM_SPEC,) * 2,
        scratch_shapes=[pltpu.VMEM((2, TOK, ALL), jnp.bfloat16),
                        pltpu.SemaphoreType.DMA((2, 6)), pltpu.SemaphoreType.DMA((PLANE,))],
        compiler_params=params(8),
        name="cut_pair",
    )(row, *wide)

    q_first, q_second = to_first(q_same), to_second(q_opp)

    main = exchange(plane_out)
    sel_all = main[:, TOK:TOK + 2, :WIN].astype(jnp.int32).reshape(PLANE, 2 * WIN)
    edge_up, edge_dn = pl.pallas_call(
        edges_kernel,
        out_shape=(bf16(REACH, TOK, KV),) * 2,
        in_specs=[VMEM_SPEC] + [ANY_SPEC] * 2,
        out_specs=(VMEM_SPEC,) * 2,
        compiler_params=params(4),
        name="edges",
    )(main, q_first, q_second)
    up, dn = send(edge_up, PLANE), send(edge_dn, -PLANE)
    rest = exchange(after(rest_out, sel_all, q_first, q_second))

    mid, stats, first, second = pl.pallas_call(
        inner_kernel,
        out_shape=(bf16(2, TOK, 256), f32(PLANE, 3, TOK, BLK), f32(PLANE, TOK, 256), f32(PLANE, TOK, BLK)),
        in_specs=[SMEM_SPEC, VMEM_SPEC],
        out_specs=(VMEM_SPEC,) * 4,
        scratch_shapes=[pltpu.VMEM((PLANE * TOK, 2 * HEAD_DIM), jnp.bfloat16)] + scratch(CHUNKS),
        compiler_params=params(16),
        cost_estimate=cost(2),
        name="inner",
    )(sel_all, main)
    mine = pl.pallas_call(
        outer_kernel,
        out_shape=(pltpu.HBM((TOK, 256), jnp.bfloat16),) * PLANE,
        in_specs=[SMEM_SPEC] * 2 + [VMEM_SPEC] * 7,
        out_specs=(ANY_SPEC,) * PLANE,
        scratch_shapes=[pltpu.VMEM((PLANE, TOK, 256), jnp.bfloat16), pltpu.SemaphoreType.DMA((PLANE,))] + scratch(REACH),
        compiler_params=params(16),
        cost_estimate=cost(276),
        name="outer",
    )(row, sel_all, main, up, dn, mid, stats, first, second)
    back = [mine[0]] + [lax.ppermute(mine[k], "ctx", [(i, i ^ k) for i in range(devices)]) for k in range(1, PLANE)]
    edge = pl.pallas_call(
        edge_kernel,
        out_shape=bf16(REACH, TOK, KV),
        in_specs=[SMEM_SPEC, VMEM_SPEC] + [ANY_SPEC] * EARLY,
        out_specs=VMEM_SPEC,
        compiler_params=params(4),
        name="edge",
    )(task, rest, *back[1:1 + EARLY])
    halo = spread(edge, lambda i, core: (i + (PLANE if (i ^ (4 * core)) % PLANE < PLANE // 2 else -PLANE)) % devices)

    own, lent = pl.pallas_call(
        pair_kernel,
        out_shape=(bf16(TOK, 256), bf16(TOK, 256)),
        in_specs=[SMEM_SPEC] * 2 + [VMEM_SPEC] * 2 + [ANY_SPEC, HBM_SPEC] + [ANY_SPEC] * GATES,
        out_specs=(VMEM_SPEC,) * 2,
        scratch_shapes=[pltpu.VMEM(((PLANE + 2 * REACH) * TOK, KV), jnp.bfloat16)] + scratch(CHUNKS) + [pltpu.SemaphoreType.DMA((PLANE + REACH,))],
        compiler_params=params(14),
        cost_estimate=cost(14),
        name="pair",
    )(task, sel_all, q_first, q_second, rest, pltpu.with_memory_space_constraint(halo, pltpu.HBM), *back[PLANE - GATES:])
    own, partner = to_first(own), to_second(lent)

    return pl.pallas_call(
        unpack_kernel,
        out_shape=(bf16(TOK, HEADS * HEAD_DIM), bf16(TOK, HEADS * HEAD_DIM)),
        in_specs=[SMEM_SPEC] + [VMEM_SPEC] * (PLANE + 2),
        out_specs=(VMEM_SPEC,) * 2,
        compiler_params=params(6),
        name="unpack",
    )(row, *back, own, partner)


def solution(mesh):
    wide = P("ctx", "head")
    return jax.shard_map(
        body,
        mesh=mesh,
        in_specs=(wide,) * 6 + (P("ctx", None),),
        out_specs=(wide, wide),
        check_vma=False,
    )
```

```python
import jax
import jax.numpy as jnp
from jax import lax
from jax.experimental import pallas as pl
from jax.experimental.pallas import tpu as pltpu
from jax.sharding import PartitionSpec as P

HEADS = 10
HEAD_DIM = 128
BLK = 128
REACH = 3
TOK = 256
WIN = 14
BPD = 2
PLANE = 8
CHUNKS = 2 * REACH + 1
EXTRA = 8
KV = 4 * HEAD_DIM
ALL = 6 * HEAD_DIM
NEG = -1.0e30
LOG2E = 1.4426950408889634
SCALE = HEAD_DIM ** -0.5
FACTOR = SCALE * LOG2E
MIB = 1 << 20

VMEM_SPEC = pl.BlockSpec(memory_space=pltpu.VMEM)
HBM_SPEC = pl.BlockSpec(memory_space=pltpu.HBM)
ANY_SPEC = pl.BlockSpec(memory_space=pl.ANY)
SMEM_SPEC = pl.BlockSpec(memory_space=pltpu.SMEM)


def run_copies(pairs, sem):
    copies = [pltpu.make_async_copy(source, target, sem.at[n]) for n, (source, target) in enumerate(pairs)]
    for copy in copies:
        copy.start()
    for copy in copies:
        copy.wait()


def lanes(n):
    return pl.ds(n * HEAD_DIM, HEAD_DIM)


def cut_plane_kernel(sel, q, qt, k, kt, v, vt, out, buf, sel_buf, sel_sem, in_sem, out_sem):
    arrays = (k, kt, v, vt, qt, q)
    ins = [[pltpu.make_async_copy(ref.at[:, lanes(j)], buf.at[j, 0:TOK, lanes(n)], in_sem.at[j, n])
            for n, ref in enumerate(arrays)] for j in range(PLANE)]
    outs = [pltpu.make_async_copy(buf.at[j], out.at[j], out_sem.at[j]) for j in range(PLANE)]
    for chunk in ins:
        for copy in chunk:
            copy.start()
    run_copies([(sel, sel_buf)], sel_sem)
    listed = sel_buf[...].astype(jnp.float32).astype(jnp.bfloat16)
    for j in range(PLANE):
        buf[j, TOK:TOK + 2, :WIN] = listed
        for copy in ins[j]:
            copy.wait()
        outs[j].start()
    for copy in outs:
        copy.wait()


def cut_pair_kernel(row_ref, q, qt, k, kt, v, vt, rest, q_same, q_opp, buf, in_sem, out_sem):
    arrays = (k, kt, v, vt, qt, q)
    ins = [pltpu.make_async_copy(ref.at[:, lanes(PLANE + h)], buf.at[h, :, lanes(n)], in_sem.at[h, n])
           for h in range(2) for n, ref in enumerate(arrays)]
    outs = [pltpu.make_async_copy(buf.at[j % 2, :, 0:KV], rest.at[j], out_sem.at[j]) for j in range(PLANE)]
    for copy in ins:
        copy.start()
    for copy in ins:
        copy.wait()
    for copy in outs:
        copy.start()
    par = row_ref[0] % 2
    q_same[...] = buf[par, :, KV:]
    q_opp[...] = buf[1 - par, :, KV:]
    for copy in outs:
        copy.wait()


def weigh(sel_ref, row, first, count, chunk, qcat, floor, s_scr, p_scr, t_scr):
    dims = (((1,), (1,)), ((), ()))
    query = qcat[:, HEAD_DIM:]
    peak = [None, None]
    for u in range(count):
        s = lax.dot_general(query, chunk(u)[:, :HEAD_DIM], dims, preferred_element_type=jnp.float32)
        for qb in range(2):
            for kb in range(2):
                listed = sel_ref[row, qb * WIN + 2 * (first + u) + kb]
                piece = s[qb * BLK:(qb + 1) * BLK, kb * BLK:(kb + 1) * BLK] + jnp.where(listed != 0, 0.0, NEG)
                s_scr[qb * BLK:(qb + 1) * BLK, u * TOK + kb * BLK:u * TOK + (kb + 1) * BLK] = piece
                peak[qb] = piece if peak[qb] is None else jnp.maximum(peak[qb], piece)
    top = jnp.concatenate([jnp.max(p, axis=1, keepdims=True) for p in peak], axis=0) * FACTOR
    if floor is not None:
        top = jnp.maximum(top, floor)
    total = jnp.zeros((TOK, BLK), jnp.float32)
    tangent_total = jnp.zeros((TOK, BLK), jnp.float32)
    for u in range(count):
        st = lax.dot_general(qcat, chunk(u), dims, preferred_element_type=jnp.float32)
        weights = jnp.exp2(s_scr[:, u * TOK:(u + 1) * TOK] * FACTOR - top)
        weighted = weights * st
        total += weights[:, :BLK] + weights[:, BLK:]
        tangent_total += weighted[:, :BLK] + weighted[:, BLK:]
        p_scr[:, u * TOK:(u + 1) * TOK] = weights.astype(jnp.bfloat16)
        t_scr[:, u * TOK:(u + 1) * TOK] = weighted.astype(jnp.bfloat16)
    return top, total, tangent_total


def finish(total, tangent_total, first, second):
    inverse = 1.0 / jnp.sum(total, axis=1, keepdims=True)
    out = first[:, :HEAD_DIM] * inverse
    tangent_sum = jnp.sum(tangent_total, axis=1, keepdims=True)
    tangent = ((second - out * tangent_sum) * SCALE + first[:, HEAD_DIM:]) * inverse
    return jnp.concatenate([out.astype(jnp.bfloat16), tangent.astype(jnp.bfloat16)], axis=1)


def mix(p_scr, t_scr, width, values):
    first = jnp.dot(p_scr[:, :width], values, preferred_element_type=jnp.float32)
    second = jnp.dot(t_scr[:, :width], values[:, :HEAD_DIM], preferred_element_type=jnp.float32)
    return first, second


def inner_kernel(sel_ref, main, o_ref, stats, first_ref, second_ref, vv, s_scr, p_scr, t_scr):
    for c in range(PLANE):
        vv[c * TOK:(c + 1) * TOK, :] = main[c, :TOK, 2 * HEAD_DIM:KV]

    def position(i, count, final):
        begin = jnp.maximum(i - REACH, 0)
        base = pl.multiple_of(begin * TOK, TOK)
        top, total, tangent_total = weigh(
            sel_ref, i, jnp.maximum(REACH - i, 0), count, lambda u: main[begin + u, :TOK, :2 * HEAD_DIM],
            main[i, :TOK, KV:], None, s_scr, p_scr, t_scr)
        first, second = mix(p_scr, t_scr, count * TOK, vv[pl.ds(base, count * TOK), :])
        if final:
            o_ref[i - REACH] = finish(total, tangent_total, first, second)
        else:
            stats[i, 0] = jnp.broadcast_to(top, (TOK, BLK))
            stats[i, 1] = total
            stats[i, 2] = tangent_total
            first_ref[i] = first
            second_ref[i] = second

    def step(n, carry):
        for low in range(REACH + 1):
            position(low + n * (PLANE - 1 - 2 * low), low + REACH + 1, low == REACH)
        return carry

    lax.fori_loop(0, 2, step, 0)


def outer_kernel(sel_ref, main, up, dn, mid, stats, first_ref, second_ref, o_ref, done, buf, sem, s_scr, p_scr, t_scr):
    done[...] = jnp.zeros_like(done)
    copies = []

    def leave(i, value):
        buf[i] = value
        copies.append(pltpu.make_async_copy(buf.at[i], o_ref.at[i], sem.at[i]))
        copies[-1].start()

    for i in (3, 4):
        leave(i, mid[i - REACH])
    for i in (0, 1, 2, 5, 6, 7):
        low = i < REACH
        halo, skip, at = (up, i, 0) if low else (dn, 0, PLANE + REACH - i)
        count = REACH - i if low else i - REACH - 1
        before = stats[i, 0][:, :1]
        top, total, tangent_total = weigh(
            sel_ref, i, at, count, lambda u: halo[skip + u, :, :2 * HEAD_DIM], main[i, :TOK, KV:], before,
            s_scr, p_scr, t_scr)
        shrink = jnp.exp2(before - top)
        first, second = first_ref[i] * shrink, second_ref[i] * shrink
        for u in range(count):
            more = mix(p_scr.at[:, u * TOK:(u + 1) * TOK], t_scr.at[:, u * TOK:(u + 1) * TOK], TOK,
                       halo[skip + u, :, 2 * HEAD_DIM:])
            first, second = first + more[0], second + more[1]
        leave(i, finish(stats[i, 1] * shrink + total, stats[i, 2] * shrink + tangent_total, first, second))
    for copy in copies:
        copy.wait()


def edges_kernel(main, gate_a, gate_b, up, dn, sem):
    del gate_a, gate_b
    run_copies([(main.at[first + n, 0:TOK, 0:KV], to.at[n]) for first, to in ((PLANE - REACH, up), (0, dn))
                for n in range(REACH)], sem)


def edge_kernel(task_ref, main, gate, edge, sem):
    del gate
    begin = jnp.where(task_ref[0] < PLANE // 2, PLANE - REACH, 0)
    run_copies([(main.at[begin + n], edge.at[n]) for n in range(REACH)], sem)


def pair_kernel(task_ref, sel_ref, q_first, q_second, main, halo, o_first, o_second, kv, s_scr, p_scr, t_scr, sem):
    task = task_ref[0]
    begin = jnp.where(task < PLANE // 2, 0, REACH + PLANE)
    pairs = [(main.at[c], kv.at[pl.ds((c + REACH) * TOK, TOK), :]) for c in range(PLANE)]
    pairs += [(halo.at[n], kv.at[pl.ds(pl.multiple_of((begin + n) * TOK, TOK), TOK), :]) for n in range(REACH)]
    run_copies(pairs, sem)
    for ref, at, o_ref in ((q_first, task, o_first), (q_second, task + 1 - 2 * (task % 2), o_second)):
        base = pl.multiple_of(at * TOK, TOK)
        _, total, tangent_total = weigh(
            sel_ref, at, 0, CHUNKS, lambda u: kv[pl.ds(base + u * TOK, TOK), :2 * HEAD_DIM], ref[...], None,
            s_scr, p_scr, t_scr)
        first, second = mix(p_scr, t_scr, CHUNKS * TOK, kv[pl.ds(base, CHUNKS * TOK), 2 * HEAD_DIM:])
        o_ref[...] = finish(total, tangent_total, first, second)


def after_kernel(*refs):
    del refs


def after(array, *others):
    return pl.pallas_call(
        after_kernel,
        out_shape=pltpu.HBM(array.shape, array.dtype),
        in_specs=[HBM_SPEC] + [ANY_SPEC] * len(others),
        out_specs=HBM_SPEC,
        input_output_aliases={0: 0},
        compiler_params=params(1),
        name="after",
    )(pltpu.with_memory_space_constraint(array, pltpu.HBM), *others)


def unpack_kernel(par_ref, mine, own, other, o_ref, t_ref):
    par = par_ref[0] % 2
    for j in range(PLANE):
        cols = pl.ds(j * HEAD_DIM, HEAD_DIM)
        o_ref[:, cols] = mine[j, :, :HEAD_DIM]
        t_ref[:, cols] = mine[j, :, HEAD_DIM:]
    for which, piece in ((par, own), (1 - par, other)):
        cols = pl.ds(pl.multiple_of((PLANE + which) * HEAD_DIM, HEAD_DIM), HEAD_DIM)
        o_ref[:, cols] = piece[:, :HEAD_DIM]
        t_ref[:, cols] = piece[:, HEAD_DIM:]


def bf16(*shape):
    return jax.ShapeDtypeStruct(shape, jnp.bfloat16)


def f32(*shape):
    return jax.ShapeDtypeStruct(shape, jnp.float32)


def scratch(chunks):
    return [
        pltpu.VMEM((TOK, chunks * TOK), jnp.float32),
        pltpu.VMEM((TOK, chunks * TOK), jnp.bfloat16),
        pltpu.VMEM((TOK, chunks * TOK), jnp.bfloat16),
    ]


def cost(chunks):
    products = chunks * TOK * TOK
    return pl.CostEstimate(flops=10 * HEAD_DIM * products, bytes_accessed=chunks * 2 * TOK * 4 * HEAD_DIM,
                           transcendentals=products)


def params(mib):
    return pltpu.CompilerParams(vmem_limit_bytes=mib * MIB)


def body(queries, query_tangents, keys, key_tangents, values, value_tangents, selection):
    devices = lax.axis_size("ctx")
    columns = lax.axis_size("head")
    row = (lax.axis_index("ctx") % PLANE).astype(jnp.int32)[None]
    task = row ^ (4 * (lax.axis_index("head") % 2).astype(jnp.int32))
    planes = [[z * PLANE + i for i in range(PLANE)] for z in range(devices // PLANE)]

    def send(array, by):
        return lax.ppermute(array, "ctx", [(i, (i + by) % devices) for i in range(devices)])

    def spread(array, target):
        pairs = [(i * columns + h, target(i, h % 2) * columns + h) for i in range(devices) for h in range(columns)]
        return lax.ppermute(array, ("ctx", "head"), pairs)

    def to_first(array):
        return spread(array, lambda i, core: i ^ (4 * core))

    def to_second(array):
        return spread(array, lambda i, core: i ^ (4 * core) ^ 1)

    def exchange(array):
        return lax.all_to_all(array, "ctx", 0, 0, axis_index_groups=planes, tiled=True)

    wide = [pltpu.with_memory_space_constraint(array, pltpu.HBM) for array in
            (queries, query_tangents, keys, key_tangents, values, value_tangents)]
    plane_out = pl.pallas_call(
        cut_plane_kernel,
        out_shape=pltpu.HBM((PLANE, TOK + EXTRA, ALL), jnp.bfloat16),
        in_specs=[HBM_SPEC] * 7,
        out_specs=ANY_SPEC,
        scratch_shapes=[pltpu.VMEM((PLANE, TOK + EXTRA, ALL), jnp.bfloat16),
                        pltpu.VMEM((BPD, WIN), jnp.int32), pltpu.SemaphoreType.DMA((1,)),
                        pltpu.SemaphoreType.DMA((PLANE, 6)), pltpu.SemaphoreType.DMA((PLANE,))],
        compiler_params=params(8),
        name="cut_plane",
    )(pltpu.with_memory_space_constraint(selection, pltpu.HBM), *wide)
    rest_out, q_same, q_opp = pl.pallas_call(
        cut_pair_kernel,
        out_shape=(pltpu.HBM((PLANE, TOK, KV), jnp.bfloat16), bf16(TOK, 256), bf16(TOK, 256)),
        in_specs=[SMEM_SPEC] + [HBM_SPEC] * 6,
        out_specs=(ANY_SPEC,) + (VMEM_SPEC,) * 2,
        scratch_shapes=[pltpu.VMEM((2, TOK, ALL), jnp.bfloat16),
                        pltpu.SemaphoreType.DMA((2, 6)), pltpu.SemaphoreType.DMA((PLANE,))],
        compiler_params=params(8),
        name="cut_pair",
    )(row, *wide)

    q_first, q_second = to_first(q_same), to_second(q_opp)

    main = exchange(plane_out)
    sel_all = main[:, TOK:TOK + 2, :WIN].astype(jnp.int32).reshape(PLANE, 2 * WIN)
    edge_up, edge_dn = pl.pallas_call(
        edges_kernel,
        out_shape=(pltpu.HBM((REACH, TOK, KV), jnp.bfloat16),) * 2,
        in_specs=[ANY_SPEC] * 3,
        out_specs=(ANY_SPEC,) * 2,
        scratch_shapes=[pltpu.SemaphoreType.DMA((2 * REACH,))],
        compiler_params=params(1),
        name="edges",
    )(main, q_first, q_second)
    up, dn = send(edge_up, PLANE), send(edge_dn, -PLANE)
    rest = exchange(after(rest_out, sel_all, edge_up))

    mid, stats, first, second = pl.pallas_call(
        inner_kernel,
        out_shape=(bf16(2, TOK, 256), f32(PLANE, 3, TOK, BLK), f32(PLANE, TOK, 256), f32(PLANE, TOK, BLK)),
        in_specs=[SMEM_SPEC, VMEM_SPEC],
        out_specs=(VMEM_SPEC,) * 4,
        scratch_shapes=[pltpu.VMEM((PLANE * TOK, 2 * HEAD_DIM), jnp.bfloat16)] + scratch(CHUNKS),
        compiler_params=params(16),
        cost_estimate=cost(44),
        name="inner",
    )(sel_all, main)
    mine, done = pl.pallas_call(
        outer_kernel,
        out_shape=(pltpu.HBM((PLANE, TOK, 256), jnp.bfloat16), f32(8, BLK)),
        in_specs=[SMEM_SPEC] + [VMEM_SPEC] * 7,
        out_specs=(ANY_SPEC, VMEM_SPEC),
        scratch_shapes=[pltpu.VMEM((PLANE, TOK, 256), jnp.bfloat16), pltpu.SemaphoreType.DMA((PLANE,))] + scratch(REACH),
        compiler_params=params(16),
        cost_estimate=cost(12),
        name="outer",
    )(sel_all, main, up, dn, mid, stats, first, second)
    edge = pl.pallas_call(
        edge_kernel,
        out_shape=bf16(REACH, TOK, KV),
        in_specs=[SMEM_SPEC, ANY_SPEC, ANY_SPEC],
        out_specs=ANY_SPEC,
        scratch_shapes=[pltpu.SemaphoreType.DMA((REACH,))],
        compiler_params=params(1),
        name="edge",
    )(task, rest, done)
    halo = spread(edge, lambda i, core: (i + (PLANE if (i ^ (4 * core)) % PLANE < PLANE // 2 else -PLANE)) % devices)
    back = exchange(after(mine, edge))

    own, lent = pl.pallas_call(
        pair_kernel,
        out_shape=(bf16(TOK, 256), bf16(TOK, 256)),
        in_specs=[SMEM_SPEC] * 2 + [VMEM_SPEC] * 2 + [ANY_SPEC, HBM_SPEC],
        out_specs=(VMEM_SPEC,) * 2,
        scratch_shapes=[pltpu.VMEM(((PLANE + 2 * REACH) * TOK, KV), jnp.bfloat16)] + scratch(CHUNKS) + [pltpu.SemaphoreType.DMA((PLANE + REACH,))],
        compiler_params=params(14),
        cost_estimate=cost(14),
        name="pair",
    )(task, sel_all, q_first, q_second, rest, pltpu.with_memory_space_constraint(halo, pltpu.HBM))
    own, partner = to_first(own), to_second(lent)

    return pl.pallas_call(
        unpack_kernel,
        out_shape=(bf16(TOK, HEADS * HEAD_DIM), bf16(TOK, HEADS * HEAD_DIM)),
        in_specs=[SMEM_SPEC] + [VMEM_SPEC] * 3,
        out_specs=(VMEM_SPEC,) * 2,
        compiler_params=params(6),
        name="unpack",
    )(row, back, own, partner)


def solution(mesh):
    wide = P("ctx", "head")
    return jax.shard_map(
        body,
        mesh=mesh,
        in_specs=(wide,) * 6 + (P("ctx", None),),
        out_specs=(wide, wide),
        check_vma=False,
    )
```

```python
import jax
import jax.numpy as jnp
from jax import lax
from jax.experimental import pallas as pl
from jax.experimental.pallas import tpu as pltpu
from jax.sharding import PartitionSpec as P

HEADS = 10
HEAD_DIM = 128
BLK = 128
REACH = 3
TOK = 256
WIN = 14
BPD = 2
PLANE = 8
CHUNKS = 2 * REACH + 1
EXTRA = 8
KV = 4 * HEAD_DIM
ALL = 6 * HEAD_DIM
NEG = -1.0e30
LOG2E = 1.4426950408889634
SCALE = HEAD_DIM ** -0.5
FACTOR = SCALE * LOG2E
MIB = 1 << 20

VMEM_SPEC = pl.BlockSpec(memory_space=pltpu.VMEM)
HBM_SPEC = pl.BlockSpec(memory_space=pltpu.HBM)
ANY_SPEC = pl.BlockSpec(memory_space=pl.ANY)
SMEM_SPEC = pl.BlockSpec(memory_space=pltpu.SMEM)


def run_copies(pairs, sem):
    copies = [pltpu.make_async_copy(source, target, sem.at[n]) for n, (source, target) in enumerate(pairs)]
    for copy in copies:
        copy.start()
    for copy in copies:
        copy.wait()


def lanes(n):
    return pl.ds(n * HEAD_DIM, HEAD_DIM)


def cut_plane_kernel(sel, q, qt, k, kt, v, vt, out, buf, sel_buf, sel_sem, in_sem, out_sem):
    arrays = (k, kt, v, vt, qt, q)
    ins = [[pltpu.make_async_copy(ref.at[:, lanes(j)], buf.at[j, 0:TOK, lanes(n)], in_sem.at[j, n])
            for n, ref in enumerate(arrays)] for j in range(PLANE)]
    outs = [pltpu.make_async_copy(buf.at[j], out.at[j], out_sem.at[j]) for j in range(PLANE)]
    listing = pltpu.make_async_copy(sel, sel_buf, sel_sem.at[0])
    listing.start()
    for chunk in ins:
        for copy in chunk:
            copy.start()
    listing.wait()
    listed = sel_buf[...].astype(jnp.float32).astype(jnp.bfloat16)
    for j in range(PLANE):
        buf[j, TOK:TOK + 2, :WIN] = listed
        for copy in ins[j]:
            copy.wait()
        outs[j].start()
    for copy in outs:
        copy.wait()


def cut_pair_kernel(row_ref, q, qt, k, kt, v, vt, rest, q_same, q_opp, buf, in_sem, out_sem):
    arrays = (k, kt, v, vt, qt, q)
    ins = [pltpu.make_async_copy(ref.at[:, lanes(PLANE + h)], buf.at[h, :, lanes(n)], in_sem.at[h, n])
           for h in range(2) for n, ref in enumerate(arrays)]
    outs = [pltpu.make_async_copy(buf.at[j % 2, :, 0:KV], rest.at[j], out_sem.at[j]) for j in range(PLANE)]
    for copy in ins:
        copy.start()
    for copy in ins:
        copy.wait()
    for copy in outs:
        copy.start()
    par = row_ref[0] % 2
    q_same[...] = buf[par, :, KV:]
    q_opp[...] = buf[1 - par, :, KV:]
    for copy in outs:
        copy.wait()


def weigh(sel_ref, row, first, count, chunk, qcat, floor, s_scr, p_scr, t_scr, inside=None):
    dims = (((1,), (1,)), ((), ()))
    query = qcat[:, HEAD_DIM:]
    peak = [None, None]
    for u in range(count):
        s = lax.dot_general(query, chunk(u)[:, :HEAD_DIM], dims, preferred_element_type=jnp.float32)
        for qb in range(2):
            for kb in range(2):
                at = first + u if inside is None else jnp.clip(first + u, 0, CHUNKS - 1)
                listed = sel_ref[row, qb * WIN + 2 * at + kb]
                if inside is not None:
                    listed = jnp.where(inside(first + u), listed, 0)
                piece = s[qb * BLK:(qb + 1) * BLK, kb * BLK:(kb + 1) * BLK] + jnp.where(listed != 0, 0.0, NEG)
                s_scr[qb * BLK:(qb + 1) * BLK, u * TOK + kb * BLK:u * TOK + (kb + 1) * BLK] = piece
                peak[qb] = piece if peak[qb] is None else jnp.maximum(peak[qb], piece)
    top = jnp.concatenate([jnp.max(p, axis=1, keepdims=True) for p in peak], axis=0) * FACTOR
    if floor is not None:
        top = jnp.maximum(top, floor)
    total = jnp.zeros((TOK, BLK), jnp.float32)
    tangent_total = jnp.zeros((TOK, BLK), jnp.float32)
    for u in range(count):
        st = lax.dot_general(qcat, chunk(u), dims, preferred_element_type=jnp.float32)
        weights = jnp.exp2(s_scr[:, u * TOK:(u + 1) * TOK] * FACTOR - top)
        weighted = weights * st
        total += weights[:, :BLK] + weights[:, BLK:]
        tangent_total += weighted[:, :BLK] + weighted[:, BLK:]
        p_scr[:, u * TOK:(u + 1) * TOK] = weights.astype(jnp.bfloat16)
        t_scr[:, u * TOK:(u + 1) * TOK] = weighted.astype(jnp.bfloat16)
    return top, total, tangent_total


def finish(total, tangent_total, first, second):
    inverse = 1.0 / jnp.sum(total, axis=1, keepdims=True)
    out = first[:, :HEAD_DIM] * inverse
    tangent_sum = jnp.sum(tangent_total, axis=1, keepdims=True)
    tangent = ((second - out * tangent_sum) * SCALE + first[:, HEAD_DIM:]) * inverse
    return jnp.concatenate([out.astype(jnp.bfloat16), tangent.astype(jnp.bfloat16)], axis=1)


def mix(p_scr, t_scr, width, values):
    first = jnp.dot(p_scr[:, :width], values, preferred_element_type=jnp.float32)
    second = jnp.dot(t_scr[:, :width], values[:, :HEAD_DIM], preferred_element_type=jnp.float32)
    return first, second


def inner_kernel(sel_ref, main, o_ref, stats, first_ref, second_ref, vv, s_scr, p_scr, t_scr):
    for c in range(PLANE):
        vv[c * TOK:(c + 1) * TOK, :] = main[c, :TOK, 2 * HEAD_DIM:KV]

    def position(i, count, final):
        begin = jnp.maximum(i - REACH, 0)
        base = pl.multiple_of(begin * TOK, TOK)
        top, total, tangent_total = weigh(
            sel_ref, i, jnp.maximum(REACH - i, 0), count, lambda u: main[begin + u, :TOK, :2 * HEAD_DIM],
            main[i, :TOK, KV:], None, s_scr, p_scr, t_scr)
        first, second = mix(p_scr, t_scr, count * TOK, vv[pl.ds(base, count * TOK), :])
        if final:
            o_ref[i - REACH] = finish(total, tangent_total, first, second)
        else:
            stats[i, 0] = jnp.broadcast_to(top, (TOK, BLK))
            stats[i, 1] = total
            stats[i, 2] = tangent_total
            first_ref[i] = first
            second_ref[i] = second

    def step(n, carry):
        for low in range(REACH + 1):
            position(low + n * (PLANE - 1 - 2 * low), low + REACH + 1, low == REACH)
        return carry

    lax.fori_loop(0, 2, step, 0)


def outer_kernel(sel_ref, main, up, dn, mid, stats, first_ref, second_ref, o_ref, done, buf, sem, s_scr, p_scr, t_scr):
    done[...] = jnp.zeros_like(done)
    copies = []

    def leave(i, value):
        buf[i] = value
        copies.append(pltpu.make_async_copy(buf.at[i], o_ref.at[i], sem.at[i]))
        copies[-1].start()

    for i in (3, 4):
        leave(i, mid[i - REACH])
    for i in (0, 1, 2, 5, 6, 7):
        low = i < REACH
        halo, skip, at = (up, i, 0) if low else (dn, 0, PLANE + REACH - i)
        count = REACH - i if low else i - REACH - 1
        before = stats[i, 0][:, :1]
        top, total, tangent_total = weigh(
            sel_ref, i, at, count, lambda u: halo[skip + u, :, :2 * HEAD_DIM], main[i, :TOK, KV:], before,
            s_scr, p_scr, t_scr)
        shrink = jnp.exp2(before - top)
        first, second = first_ref[i] * shrink, second_ref[i] * shrink
        for u in range(count):
            more = mix(p_scr.at[:, u * TOK:(u + 1) * TOK], t_scr.at[:, u * TOK:(u + 1) * TOK], TOK,
                       halo[skip + u, :, 2 * HEAD_DIM:])
            first, second = first + more[0], second + more[1]
        leave(i, finish(stats[i, 1] * shrink + total, stats[i, 2] * shrink + tangent_total, first, second))
    for copy in copies:
        copy.wait()


def edges_kernel(main, gate_a, gate_b, up, dn, sem):
    del gate_a, gate_b
    run_copies([(main.at[first + n, 0:TOK, 0:KV], to.at[n]) for first, to in ((PLANE - REACH, up), (0, dn))
                for n in range(REACH)], sem)


def edge_kernel(task_ref, main, gate, edge, sem):
    del gate
    begin = jnp.where(task_ref[0] < PLANE // 2, PLANE - REACH, 0)
    run_copies([(main.at[begin + n], edge.at[n]) for n in range(REACH)], sem)


def pair_tasks(task_ref, q_first, q_second):
    task = task_ref[0]
    return ((q_first, task), (q_second, task + 1 - 2 * (task % 2)))


def pair_inner_kernel(task_ref, sel_ref, q_first, q_second, main, gate, stats, first_ref, second_ref,
                      kv, s_scr, p_scr, t_scr, sem):
    del gate
    copies = [pltpu.make_async_copy(main.at[c], kv.at[pl.ds((c + REACH) * TOK, TOK), :], sem.at[c]) for c in range(PLANE)]
    for copy in copies:
        copy.start()
    for begin in (0, REACH + PLANE):
        kv[begin * TOK:(begin + REACH) * TOK, :] = jnp.zeros((REACH * TOK, KV), jnp.bfloat16)
    for copy in copies:
        copy.wait()
    for n, (ref, at) in enumerate(pair_tasks(task_ref, q_first, q_second)):
        base = pl.multiple_of(at * TOK, TOK)
        top, total, tangent_total = weigh(
            sel_ref, at, 0, CHUNKS, lambda u: kv[pl.ds(base + u * TOK, TOK), :2 * HEAD_DIM], ref[...], None,
            s_scr, p_scr, t_scr, lambda t: jnp.logical_and(at + t >= REACH, at + t < REACH + PLANE))
        first, second = mix(p_scr, t_scr, CHUNKS * TOK, kv[pl.ds(base, CHUNKS * TOK), 2 * HEAD_DIM:])
        stats[n, 0] = jnp.broadcast_to(top, (TOK, BLK))
        stats[n, 1] = total
        stats[n, 2] = tangent_total
        first_ref[n] = first
        second_ref[n] = second


def pair_outer_kernel(task_ref, sel_ref, q_first, q_second, halo, stats, first_ref, second_ref, o_first, o_second,
                      s_scr, p_scr, t_scr):
    begin = jnp.where(task_ref[0] < PLANE // 2, 0, REACH + PLANE)
    outs = (o_first, o_second)
    for n, (ref, at) in enumerate(pair_tasks(task_ref, q_first, q_second)):
        before = stats[n, 0][:, :1]
        top, total, tangent_total = weigh(
            sel_ref, at, begin - at, REACH, lambda u: halo[u, :, :2 * HEAD_DIM], ref[...], before,
            s_scr, p_scr, t_scr, lambda t: jnp.logical_and(t >= 0, t < CHUNKS))
        shrink = jnp.exp2(before - top)
        first, second = first_ref[n] * shrink, second_ref[n] * shrink
        for u in range(REACH):
            more = mix(p_scr.at[:, u * TOK:(u + 1) * TOK], t_scr.at[:, u * TOK:(u + 1) * TOK], TOK,
                       halo[u, :, 2 * HEAD_DIM:])
            first, second = first + more[0], second + more[1]
        outs[n][...] = finish(stats[n, 1] * shrink + total, stats[n, 2] * shrink + tangent_total, first, second)


def after_kernel(*refs):
    del refs


def after(array, *others):
    return pl.pallas_call(
        after_kernel,
        out_shape=pltpu.HBM(array.shape, array.dtype),
        in_specs=[HBM_SPEC] + [ANY_SPEC] * len(others),
        out_specs=HBM_SPEC,
        input_output_aliases={0: 0},
        compiler_params=params(1),
        name="after",
    )(pltpu.with_memory_space_constraint(array, pltpu.HBM), *others)


def unpack_kernel(par_ref, mine, own, other, o_ref, t_ref):
    par = par_ref[0] % 2
    for j in range(PLANE):
        cols = pl.ds(j * HEAD_DIM, HEAD_DIM)
        o_ref[:, cols] = mine[j, :, :HEAD_DIM]
        t_ref[:, cols] = mine[j, :, HEAD_DIM:]
    for which, piece in ((par, own), (1 - par, other)):
        cols = pl.ds(pl.multiple_of((PLANE + which) * HEAD_DIM, HEAD_DIM), HEAD_DIM)
        o_ref[:, cols] = piece[:, :HEAD_DIM]
        t_ref[:, cols] = piece[:, HEAD_DIM:]


def bf16(*shape):
    return jax.ShapeDtypeStruct(shape, jnp.bfloat16)


def f32(*shape):
    return jax.ShapeDtypeStruct(shape, jnp.float32)


def scratch(chunks):
    return [
        pltpu.VMEM((TOK, chunks * TOK), jnp.float32),
        pltpu.VMEM((TOK, chunks * TOK), jnp.bfloat16),
        pltpu.VMEM((TOK, chunks * TOK), jnp.bfloat16),
    ]


def cost(chunks):
    products = chunks * TOK * TOK
    return pl.CostEstimate(flops=10 * HEAD_DIM * products, bytes_accessed=chunks * 2 * TOK * 4 * HEAD_DIM,
                           transcendentals=products)


def params(mib):
    return pltpu.CompilerParams(vmem_limit_bytes=mib * MIB)


def body(queries, query_tangents, keys, key_tangents, values, value_tangents, selection):
    devices = lax.axis_size("ctx")
    columns = lax.axis_size("head")
    row = (lax.axis_index("ctx") % PLANE).astype(jnp.int32)[None]
    task = row ^ (4 * (lax.axis_index("head") % 2).astype(jnp.int32))
    planes = [[z * PLANE + i for i in range(PLANE)] for z in range(devices // PLANE)]

    def send(array, by):
        return lax.ppermute(array, "ctx", [(i, (i + by) % devices) for i in range(devices)])

    def spread(array, target):
        pairs = [(i * columns + h, target(i, h % 2) * columns + h) for i in range(devices) for h in range(columns)]
        return lax.ppermute(array, ("ctx", "head"), pairs)

    def to_first(array):
        return spread(array, lambda i, core: i ^ (4 * core))

    def to_second(array):
        return spread(array, lambda i, core: i ^ (4 * core) ^ 1)

    def exchange(array):
        return lax.all_to_all(array, "ctx", 0, 0, axis_index_groups=planes, tiled=True)

    wide = [pltpu.with_memory_space_constraint(array, pltpu.HBM) for array in
            (queries, query_tangents, keys, key_tangents, values, value_tangents)]
    plane_out = pl.pallas_call(
        cut_plane_kernel,
        out_shape=pltpu.HBM((PLANE, TOK + EXTRA, ALL), jnp.bfloat16),
        in_specs=[HBM_SPEC] * 7,
        out_specs=ANY_SPEC,
        scratch_shapes=[pltpu.VMEM((PLANE, TOK + EXTRA, ALL), jnp.bfloat16),
                        pltpu.VMEM((BPD, WIN), jnp.int32), pltpu.SemaphoreType.DMA((1,)),
                        pltpu.SemaphoreType.DMA((PLANE, 6)), pltpu.SemaphoreType.DMA((PLANE,))],
        compiler_params=params(8),
        name="cut_plane",
    )(pltpu.with_memory_space_constraint(selection, pltpu.HBM), *wide)
    rest_out, q_same, q_opp = pl.pallas_call(
        cut_pair_kernel,
        out_shape=(pltpu.HBM((PLANE, TOK, KV), jnp.bfloat16), bf16(TOK, 256), bf16(TOK, 256)),
        in_specs=[SMEM_SPEC] + [HBM_SPEC] * 6,
        out_specs=(ANY_SPEC,) + (VMEM_SPEC,) * 2,
        scratch_shapes=[pltpu.VMEM((2, TOK, ALL), jnp.bfloat16),
                        pltpu.SemaphoreType.DMA((2, 6)), pltpu.SemaphoreType.DMA((PLANE,))],
        compiler_params=params(8),
        name="cut_pair",
    )(row, *wide)

    q_first, q_second = to_first(q_same), to_second(q_opp)

    main = exchange(plane_out)
    sel_all = main[:, TOK:TOK + 2, :WIN].astype(jnp.int32).reshape(PLANE, 2 * WIN)
    edge_up, edge_dn = pl.pallas_call(
        edges_kernel,
        out_shape=(pltpu.HBM((REACH, TOK, KV), jnp.bfloat16),) * 2,
        in_specs=[ANY_SPEC] * 3,
        out_specs=(ANY_SPEC,) * 2,
        scratch_shapes=[pltpu.SemaphoreType.DMA((2 * REACH,))],
        compiler_params=params(1),
        name="edges",
    )(main, q_first, q_second)
    up, dn = send(edge_up, PLANE), send(edge_dn, -PLANE)
    rest = exchange(after(rest_out, sel_all, q_first, q_second))

    mid, stats, first, second = pl.pallas_call(
        inner_kernel,
        out_shape=(bf16(2, TOK, 256), f32(PLANE, 3, TOK, BLK), f32(PLANE, TOK, 256), f32(PLANE, TOK, BLK)),
        in_specs=[SMEM_SPEC, VMEM_SPEC],
        out_specs=(VMEM_SPEC,) * 4,
        scratch_shapes=[pltpu.VMEM((PLANE * TOK, 2 * HEAD_DIM), jnp.bfloat16)] + scratch(CHUNKS),
        compiler_params=params(16),
        cost_estimate=cost(44),
        name="inner",
    )(sel_all, main)
    mine, done = pl.pallas_call(
        outer_kernel,
        out_shape=(pltpu.HBM((PLANE, TOK, 256), jnp.bfloat16), f32(8, BLK)),
        in_specs=[SMEM_SPEC] + [VMEM_SPEC] * 7,
        out_specs=(ANY_SPEC, VMEM_SPEC),
        scratch_shapes=[pltpu.VMEM((PLANE, TOK, 256), jnp.bfloat16), pltpu.SemaphoreType.DMA((PLANE,))] + scratch(REACH),
        compiler_params=params(16),
        cost_estimate=cost(12),
        name="outer",
    )(sel_all, main, up, dn, mid, stats, first, second)
    edge = pl.pallas_call(
        edge_kernel,
        out_shape=bf16(REACH, TOK, KV),
        in_specs=[SMEM_SPEC, ANY_SPEC, ANY_SPEC],
        out_specs=ANY_SPEC,
        scratch_shapes=[pltpu.SemaphoreType.DMA((REACH,))],
        compiler_params=params(1),
        name="edge",
    )(task, rest, done)
    halo = spread(edge, lambda i, core: (i + (PLANE if (i ^ (4 * core)) % PLANE < PLANE // 2 else -PLANE)) % devices)
    back = exchange(after(mine, edge))

    pair_sums = pl.pallas_call(
        pair_inner_kernel,
        out_shape=(f32(2, 3, TOK, BLK), f32(2, TOK, 256), f32(2, TOK, BLK)),
        in_specs=[SMEM_SPEC] * 2 + [VMEM_SPEC] * 2 + [ANY_SPEC] * 2,
        out_specs=(VMEM_SPEC,) * 3,
        scratch_shapes=[pltpu.VMEM(((PLANE + 2 * REACH) * TOK, KV), jnp.bfloat16)] + scratch(CHUNKS)
        + [pltpu.SemaphoreType.DMA((PLANE,))],
        compiler_params=params(16),
        cost_estimate=cost(14),
        name="pair_inner",
    )(task, sel_all, q_first, q_second, rest, edge)
    own, lent = pl.pallas_call(
        pair_outer_kernel,
        out_shape=(bf16(TOK, 256), bf16(TOK, 256)),
        in_specs=[SMEM_SPEC] * 2 + [VMEM_SPEC] * 6,
        out_specs=(VMEM_SPEC,) * 2,
        scratch_shapes=scratch(REACH),
        compiler_params=params(8),
        cost_estimate=cost(6),
        name="pair_outer",
    )(task, sel_all, q_first, q_second, halo, *pair_sums)
    own, partner = to_first(own), to_second(lent)

    return pl.pallas_call(
        unpack_kernel,
        out_shape=(bf16(TOK, HEADS * HEAD_DIM), bf16(TOK, HEADS * HEAD_DIM)),
        in_specs=[SMEM_SPEC] + [VMEM_SPEC] * 3,
        out_specs=(VMEM_SPEC,) * 2,
        compiler_params=params(6),
        name="unpack",
    )(row, back, own, partner)


def solution(mesh):
    wide = P("ctx", "head")
    return jax.shard_map(
        body,
        mesh=mesh,
        in_specs=(wide,) * 6 + (P("ctx", None),),
        out_specs=(wide, wide),
        check_vma=False,
    )
```

```python
import jax
import jax.numpy as jnp
from jax import lax
from jax.experimental import pallas as pl
from jax.experimental.pallas import tpu as pltpu
from jax.sharding import PartitionSpec as P

HEADS = 10
HEAD_DIM = 128
BLK = 128
REACH = 3
TOK = 256
WIN = 14
BPD = 2
PLANE = 8
CHUNKS = 2 * REACH + 1
EXTRA = 8
KV = 4 * HEAD_DIM
ALL = 6 * HEAD_DIM
AHEAD = 4
NEG = -1.0e30
LOG2E = 1.4426950408889634
SCALE = HEAD_DIM ** -0.5
FACTOR = SCALE * LOG2E
MIB = 1 << 20

VMEM_SPEC = pl.BlockSpec(memory_space=pltpu.VMEM)
HBM_SPEC = pl.BlockSpec(memory_space=pltpu.HBM)
ANY_SPEC = pl.BlockSpec(memory_space=pl.ANY)
SMEM_SPEC = pl.BlockSpec(memory_space=pltpu.SMEM)


def run_copies(pairs, sem):
    copies = [pltpu.make_async_copy(source, target, sem.at[n]) for n, (source, target) in enumerate(pairs)]
    for copy in copies:
        copy.start()
    for copy in copies:
        copy.wait()


def lanes(n):
    return pl.ds(n * HEAD_DIM, HEAD_DIM)


def cut_plane_kernel(sel, q, qt, k, kt, v, vt, out, buf, sel_buf, sel_sem, in_sem, out_sem):
    arrays = (k, kt, v, vt, qt, q)
    ins = [[pltpu.make_async_copy(ref.at[:, lanes(j)], buf.at[j, 0:TOK, lanes(n)], in_sem.at[j, n])
            for n, ref in enumerate(arrays)] for j in range(PLANE)]
    outs = [pltpu.make_async_copy(buf.at[j], out.at[j], out_sem.at[j]) for j in range(PLANE)]
    listing = pltpu.make_async_copy(sel, sel_buf, sel_sem.at[0])
    listing.start()
    for chunk in ins[:AHEAD]:
        for copy in chunk:
            copy.start()
    listing.wait()
    listed = sel_buf[...].astype(jnp.float32).astype(jnp.bfloat16)
    for j in range(PLANE):
        buf[j, TOK:TOK + 2, :WIN] = listed
        for copy in ins[j]:
            copy.wait()
        outs[j].start()
        for copy in ins[j + AHEAD] if j + AHEAD < PLANE else ():
            copy.start()
    for copy in outs:
        copy.wait()


def cut_pair_kernel(row_ref, q, qt, k, kt, v, vt, rest, q_same, q_opp, buf, in_sem, out_sem):
    arrays = (k, kt, v, vt, qt, q)
    ins = [pltpu.make_async_copy(ref.at[:, lanes(PLANE + h)], buf.at[h, :, lanes(n)], in_sem.at[h, n])
           for h in range(2) for n, ref in enumerate(arrays)]
    outs = [pltpu.make_async_copy(buf.at[j % 2, :, 0:KV], rest.at[j], out_sem.at[j]) for j in range(PLANE)]
    for copy in ins:
        copy.start()
    for copy in ins:
        copy.wait()
    for copy in outs:
        copy.start()
    par = row_ref[0] % 2
    q_same[...] = buf[par, :, KV:]
    q_opp[...] = buf[1 - par, :, KV:]
    for copy in outs:
        copy.wait()


def weigh(sel_ref, row, first, count, chunk, qcat, floor, s_scr, p_scr, t_scr, inside=None):
    dims = (((1,), (1,)), ((), ()))
    query = qcat[:, HEAD_DIM:]
    peak = [None, None]
    for u in range(count):
        s = lax.dot_general(query, chunk(u)[:, :HEAD_DIM], dims, preferred_element_type=jnp.float32)
        for qb in range(2):
            for kb in range(2):
                at = first + u if inside is None else jnp.clip(first + u, 0, CHUNKS - 1)
                listed = sel_ref[row, qb * WIN + 2 * at + kb]
                if inside is not None:
                    listed = jnp.where(inside(first + u), listed, 0)
                piece = s[qb * BLK:(qb + 1) * BLK, kb * BLK:(kb + 1) * BLK] + jnp.where(listed != 0, 0.0, NEG)
                s_scr[qb * BLK:(qb + 1) * BLK, u * TOK + kb * BLK:u * TOK + (kb + 1) * BLK] = piece
                peak[qb] = piece if peak[qb] is None else jnp.maximum(peak[qb], piece)
    top = jnp.concatenate([jnp.max(p, axis=1, keepdims=True) for p in peak], axis=0) * FACTOR
    if floor is not None:
        top = jnp.maximum(top, floor)
    total = jnp.zeros((TOK, BLK), jnp.float32)
    tangent_total = jnp.zeros((TOK, BLK), jnp.float32)
    for u in range(count):
        st = lax.dot_general(qcat, chunk(u), dims, preferred_element_type=jnp.float32)
        weights = jnp.exp2(s_scr[:, u * TOK:(u + 1) * TOK] * FACTOR - top)
        weighted = weights * st
        total += weights[:, :BLK] + weights[:, BLK:]
        tangent_total += weighted[:, :BLK] + weighted[:, BLK:]
        p_scr[:, u * TOK:(u + 1) * TOK] = weights.astype(jnp.bfloat16)
        t_scr[:, u * TOK:(u + 1) * TOK] = weighted.astype(jnp.bfloat16)
    return top, total, tangent_total


def finish(total, tangent_total, first, second):
    inverse = 1.0 / jnp.sum(total, axis=1, keepdims=True)
    out = first[:, :HEAD_DIM] * inverse
    tangent_sum = jnp.sum(tangent_total, axis=1, keepdims=True)
    tangent = ((second - out * tangent_sum) * SCALE + first[:, HEAD_DIM:]) * inverse
    return jnp.concatenate([out.astype(jnp.bfloat16), tangent.astype(jnp.bfloat16)], axis=1)


def mix(p_scr, t_scr, width, values):
    first = jnp.dot(p_scr[:, :width], values, preferred_element_type=jnp.float32)
    second = jnp.dot(t_scr[:, :width], values[:, :HEAD_DIM], preferred_element_type=jnp.float32)
    return first, second


def inner_kernel(sel_ref, main, o_ref, stats, first_ref, second_ref, vv, s_scr, p_scr, t_scr):
    for c in range(PLANE):
        vv[c * TOK:(c + 1) * TOK, :] = main[c, :TOK, 2 * HEAD_DIM:KV]

    def position(i, count, final):
        begin = jnp.maximum(i - REACH, 0)
        base = pl.multiple_of(begin * TOK, TOK)
        top, total, tangent_total = weigh(
            sel_ref, i, jnp.maximum(REACH - i, 0), count, lambda u: main[begin + u, :TOK, :2 * HEAD_DIM],
            main[i, :TOK, KV:], None, s_scr, p_scr, t_scr)
        first, second = mix(p_scr, t_scr, count * TOK, vv[pl.ds(base, count * TOK), :])
        if final:
            o_ref[i - REACH] = finish(total, tangent_total, first, second)
        else:
            stats[i, 0] = jnp.broadcast_to(top, (TOK, BLK))
            stats[i, 1] = total
            stats[i, 2] = tangent_total
            first_ref[i] = first
            second_ref[i] = second

    def step(n, carry):
        for low in range(REACH + 1):
            position(low + n * (PLANE - 1 - 2 * low), low + REACH + 1, low == REACH)
        return carry

    lax.fori_loop(0, 2, step, 0)


def outer_kernel(sel_ref, main, up, dn, mid, stats, first_ref, second_ref, o_ref, done, buf, sem, s_scr, p_scr, t_scr):
    done[...] = jnp.zeros_like(done)
    copies = []

    def leave(i, value):
        buf[i] = value
        copies.append(pltpu.make_async_copy(buf.at[i], o_ref.at[i], sem.at[i]))
        copies[-1].start()

    for i in (3, 4):
        leave(i, mid[i - REACH])
    for i in (0, 1, 2, 5, 6, 7):
        low = i < REACH
        halo, skip, at = (up, i, 0) if low else (dn, 0, PLANE + REACH - i)
        count = REACH - i if low else i - REACH - 1
        before = stats[i, 0][:, :1]
        top, total, tangent_total = weigh(
            sel_ref, i, at, count, lambda u: halo[skip + u, :, :2 * HEAD_DIM], main[i, :TOK, KV:], before,
            s_scr, p_scr, t_scr)
        shrink = jnp.exp2(before - top)
        first, second = first_ref[i] * shrink, second_ref[i] * shrink
        for u in range(count):
            more = mix(p_scr.at[:, u * TOK:(u + 1) * TOK], t_scr.at[:, u * TOK:(u + 1) * TOK], TOK,
                       halo[skip + u, :, 2 * HEAD_DIM:])
            first, second = first + more[0], second + more[1]
        leave(i, finish(stats[i, 1] * shrink + total, stats[i, 2] * shrink + tangent_total, first, second))
    for copy in copies:
        copy.wait()


def edges_kernel(main, gate_a, gate_b, up, dn, sem):
    del gate_a, gate_b
    run_copies([(main.at[first + n, 0:TOK, 0:KV], to.at[n]) for first, to in ((PLANE - REACH, up), (0, dn))
                for n in range(REACH)], sem)


def edge_kernel(task_ref, main, gate, edge, sem):
    del gate
    begin = jnp.where(task_ref[0] < PLANE // 2, PLANE - REACH, 0)
    run_copies([(main.at[begin + n], edge.at[n]) for n in range(REACH)], sem)


def pair_tasks(task_ref, q_first, q_second):
    task = task_ref[0]
    return ((q_first, task), (q_second, task + 1 - 2 * (task % 2)))


def pair_inner_kernel(task_ref, sel_ref, q_first, q_second, main, gate, stats, first_ref, second_ref,
                      kv, s_scr, p_scr, t_scr, sem):
    del gate
    copies = [pltpu.make_async_copy(main.at[c], kv.at[pl.ds((c + REACH) * TOK, TOK), :], sem.at[c]) for c in range(PLANE)]
    for copy in copies:
        copy.start()
    for begin in (0, REACH + PLANE):
        kv[begin * TOK:(begin + REACH) * TOK, :] = jnp.zeros((REACH * TOK, KV), jnp.bfloat16)
    for copy in copies:
        copy.wait()
    for n, (ref, at) in enumerate(pair_tasks(task_ref, q_first, q_second)):
        base = pl.multiple_of(at * TOK, TOK)
        top, total, tangent_total = weigh(
            sel_ref, at, 0, CHUNKS, lambda u: kv[pl.ds(base + u * TOK, TOK), :2 * HEAD_DIM], ref[...], None,
            s_scr, p_scr, t_scr, lambda t: jnp.logical_and(at + t >= REACH, at + t < REACH + PLANE))
        first, second = mix(p_scr, t_scr, CHUNKS * TOK, kv[pl.ds(base, CHUNKS * TOK), 2 * HEAD_DIM:])
        stats[n, 0] = jnp.broadcast_to(top, (TOK, BLK))
        stats[n, 1] = total
        stats[n, 2] = tangent_total
        first_ref[n] = first
        second_ref[n] = second


def pair_outer_kernel(task_ref, sel_ref, q_first, q_second, halo, stats, first_ref, second_ref, o_first, o_second,
                      s_scr, p_scr, t_scr):
    begin = jnp.where(task_ref[0] < PLANE // 2, 0, REACH + PLANE)
    outs = (o_first, o_second)
    for n, (ref, at) in enumerate(pair_tasks(task_ref, q_first, q_second)):
        before = stats[n, 0][:, :1]
        top, total, tangent_total = weigh(
            sel_ref, at, begin - at, REACH, lambda u: halo[u, :, :2 * HEAD_DIM], ref[...], before,
            s_scr, p_scr, t_scr, lambda t: jnp.logical_and(t >= 0, t < CHUNKS))
        shrink = jnp.exp2(before - top)
        first, second = first_ref[n] * shrink, second_ref[n] * shrink
        for u in range(REACH):
            more = mix(p_scr.at[:, u * TOK:(u + 1) * TOK], t_scr.at[:, u * TOK:(u + 1) * TOK], TOK,
                       halo[u, :, 2 * HEAD_DIM:])
            first, second = first + more[0], second + more[1]
        outs[n][...] = finish(stats[n, 1] * shrink + total, stats[n, 2] * shrink + tangent_total, first, second)


def after_kernel(*refs):
    del refs


def after(array, *others):
    return pl.pallas_call(
        after_kernel,
        out_shape=pltpu.HBM(array.shape, array.dtype),
        in_specs=[HBM_SPEC] + [ANY_SPEC] * len(others),
        out_specs=HBM_SPEC,
        input_output_aliases={0: 0},
        compiler_params=params(1),
        name="after",
    )(pltpu.with_memory_space_constraint(array, pltpu.HBM), *others)


def unpack_kernel(par_ref, mine, own, other, o_ref, t_ref):
    par = par_ref[0] % 2
    for j in range(PLANE):
        cols = pl.ds(j * HEAD_DIM, HEAD_DIM)
        o_ref[:, cols] = mine[j, :, :HEAD_DIM]
        t_ref[:, cols] = mine[j, :, HEAD_DIM:]
    for which, piece in ((par, own), (1 - par, other)):
        cols = pl.ds(pl.multiple_of((PLANE + which) * HEAD_DIM, HEAD_DIM), HEAD_DIM)
        o_ref[:, cols] = piece[:, :HEAD_DIM]
        t_ref[:, cols] = piece[:, HEAD_DIM:]


def bf16(*shape):
    return jax.ShapeDtypeStruct(shape, jnp.bfloat16)


def f32(*shape):
    return jax.ShapeDtypeStruct(shape, jnp.float32)


def scratch(chunks):
    return [
        pltpu.VMEM((TOK, chunks * TOK), jnp.float32),
        pltpu.VMEM((TOK, chunks * TOK), jnp.bfloat16),
        pltpu.VMEM((TOK, chunks * TOK), jnp.bfloat16),
    ]


def cost(chunks):
    products = chunks * TOK * TOK
    return pl.CostEstimate(flops=10 * HEAD_DIM * products, bytes_accessed=chunks * 2 * TOK * 4 * HEAD_DIM,
                           transcendentals=products)


def params(mib):
    return pltpu.CompilerParams(vmem_limit_bytes=mib * MIB)


def body(queries, query_tangents, keys, key_tangents, values, value_tangents, selection):
    devices = lax.axis_size("ctx")
    columns = lax.axis_size("head")
    row = (lax.axis_index("ctx") % PLANE).astype(jnp.int32)[None]
    task = row ^ (4 * (lax.axis_index("head") % 2).astype(jnp.int32))
    planes = [[z * PLANE + i for i in range(PLANE)] for z in range(devices // PLANE)]

    def send(array, by):
        return lax.ppermute(array, "ctx", [(i, (i + by) % devices) for i in range(devices)])

    def spread(array, target):
        pairs = [(i * columns + h, target(i, h % 2) * columns + h) for i in range(devices) for h in range(columns)]
        return lax.ppermute(array, ("ctx", "head"), pairs)

    def to_first(array):
        return spread(array, lambda i, core: i ^ (4 * core))

    def to_second(array):
        return spread(array, lambda i, core: i ^ (4 * core) ^ 1)

    def exchange(array):
        return lax.all_to_all(array, "ctx", 0, 0, axis_index_groups=planes, tiled=True)

    wide = [pltpu.with_memory_space_constraint(array, pltpu.HBM) for array in
            (queries, query_tangents, keys, key_tangents, values, value_tangents)]
    plane_out = pl.pallas_call(
        cut_plane_kernel,
        out_shape=pltpu.HBM((PLANE, TOK + EXTRA, ALL), jnp.bfloat16),
        in_specs=[HBM_SPEC] * 7,
        out_specs=ANY_SPEC,
        scratch_shapes=[pltpu.VMEM((PLANE, TOK + EXTRA, ALL), jnp.bfloat16),
                        pltpu.VMEM((BPD, WIN), jnp.int32), pltpu.SemaphoreType.DMA((1,)),
                        pltpu.SemaphoreType.DMA((PLANE, 6)), pltpu.SemaphoreType.DMA((PLANE,))],
        compiler_params=params(8),
        name="cut_plane",
    )(pltpu.with_memory_space_constraint(selection, pltpu.HBM), *wide)
    rest_out, q_same, q_opp = pl.pallas_call(
        cut_pair_kernel,
        out_shape=(pltpu.HBM((PLANE, TOK, KV), jnp.bfloat16), bf16(TOK, 256), bf16(TOK, 256)),
        in_specs=[SMEM_SPEC] + [HBM_SPEC] * 6,
        out_specs=(ANY_SPEC,) + (VMEM_SPEC,) * 2,
        scratch_shapes=[pltpu.VMEM((2, TOK, ALL), jnp.bfloat16),
                        pltpu.SemaphoreType.DMA((2, 6)), pltpu.SemaphoreType.DMA((PLANE,))],
        compiler_params=params(8),
        name="cut_pair",
    )(row, *wide)

    q_first, q_second = to_first(q_same), to_second(q_opp)

    main = exchange(plane_out)
    sel_all = main[:, TOK:TOK + 2, :WIN].astype(jnp.int32).reshape(PLANE, 2 * WIN)
    edge_up, edge_dn = pl.pallas_call(
        edges_kernel,
        out_shape=(pltpu.HBM((REACH, TOK, KV), jnp.bfloat16),) * 2,
        in_specs=[ANY_SPEC] * 3,
        out_specs=(ANY_SPEC,) * 2,
        scratch_shapes=[pltpu.SemaphoreType.DMA((2 * REACH,))],
        compiler_params=params(1),
        name="edges",
    )(main, q_first, q_second)
    up, dn = send(edge_up, PLANE), send(edge_dn, -PLANE)
    rest = exchange(after(rest_out, sel_all, q_first, q_second))

    mid, stats, first, second = pl.pallas_call(
        inner_kernel,
        out_shape=(bf16(2, TOK, 256), f32(PLANE, 3, TOK, BLK), f32(PLANE, TOK, 256), f32(PLANE, TOK, BLK)),
        in_specs=[SMEM_SPEC, VMEM_SPEC],
        out_specs=(VMEM_SPEC,) * 4,
        scratch_shapes=[pltpu.VMEM((PLANE * TOK, 2 * HEAD_DIM), jnp.bfloat16)] + scratch(CHUNKS),
        compiler_params=params(16),
        cost_estimate=cost(44),
        name="inner",
    )(sel_all, main)
    mine, done = pl.pallas_call(
        outer_kernel,
        out_shape=(pltpu.HBM((PLANE, TOK, 256), jnp.bfloat16), f32(8, BLK)),
        in_specs=[SMEM_SPEC] + [VMEM_SPEC] * 7,
        out_specs=(ANY_SPEC, VMEM_SPEC),
        scratch_shapes=[pltpu.VMEM((PLANE, TOK, 256), jnp.bfloat16), pltpu.SemaphoreType.DMA((PLANE,))] + scratch(REACH),
        compiler_params=params(16),
        cost_estimate=cost(12),
        name="outer",
    )(sel_all, main, up, dn, mid, stats, first, second)
    edge = pl.pallas_call(
        edge_kernel,
        out_shape=bf16(REACH, TOK, KV),
        in_specs=[SMEM_SPEC, ANY_SPEC, ANY_SPEC],
        out_specs=ANY_SPEC,
        scratch_shapes=[pltpu.SemaphoreType.DMA((REACH,))],
        compiler_params=params(1),
        name="edge",
    )(task, rest, done)
    halo = spread(edge, lambda i, core: (i + (PLANE if (i ^ (4 * core)) % PLANE < PLANE // 2 else -PLANE)) % devices)
    back = exchange(after(mine, edge))

    pair_sums = pl.pallas_call(
        pair_inner_kernel,
        out_shape=(f32(2, 3, TOK, BLK), f32(2, TOK, 256), f32(2, TOK, BLK)),
        in_specs=[SMEM_SPEC] * 2 + [VMEM_SPEC] * 2 + [ANY_SPEC] * 2,
        out_specs=(VMEM_SPEC,) * 3,
        scratch_shapes=[pltpu.VMEM(((PLANE + 2 * REACH) * TOK, KV), jnp.bfloat16)] + scratch(CHUNKS)
        + [pltpu.SemaphoreType.DMA((PLANE,))],
        compiler_params=params(16),
        cost_estimate=cost(14),
        name="pair_inner",
    )(task, sel_all, q_first, q_second, rest, edge)
    own, lent = pl.pallas_call(
        pair_outer_kernel,
        out_shape=(bf16(TOK, 256), bf16(TOK, 256)),
        in_specs=[SMEM_SPEC] * 2 + [VMEM_SPEC] * 6,
        out_specs=(VMEM_SPEC,) * 2,
        scratch_shapes=scratch(REACH),
        compiler_params=params(8),
        cost_estimate=cost(6),
        name="pair_outer",
    )(task, sel_all, q_first, q_second, halo, *pair_sums)
    own, partner = to_first(own), to_second(lent)

    return pl.pallas_call(
        unpack_kernel,
        out_shape=(bf16(TOK, HEADS * HEAD_DIM), bf16(TOK, HEADS * HEAD_DIM)),
        in_specs=[SMEM_SPEC] + [VMEM_SPEC] * 3,
        out_specs=(VMEM_SPEC,) * 2,
        compiler_params=params(6),
        name="unpack",
    )(row, back, own, partner)


def solution(mesh):
    wide = P("ctx", "head")
    return jax.shard_map(
        body,
        mesh=mesh,
        in_specs=(wide,) * 6 + (P("ctx", None),),
        out_specs=(wide, wide),
        check_vma=False,
    )
```

```python
import jax
import jax.numpy as jnp
from jax import lax
from jax.experimental import pallas as pl
from jax.experimental.pallas import tpu as pltpu
from jax.sharding import PartitionSpec as P

HEADS = 10
HEAD_DIM = 128
BLK = 128
REACH = 3
TOK = 256
WIN = 14
BPD = 2
PLANE = 8
CHUNKS = 2 * REACH + 1
EXTRA = 8
KV = 4 * HEAD_DIM
ALL = 6 * HEAD_DIM
NEG = -1.0e30
LOG2E = 1.4426950408889634
SCALE = HEAD_DIM ** -0.5
FACTOR = SCALE * LOG2E
MIB = 1 << 20

VMEM_SPEC = pl.BlockSpec(memory_space=pltpu.VMEM)
HBM_SPEC = pl.BlockSpec(memory_space=pltpu.HBM)
ANY_SPEC = pl.BlockSpec(memory_space=pl.ANY)
SMEM_SPEC = pl.BlockSpec(memory_space=pltpu.SMEM)


def run_copies(pairs, sem):
    copies = [pltpu.make_async_copy(source, target, sem.at[n]) for n, (source, target) in enumerate(pairs)]
    for copy in copies:
        copy.start()
    for copy in copies:
        copy.wait()


def lanes(n):
    return pl.ds(n * HEAD_DIM, HEAD_DIM)


def cut_plane_kernel(sel, q, qt, k, kt, v, vt, out, buf, sel_buf, sel_sem, in_sem, out_sem):
    arrays = (k, kt, v, vt, qt, q)
    ins = [[pltpu.make_async_copy(ref.at[:, lanes(j)], buf.at[j, 0:TOK, lanes(n)], in_sem.at[j, n])
            for n, ref in enumerate(arrays)] for j in range(PLANE)]
    outs = [pltpu.make_async_copy(buf.at[j], out.at[j], out_sem.at[j]) for j in range(PLANE)]
    listing = pltpu.make_async_copy(sel, sel_buf, sel_sem.at[0])
    listing.start()
    for chunk in ins:
        for copy in chunk:
            copy.start()
    listing.wait()
    listed = sel_buf[...].astype(jnp.float32).astype(jnp.bfloat16)
    for j in range(PLANE):
        buf[j, TOK:TOK + 2, :WIN] = listed
        for copy in ins[j]:
            copy.wait()
        outs[j].start()
    for copy in outs:
        copy.wait()


def cut_pair_kernel(row_ref, q, qt, k, kt, v, vt, rest, q_same, q_opp, buf, in_sem, out_sem):
    arrays = (k, kt, v, vt, qt, q)
    ins = [pltpu.make_async_copy(ref.at[:, lanes(PLANE + h)], buf.at[h, :, lanes(n)], in_sem.at[h, n])
           for h in range(2) for n, ref in enumerate(arrays)]
    outs = [pltpu.make_async_copy(buf.at[j % 2, :, 0:KV], rest.at[j], out_sem.at[j]) for j in range(PLANE)]
    for copy in ins:
        copy.start()
    for copy in ins:
        copy.wait()
    for copy in outs:
        copy.start()
    par = row_ref[0] % 2
    q_same[...] = buf[par, :, KV:]
    q_opp[...] = buf[1 - par, :, KV:]
    for copy in outs:
        copy.wait()


def weigh(sel_ref, row, first, count, chunk, qcat, floor, s_scr, p_scr, t_scr, inside=None):
    dims = (((1,), (1,)), ((), ()))
    query = qcat[:, HEAD_DIM:]
    peak = [None, None]
    for u in range(count):
        s = lax.dot_general(query, chunk(u)[:, :HEAD_DIM], dims, preferred_element_type=jnp.float32)
        for qb in range(2):
            for kb in range(2):
                at = first + u if inside is None else jnp.clip(first + u, 0, CHUNKS - 1)
                listed = sel_ref[row, qb * WIN + 2 * at + kb]
                if inside is not None:
                    listed = jnp.where(inside(first + u), listed, 0)
                piece = s[qb * BLK:(qb + 1) * BLK, kb * BLK:(kb + 1) * BLK] + jnp.where(listed != 0, 0.0, NEG)
                s_scr[qb * BLK:(qb + 1) * BLK, u * TOK + kb * BLK:u * TOK + (kb + 1) * BLK] = piece
                peak[qb] = piece if peak[qb] is None else jnp.maximum(peak[qb], piece)
    top = jnp.concatenate([jnp.max(p, axis=1, keepdims=True) for p in peak], axis=0) * FACTOR
    if floor is not None:
        top = jnp.maximum(top, floor)
    total = jnp.zeros((TOK, BLK), jnp.float32)
    tangent_total = jnp.zeros((TOK, BLK), jnp.float32)
    for u in range(count):
        st = lax.dot_general(qcat, chunk(u), dims, preferred_element_type=jnp.float32)
        weights = jnp.exp2(s_scr[:, u * TOK:(u + 1) * TOK] * FACTOR - top)
        weighted = weights * st
        total += weights[:, :BLK] + weights[:, BLK:]
        tangent_total += weighted[:, :BLK] + weighted[:, BLK:]
        p_scr[:, u * TOK:(u + 1) * TOK] = weights.astype(jnp.bfloat16)
        t_scr[:, u * TOK:(u + 1) * TOK] = weighted.astype(jnp.bfloat16)
    return top, total, tangent_total


def finish(total, tangent_total, first, second):
    inverse = 1.0 / jnp.sum(total, axis=1, keepdims=True)
    out = first[:, :HEAD_DIM] * inverse
    tangent_sum = jnp.sum(tangent_total, axis=1, keepdims=True)
    tangent = ((second - out * tangent_sum) * SCALE + first[:, HEAD_DIM:]) * inverse
    return jnp.concatenate([out.astype(jnp.bfloat16), tangent.astype(jnp.bfloat16)], axis=1)


def mix(p_scr, t_scr, width, values):
    first = jnp.dot(p_scr[:, :width], values, preferred_element_type=jnp.float32)
    second = jnp.dot(t_scr[:, :width], values[:, :HEAD_DIM], preferred_element_type=jnp.float32)
    return first, second


def inner_kernel(sel_ref, main, gate_a, gate_b, o_ref, stats, first_ref, second_ref, vv, s_scr, p_scr, t_scr):
    del gate_a, gate_b
    for c in range(PLANE):
        vv[c * TOK:(c + 1) * TOK, :] = main[c, :TOK, 2 * HEAD_DIM:KV]

    def position(i, count, final):
        begin = jnp.maximum(i - REACH, 0)
        base = pl.multiple_of(begin * TOK, TOK)
        top, total, tangent_total = weigh(
            sel_ref, i, jnp.maximum(REACH - i, 0), count, lambda u: main[begin + u, :TOK, :2 * HEAD_DIM],
            main[i, :TOK, KV:], None, s_scr, p_scr, t_scr)
        first, second = mix(p_scr, t_scr, count * TOK, vv[pl.ds(base, count * TOK), :])
        if final:
            o_ref[i - REACH] = finish(total, tangent_total, first, second)
        else:
            stats[i, 0] = jnp.broadcast_to(top, (TOK, BLK))
            stats[i, 1] = total
            stats[i, 2] = tangent_total
            first_ref[i] = first
            second_ref[i] = second

    def step(n, carry):
        for low in range(REACH + 1):
            position(low + n * (PLANE - 1 - 2 * low), low + REACH + 1, low == REACH)
        return carry

    lax.fori_loop(0, 2, step, 0)


def outer_kernel(sel_ref, main, up, dn, mid, stats, first_ref, second_ref, o_ref, done, buf, sem, s_scr, p_scr, t_scr):
    done[...] = jnp.zeros_like(done)
    copies = []

    def leave(i, value):
        buf[i] = value
        copies.append(pltpu.make_async_copy(buf.at[i], o_ref.at[i], sem.at[i]))
        copies[-1].start()

    for i in (3, 4):
        leave(i, mid[i - REACH])
    for i in (0, 1, 2, 5, 6, 7):
        low = i < REACH
        halo, skip, at = (up, i, 0) if low else (dn, 0, PLANE + REACH - i)
        count = REACH - i if low else i - REACH - 1
        before = stats[i, 0][:, :1]
        top, total, tangent_total = weigh(
            sel_ref, i, at, count, lambda u: halo[skip + u, :, :2 * HEAD_DIM], main[i, :TOK, KV:], before,
            s_scr, p_scr, t_scr)
        shrink = jnp.exp2(before - top)
        first, second = first_ref[i] * shrink, second_ref[i] * shrink
        for u in range(count):
            more = mix(p_scr.at[:, u * TOK:(u + 1) * TOK], t_scr.at[:, u * TOK:(u + 1) * TOK], TOK,
                       halo[skip + u, :, 2 * HEAD_DIM:])
            first, second = first + more[0], second + more[1]
        leave(i, finish(stats[i, 1] * shrink + total, stats[i, 2] * shrink + tangent_total, first, second))
    for copy in copies:
        copy.wait()


def edges_kernel(main, gate_a, gate_b, up, dn, sem):
    del gate_a, gate_b
    run_copies([(main.at[first + n, 0:TOK, 0:KV], to.at[n]) for first, to in ((PLANE - REACH, up), (0, dn))
                for n in range(REACH)], sem)


def edge_kernel(task_ref, main, gate, edge, sem):
    del gate
    begin = jnp.where(task_ref[0] < PLANE // 2, PLANE - REACH, 0)
    run_copies([(main.at[begin + n], edge.at[n]) for n in range(REACH)], sem)


def pair_tasks(task_ref, q_first, q_second):
    task = task_ref[0]
    return ((q_first, task), (q_second, task + 1 - 2 * (task % 2)))


def pair_inner_kernel(task_ref, sel_ref, q_first, q_second, main, gate, stats, first_ref, second_ref,
                      kv, s_scr, p_scr, t_scr, sem):
    del gate
    copies = [pltpu.make_async_copy(main.at[c], kv.at[pl.ds((c + REACH) * TOK, TOK), :], sem.at[c]) for c in range(PLANE)]
    for copy in copies:
        copy.start()
    for begin in (0, REACH + PLANE):
        kv[begin * TOK:(begin + REACH) * TOK, :] = jnp.zeros((REACH * TOK, KV), jnp.bfloat16)
    for copy in copies:
        copy.wait()
    for n, (ref, at) in enumerate(pair_tasks(task_ref, q_first, q_second)):
        base = pl.multiple_of(at * TOK, TOK)
        top, total, tangent_total = weigh(
            sel_ref, at, 0, CHUNKS, lambda u: kv[pl.ds(base + u * TOK, TOK), :2 * HEAD_DIM], ref[...], None,
            s_scr, p_scr, t_scr, lambda t: jnp.logical_and(at + t >= REACH, at + t < REACH + PLANE))
        first, second = mix(p_scr, t_scr, CHUNKS * TOK, kv[pl.ds(base, CHUNKS * TOK), 2 * HEAD_DIM:])
        stats[n, 0] = jnp.broadcast_to(top, (TOK, BLK))
        stats[n, 1] = total
        stats[n, 2] = tangent_total
        first_ref[n] = first
        second_ref[n] = second


def pair_outer_kernel(task_ref, sel_ref, q_first, q_second, halo, stats, first_ref, second_ref, o_first, o_second,
                      s_scr, p_scr, t_scr):
    begin = jnp.where(task_ref[0] < PLANE // 2, 0, REACH + PLANE)
    outs = (o_first, o_second)
    for n, (ref, at) in enumerate(pair_tasks(task_ref, q_first, q_second)):
        before = stats[n, 0][:, :1]
        top, total, tangent_total = weigh(
            sel_ref, at, begin - at, REACH, lambda u: halo[u, :, :2 * HEAD_DIM], ref[...], before,
            s_scr, p_scr, t_scr, lambda t: jnp.logical_and(t >= 0, t < CHUNKS))
        shrink = jnp.exp2(before - top)
        first, second = first_ref[n] * shrink, second_ref[n] * shrink
        for u in range(REACH):
            more = mix(p_scr.at[:, u * TOK:(u + 1) * TOK], t_scr.at[:, u * TOK:(u + 1) * TOK], TOK,
                       halo[u, :, 2 * HEAD_DIM:])
            first, second = first + more[0], second + more[1]
        outs[n][...] = finish(stats[n, 1] * shrink + total, stats[n, 2] * shrink + tangent_total, first, second)


def after_kernel(*refs):
    del refs


def after(array, *others):
    return pl.pallas_call(
        after_kernel,
        out_shape=pltpu.HBM(array.shape, array.dtype),
        in_specs=[HBM_SPEC] + [ANY_SPEC] * len(others),
        out_specs=HBM_SPEC,
        input_output_aliases={0: 0},
        compiler_params=params(1),
        name="after",
    )(pltpu.with_memory_space_constraint(array, pltpu.HBM), *others)


def unpack_kernel(par_ref, mine, own, other, o_ref, t_ref):
    par = par_ref[0] % 2
    for j in range(PLANE):
        cols = pl.ds(j * HEAD_DIM, HEAD_DIM)
        o_ref[:, cols] = mine[j, :, :HEAD_DIM]
        t_ref[:, cols] = mine[j, :, HEAD_DIM:]
    for which, piece in ((par, own), (1 - par, other)):
        cols = pl.ds(pl.multiple_of((PLANE + which) * HEAD_DIM, HEAD_DIM), HEAD_DIM)
        o_ref[:, cols] = piece[:, :HEAD_DIM]
        t_ref[:, cols] = piece[:, HEAD_DIM:]


def bf16(*shape):
    return jax.ShapeDtypeStruct(shape, jnp.bfloat16)


def f32(*shape):
    return jax.ShapeDtypeStruct(shape, jnp.float32)


def scratch(chunks):
    return [
        pltpu.VMEM((TOK, chunks * TOK), jnp.float32),
        pltpu.VMEM((TOK, chunks * TOK), jnp.bfloat16),
        pltpu.VMEM((TOK, chunks * TOK), jnp.bfloat16),
    ]


def cost(chunks):
    products = chunks * TOK * TOK
    return pl.CostEstimate(flops=10 * HEAD_DIM * products, bytes_accessed=chunks * 2 * TOK * 4 * HEAD_DIM,
                           transcendentals=products)


def params(mib):
    return pltpu.CompilerParams(vmem_limit_bytes=mib * MIB)


def body(queries, query_tangents, keys, key_tangents, values, value_tangents, selection):
    devices = lax.axis_size("ctx")
    columns = lax.axis_size("head")
    row = (lax.axis_index("ctx") % PLANE).astype(jnp.int32)[None]
    task = row ^ (4 * (lax.axis_index("head") % 2).astype(jnp.int32))
    planes = [[z * PLANE + i for i in range(PLANE)] for z in range(devices // PLANE)]

    def send(array, by):
        return lax.ppermute(array, "ctx", [(i, (i + by) % devices) for i in range(devices)])

    def spread(array, target):
        pairs = [(i * columns + h, target(i, h % 2) * columns + h) for i in range(devices) for h in range(columns)]
        return lax.ppermute(array, ("ctx", "head"), pairs)

    def to_first(array):
        return spread(array, lambda i, core: i ^ (4 * core))

    def to_second(array):
        return spread(array, lambda i, core: i ^ (4 * core) ^ 1)

    def exchange(array):
        return lax.all_to_all(array, "ctx", 0, 0, axis_index_groups=planes, tiled=True)

    wide = [pltpu.with_memory_space_constraint(array, pltpu.HBM) for array in
            (queries, query_tangents, keys, key_tangents, values, value_tangents)]
    plane_out = pl.pallas_call(
        cut_plane_kernel,
        out_shape=pltpu.HBM((PLANE, TOK + EXTRA, ALL), jnp.bfloat16),
        in_specs=[HBM_SPEC] * 7,
        out_specs=ANY_SPEC,
        scratch_shapes=[pltpu.VMEM((PLANE, TOK + EXTRA, ALL), jnp.bfloat16),
                        pltpu.VMEM((BPD, WIN), jnp.int32), pltpu.SemaphoreType.DMA((1,)),
                        pltpu.SemaphoreType.DMA((PLANE, 6)), pltpu.SemaphoreType.DMA((PLANE,))],
        compiler_params=params(8),
        name="cut_plane",
    )(pltpu.with_memory_space_constraint(selection, pltpu.HBM), *wide)
    rest_out, q_same, q_opp = pl.pallas_call(
        cut_pair_kernel,
        out_shape=(pltpu.HBM((PLANE, TOK, KV), jnp.bfloat16), bf16(TOK, 256), bf16(TOK, 256)),
        in_specs=[SMEM_SPEC] + [HBM_SPEC] * 6,
        out_specs=(ANY_SPEC,) + (VMEM_SPEC,) * 2,
        scratch_shapes=[pltpu.VMEM((2, TOK, ALL), jnp.bfloat16),
                        pltpu.SemaphoreType.DMA((2, 6)), pltpu.SemaphoreType.DMA((PLANE,))],
        compiler_params=params(8),
        name="cut_pair",
    )(row, *wide)

    q_first, q_second = to_first(q_same), to_second(q_opp)

    main = exchange(plane_out)
    sel_all = main[:, TOK:TOK + 2, :WIN].astype(jnp.int32).reshape(PLANE, 2 * WIN)
    edge_up, edge_dn = pl.pallas_call(
        edges_kernel,
        out_shape=(pltpu.HBM((REACH, TOK, KV), jnp.bfloat16),) * 2,
        in_specs=[ANY_SPEC] * 3,
        out_specs=(ANY_SPEC,) * 2,
        scratch_shapes=[pltpu.SemaphoreType.DMA((2 * REACH,))],
        compiler_params=params(1),
        name="edges",
    )(main, q_same, q_opp)
    up, dn = send(edge_up, PLANE), send(edge_dn, -PLANE)
    rest = exchange(after(rest_out, sel_all))

    mid, stats, first, second = pl.pallas_call(
        inner_kernel,
        out_shape=(bf16(2, TOK, 256), f32(PLANE, 3, TOK, BLK), f32(PLANE, TOK, 256), f32(PLANE, TOK, BLK)),
        in_specs=[SMEM_SPEC, VMEM_SPEC] + [ANY_SPEC] * 2,
        out_specs=(VMEM_SPEC,) * 4,
        scratch_shapes=[pltpu.VMEM((PLANE * TOK, 2 * HEAD_DIM), jnp.bfloat16)] + scratch(CHUNKS),
        compiler_params=params(16),
        cost_estimate=cost(44),
        name="inner",
    )(sel_all, main, q_first, q_second)
    mine, done = pl.pallas_call(
        outer_kernel,
        out_shape=(pltpu.HBM((PLANE, TOK, 256), jnp.bfloat16), f32(8, BLK)),
        in_specs=[SMEM_SPEC] + [VMEM_SPEC] * 7,
        out_specs=(ANY_SPEC, VMEM_SPEC),
        scratch_shapes=[pltpu.VMEM((PLANE, TOK, 256), jnp.bfloat16), pltpu.SemaphoreType.DMA((PLANE,))] + scratch(REACH),
        compiler_params=params(16),
        cost_estimate=cost(12),
        name="outer",
    )(sel_all, main, up, dn, mid, stats, first, second)
    edge = pl.pallas_call(
        edge_kernel,
        out_shape=bf16(REACH, TOK, KV),
        in_specs=[SMEM_SPEC, ANY_SPEC, ANY_SPEC],
        out_specs=ANY_SPEC,
        scratch_shapes=[pltpu.SemaphoreType.DMA((REACH,))],
        compiler_params=params(1),
        name="edge",
    )(task, rest, done)
    halo = spread(edge, lambda i, core: (i + (PLANE if (i ^ (4 * core)) % PLANE < PLANE // 2 else -PLANE)) % devices)
    back = exchange(after(mine, edge))

    pair_sums = pl.pallas_call(
        pair_inner_kernel,
        out_shape=(f32(2, 3, TOK, BLK), f32(2, TOK, 256), f32(2, TOK, BLK)),
        in_specs=[SMEM_SPEC] * 2 + [VMEM_SPEC] * 2 + [ANY_SPEC] * 2,
        out_specs=(VMEM_SPEC,) * 3,
        scratch_shapes=[pltpu.VMEM(((PLANE + 2 * REACH) * TOK, KV), jnp.bfloat16)] + scratch(CHUNKS)
        + [pltpu.SemaphoreType.DMA((PLANE,))],
        compiler_params=params(16),
        cost_estimate=cost(14),
        name="pair_inner",
    )(task, sel_all, q_first, q_second, rest, edge)
    own, lent = pl.pallas_call(
        pair_outer_kernel,
        out_shape=(bf16(TOK, 256), bf16(TOK, 256)),
        in_specs=[SMEM_SPEC] * 2 + [VMEM_SPEC] * 6,
        out_specs=(VMEM_SPEC,) * 2,
        scratch_shapes=scratch(REACH),
        compiler_params=params(8),
        cost_estimate=cost(6),
        name="pair_outer",
    )(task, sel_all, q_first, q_second, halo, *pair_sums)
    own, partner = to_first(own), to_second(lent)

    return pl.pallas_call(
        unpack_kernel,
        out_shape=(bf16(TOK, HEADS * HEAD_DIM), bf16(TOK, HEADS * HEAD_DIM)),
        in_specs=[SMEM_SPEC] + [VMEM_SPEC] * 3,
        out_specs=(VMEM_SPEC,) * 2,
        compiler_params=params(6),
        name="unpack",
    )(row, back, own, partner)


def solution(mesh):
    wide = P("ctx", "head")
    return jax.shard_map(
        body,
        mesh=mesh,
        in_specs=(wide,) * 6 + (P("ctx", None),),
        out_specs=(wide, wide),
        check_vma=False,
    )
```
